32 devices in a mesh: row: 8 (over z, y), rep: 4 (over x, core).
Axes of the slice: x: 2, y: 2, z: 4, core: 2. Of those that a mesh axis runs over, the one named last changes fastest.
Arguments:
- features: bfloat16 [4096, 256], P(('row', 'rep')), may hold values from -6 to 6
- w_self: bfloat16 [256, 256], replicated, may hold values from -0.375 to 0.375
- w_neigh: bfloat16 [256, 256], replicated, may hold values from -0.75 to 0.75
- bias: float32 [256], replicated, may hold values from -3 to 3
- d_out: bfloat16 [4096, 256], P(('row', 'rep')), may hold values from -6 to 6
- tile_row: int32 [8192], P(('row', 'rep')), may hold values from 0 to 3
- tile_col: int32 [8192], P(('row', 'rep')), may hold values from 0 to 7
- tile_count: int32 [8192], P(('row', 'rep')), may hold values from 64 to 256, as said below
- edge_src: int32 [8192, 256], P(('row', 'rep')), may hold values from 0 to 127
- edge_dst: int32 [8192, 256], P(('row', 'rep')), may hold values from 0 to 127
Outputs:
- out: bfloat16 [4096, 256], P(('row', 'rep'))
- d_features: float32 [4096, 256], P(('row', 'rep'))
- grad_self: float32 [256, 256], replicated
- grad_neigh: float32 [256, 256], replicated
- grad_bias: float32 [256], replicated
The draws below stay inside these ranges and needn't reach their ends.
Inputs may be any that keep to these rules, and one draw needn't show every extreme that they name: `tile_count`: every device has a tile with exactly 256 live edges in every draw; each device's live counts lie between a lower bound of its own and 256.
All inputs are finite; a program needn't handle non-finite values.
Results may differ from the reference program's by a relative error of at most 0.014.
Values may be sent and summed in bfloat16 or wider, within the bound.
No kernel may reach another device: no remote copies, remote signals or barrier semaphores. Data moves between devices by JAX's collectives and lax.ppermute only.
A program may use at most 128 MiB of HBM per device.

```python
import jax
import jax.numpy as jnp
from jax import lax

F = 256
BLK = 128
EMAX = 256
TILE_DEV = 256
ROWS_DEV = 128
GROUP_BLK = 4
CLASS_BLK = 8
NODES = 4096
TILES = 8192
N_ROW = 8
N_REP = 4


def draw_tile_count(key, part):
    first_key, second_key, third_key = jax.random.split(jax.random.fold_in(key, 7), 3)
    devices_all = TILES // TILE_DEV
    lowest = jax.random.randint(first_key, (devices_all, 1), EMAX // 4, EMAX + 1)
    spread_bits = jax.random.randint(second_key, (devices_all, TILE_DEV), 0, 1 << 20)
    counts = lowest + spread_bits % (EMAX + 1 - lowest)
    position = jax.random.randint(third_key, (devices_all, 1), 0, TILE_DEV)
    slots = jnp.arange(TILE_DEV, dtype=jnp.int32)[None, :]
    counts = jnp.where(slots == position, EMAX, counts)
    return counts.reshape(TILES).astype(jnp.int32)


def set_ends(drawn, stream_key, least, largest):
    longest = drawn.shape.index(max(drawn.shape))
    spots = []
    for shift in (0, 1):
        where = [jax.random.randint(jax.random.fold_in(stream_key, axis), (), 0, length) for axis, length in enumerate(drawn.shape)]
        where[longest] = (where[longest] + shift) % drawn.shape[longest]
        spots.append(tuple(where))
    return drawn.at[spots[0]].set(least).at[spots[1]].set(largest)


def level_of(own_key, dims, cuts, low, high):
    factor_of, own = 1.0, jax.random.fold_in(own_key, 6)
    for dim, parts in cuts:
        draws = jnp.exp(jax.random.uniform(jax.random.fold_in(own, dim), (parts,), jnp.float32, low / len(cuts), high / len(cuts)))
        factor_of = factor_of * jnp.repeat(draws, dims[dim] // parts).reshape([-1 if axis == dim else 1 for axis in range(len(dims))])
    return factor_of


def scatter_about(key, shape, width, reach, cuts=(), kind=jnp.bfloat16):
    array = width * jax.random.normal(key, shape, jnp.float32)
    if cuts:
        array = array * level_of(key, shape, cuts, -0.22, 0.18)
    return jnp.clip(array, -reach, reach).astype(kind)


def setup_inputs(seed: int = 0) -> dict:
    keys = jax.random.split(jax.random.key(seed), 11)
    features = scatter_about(keys[0], (NODES, F), 1.0, 6.0, ((0, 32),))
    w_self = scatter_about(keys[1], (F, F), F ** -0.5, 0.375)
    w_neigh = scatter_about(keys[2], (F, F), (F // 4) ** -0.5, 0.75)
    bias = scatter_about(keys[3], (F,), 0.5, 3.0, (), jnp.float32)
    d_out = scatter_about(keys[4], (NODES, F), 1.0, 6.0, ((0, 32),))
    tile_row = set_ends(jax.random.randint(keys[5], (TILES,), 0, GROUP_BLK), jax.random.fold_in(keys[5], 1), 0, GROUP_BLK - 1).astype(jnp.int32)
    tile_col = set_ends(jax.random.randint(keys[6], (TILES,), 0, CLASS_BLK), jax.random.fold_in(keys[6], 1), 0, CLASS_BLK - 1).astype(jnp.int32)
    tile_count = draw_tile_count(jax.random.fold_in(keys[10], 71), 0)
    edge_src = set_ends(jax.random.randint(keys[8], (TILES, EMAX), 0, BLK), jax.random.fold_in(keys[8], 1), 0, BLK - 1).astype(jnp.int32)
    edge_dst = set_ends(jax.random.randint(keys[9], (TILES, EMAX), 0, BLK), jax.random.fold_in(keys[9], 1), 0, BLK - 1).astype(jnp.int32)
    return dict(features=features, w_self=w_self, w_neigh=w_neigh, bias=bias, d_out=d_out, tile_row=tile_row, tile_col=tile_col, tile_count=tile_count, edge_src=edge_src, edge_dst=edge_dst)


def smooth_gate(value):
    return jax.nn.gelu(value, approximate=True)

def tile_pieces(device, tile_row, tile_col, tile_count, edge_src, edge_dst):
    first = device * TILE_DEV
    rows_of = lax.dynamic_slice_in_dim(tile_row, first, TILE_DEV, 0)
    cols_of = lax.dynamic_slice_in_dim(tile_col, first, TILE_DEV, 0)
    counts_of = lax.dynamic_slice_in_dim(tile_count, first, TILE_DEV, 0)
    src_of = lax.dynamic_slice_in_dim(edge_src, first, TILE_DEV, 0)
    dst_of = lax.dynamic_slice_in_dim(edge_dst, first, TILE_DEV, 0)
    lanes = jnp.arange(BLK, dtype=jnp.int32)
    live = jnp.arange(EMAX, dtype=jnp.int32)[None, :] < counts_of[:, None]
    dst_hot = ((dst_of[:, :, None] == lanes) & live[:, :, None]).astype(jnp.float32)
    src_hot = (src_of[:, :, None] == lanes).astype(jnp.float32)
    adjacency = jnp.einsum('teb,tec->tbc', dst_hot, src_hot).astype(jnp.bfloat16)
    row_hot = (rows_of[:, None] == jnp.arange(GROUP_BLK, dtype=jnp.int32)).astype(jnp.float32)
    col_hot = (cols_of[:, None] == jnp.arange(CLASS_BLK, dtype=jnp.int32)).astype(jnp.float32)
    return (adjacency, row_hot, col_hot, rows_of, cols_of)

def reference(features, w_self, w_neigh, bias, d_out, tile_row, tile_col, tile_count, edge_src, edge_dst):
    group = GROUP_BLK * BLK
    lattice = features.reshape(N_ROW, N_REP, ROWS_DEV, F)

    def forward_step(device, carry):
        agg_sum, degree = carry
        rank = device // N_REP
        klass = device % N_REP
        adjacency, row_hot, col_hot, rows_of, cols_of = tile_pieces(device, tile_row, tile_col, tile_count, edge_src, edge_dst)
        members = lax.dynamic_index_in_dim(lattice, klass, 1, keepdims=False).reshape(CLASS_BLK, BLK, F)
        col_blocks = members[cols_of]
        contrib = jnp.einsum('tbc,tcf->tbf', adjacency.astype(jnp.float32), col_blocks.astype(jnp.float32))
        part = jnp.einsum('tg,tbf->gbf', row_hot, contrib).reshape(group, F)
        in_degree = lax.optimization_barrier(jnp.sum(adjacency.astype(jnp.float32), axis=2))
        part_degree = jnp.einsum('tg,tb->gb', row_hot, in_degree).reshape(group)
        start = (rank * group).astype(jnp.int32)
        agg_sum = lax.dynamic_update_slice_in_dim(agg_sum, lax.dynamic_slice_in_dim(agg_sum, start, group, 0) + part, start, 0)
        degree = lax.dynamic_update_slice_in_dim(degree, lax.dynamic_slice_in_dim(degree, start, group, 0) + part_degree, start, 0)
        return (agg_sum, degree)
    start_carry = (jnp.zeros((NODES, F), jnp.float32), jnp.zeros((NODES,), jnp.float32))
    agg_sum, degree = lax.fori_loop(0, N_ROW * N_REP, forward_step, start_carry)
    inverse = 1.0 / jnp.maximum(degree, 1.0)
    agg = (agg_sum * inverse[:, None]).astype(jnp.bfloat16)
    pre = jnp.dot(features, w_self, preferred_element_type=jnp.float32) + jnp.dot(agg, w_neigh, preferred_element_type=jnp.float32) + bias
    out_full, pullback = jax.vjp(smooth_gate, pre)
    out = out_full.astype(jnp.bfloat16)
    d_pre = pullback(d_out.astype(jnp.float32))[0].astype(jnp.bfloat16)
    grad_self = jnp.dot(features.T, d_pre, preferred_element_type=jnp.float32)
    grad_neigh = jnp.dot(agg.T, d_pre, preferred_element_type=jnp.float32)
    grad_bias = lax.optimization_barrier(jnp.sum(d_pre.astype(jnp.float32), axis=0))
    g_agg = (jnp.dot(d_pre, w_neigh.T, preferred_element_type=jnp.float32) * inverse[:, None]).astype(jnp.bfloat16)

    def backward_step(device, spread):
        rank = device // N_REP
        klass = device % N_REP
        adjacency, row_hot, col_hot, rows_of, cols_of = tile_pieces(device, tile_row, tile_col, tile_count, edge_src, edge_dst)
        start = (rank * group).astype(jnp.int32)
        g_group = lax.dynamic_slice_in_dim(g_agg, start, group, 0).reshape(GROUP_BLK, BLK, F)
        row_blocks = g_group[rows_of]
        back = jnp.einsum('tbc,tbf->tcf', adjacency.astype(jnp.float32), row_blocks.astype(jnp.float32))
        col_part = jnp.einsum('tk,tcf->kcf', col_hot, back).reshape(N_ROW, ROWS_DEV, F)
        current = lax.dynamic_index_in_dim(spread, klass, 1, keepdims=False)
        return lax.dynamic_update_index_in_dim(spread, current + col_part, klass, 1)
    spread = lax.fori_loop(0, N_ROW * N_REP, backward_step, jnp.zeros((N_ROW, N_REP, ROWS_DEV, F), jnp.float32))
    d_features = jnp.dot(d_pre, w_self.T, preferred_element_type=jnp.float32) + spread.reshape(NODES, F)
    return (out, d_features, grad_self, grad_neigh, grad_bias)
```

```python
import jax
import jax.numpy as jnp
from jax import lax
from jax.experimental import pallas as pl
from jax.experimental.pallas import tpu as pltpu
from jax.sharding import PartitionSpec as P

BLK = 128
PAD = 16
BF16 = jnp.bfloat16
F32 = jnp.float32
UNROLL = 8
VMEM = pl.BlockSpec(memory_space=pltpu.VMEM)
SMEM = pl.BlockSpec(memory_space=pltpu.SMEM)


def params():
    return pltpu.CompilerParams(vmem_limit_bytes=56 * 1024 * 1024)


def row_place(block):
    away = block ^ lax.axis_index("rep")
    return ((away & 1) << 1) | (away >> 1)


def col_place(block, row_count):
    me = lax.axis_index("row")
    half = row_count // 2
    return 2 * lax.rem((me >> 1) - (block >> 1) + half, half) + ((block ^ me) & 1)


def col_block(place, row_count):
    me = lax.axis_index("row")
    half = row_count // 2
    return 2 * lax.rem((me >> 1) - place // 2 + half, half) + ((me & 1) ^ (place & 1))


def split(value):
    high = value.astype(BF16).astype(F32)
    line = lax.broadcasted_iota(jnp.int32, (PAD, value.shape[1]), 0)
    return jnp.where(line == 0, high, jnp.where(line == 1, value - high, 0.0)).astype(BF16)


def joined(rows):
    rows = rows.astype(F32)
    return rows[0:1] + rows[1:2]


def build_kernel(row_ref, col_ref, count_ref, src_ref, dst_ref, adj_ref, acc_ref):
    tiles, slots = src_ref.shape
    row_blocks, col_blocks = acc_ref.shape[:2]
    acc_ref[...] = jnp.zeros_like(acc_ref)
    line = lax.broadcasted_iota(jnp.int32, (BLK, slots), 0).astype(BF16)
    slot = lax.broadcasted_iota(jnp.int32, (1, slots), 1)
    one, zero = jnp.ones((), BF16), jnp.zeros((), BF16)

    def step(i, carry):
        base = pl.multiple_of(i * UNROLL, UNROLL)
        dst, src = dst_ref[pl.ds(base, UNROLL), :], src_ref[pl.ds(base, UNROLL), :]
        for u in range(UNROLL):
            tile = base + u
            live = jnp.where(slot < count_ref[tile], dst[u : u + 1], -1)
            dst_hot = jnp.where(line == live.astype(BF16), one, zero)
            src_hot = jnp.where(line == src[u : u + 1].astype(BF16), one, zero)
            part = lax.dot_general(
                dst_hot, src_hot, (((1,), (1,)), ((), ())), preferred_element_type=F32
            )
            acc_ref[row_place(row_ref[tile]), col_place(col_ref[tile], col_blocks)] += part
        return carry

    lax.fori_loop(0, tiles // UNROLL, step, 0)
    for g in range(row_blocks):
        for c in range(col_blocks):
            adj_ref[g * BLK : (g + 1) * BLK, c * BLK : (c + 1) * BLK] = acc_ref[g, c].astype(BF16)


def gather_kernel(adj_ref, *refs):
    *feature_refs, keep_ref, send_ref = refs
    half = keep_ref.shape[0] - PAD
    total, at = None, 0
    for ref in feature_refs:
        size = ref.shape[0]
        part = jnp.dot(adj_ref[:, at : at + size], ref[...], preferred_element_type=F32)
        total = part if total is None else total + part
        at += size
    ones = jnp.ones((PAD, adj_ref.shape[1]), BF16)
    degree = lax.dot_general(
        ones, adj_ref[...], (((1,), (1,)), ((), ())), preferred_element_type=F32
    )
    keep_ref[:half] = total[:half]
    keep_ref[half:] = degree[:, :half]
    send_ref[:half] = total[half:].astype(BF16)
    send_ref[half:] = split(degree[:1, half:])


def pair_kernel(keep_ref, got_ref, pair_ref):
    half = keep_ref.shape[0] - PAD
    pair_ref[:half] = (keep_ref[:half] + got_ref[:half].astype(F32)).astype(BF16)
    pair_ref[half:] = split(keep_ref[half : half + 1] + joined(got_ref[half:]))


def node_kernel(
    pair_ref, got_ref, own_ref, near_ref, w_self_ref, w_neigh_ref, bias_ref,
    out_ref, self_ref, keep_ref, send_ref,
):
    rows, width = out_ref.shape
    half = 2 * rows
    swapped = jnp.concatenate([got_ref[rows:half], got_ref[:rows]], axis=0).astype(F32)
    sums = pair_ref[:half].astype(F32) + swapped
    far = joined(got_ref[half:])
    degree = joined(pair_ref[half:]) + jnp.concatenate([far[:, rows:], far[:, :rows]], axis=1)
    inverse_row = 1.0 / jnp.maximum(degree, 1.0)
    diagonal = lax.broadcasted_iota(jnp.int32, (half, half), 0) == lax.broadcasted_iota(
        jnp.int32, (half, half), 1
    )
    inverse = jnp.sum(jnp.where(diagonal, inverse_row, 0.0), axis=1, keepdims=True)
    agg = (sums * inverse).astype(BF16)
    features = jnp.concatenate([own_ref[:rows], near_ref[:rows]], axis=0)
    d_out = jnp.concatenate([own_ref[rows:], near_ref[rows:]], axis=0).astype(F32)
    pre = (
        jnp.dot(features, w_self_ref[...], preferred_element_type=F32)
        + jnp.dot(agg, w_neigh_ref[...], preferred_element_type=F32)
        + bias_ref[...]
    )
    square = pre * pre
    bend = jnp.tanh(0.7978845608 * pre * (1.0 + 0.044715 * square))
    out_ref[...] = (0.5 * pre[:rows] * (1.0 + bend[:rows])).astype(BF16)
    slope = 0.5 * (1.0 + bend) + 0.5 * pre * (1.0 - bend * bend) * (
        0.7978845608 * (1.0 + 3.0 * 0.044715 * square)
    )
    d_pre = (d_out * slope).astype(BF16)
    transposed = (((1,), (1,)), ((), ()))
    self_ref[...] = lax.dot_general(
        d_pre[:rows], w_self_ref[...], transposed, preferred_element_type=F32
    )
    back = lax.dot_general(d_pre, w_neigh_ref[...], transposed, preferred_element_type=F32)
    send_ref[:half] = (back * inverse).astype(BF16)
    me = lax.axis_index("rep")
    terms = jnp.where(me >> 1 == 0, features, agg)
    grads = lax.dot_general(terms, d_pre, (((0,), (0,)), ((), ())), preferred_element_type=F32)
    middle = width // 2
    low = me & 1 == 0
    bias_term = jnp.sum(d_pre.astype(F32), axis=0, keepdims=True)
    keep_ref[:middle] = jnp.where(low, grads[:middle], grads[middle:])
    keep_ref[middle:] = jnp.broadcast_to(bias_term, (PAD, width))
    send_ref[half : half + middle] = jnp.where(low, grads[middle:], grads[:middle]).astype(BF16)
    send_ref[half + middle :] = split(bias_term)


def spread_kernel(adj_ref, sent_ref, got_ref, keep_ref, msg_ref):
    row_count = msg_ref.shape[0]
    half = adj_ref.shape[0] // 2
    middle = keep_ref.shape[0] - PAD
    share = middle // row_count
    g = jnp.concatenate([sent_ref[:half], got_ref[:half]], axis=0)
    grads = keep_ref[:middle] + got_ref[half : half + middle].astype(F32)
    bias_rows = split(keep_ref[middle : middle + 1] + joined(got_ref[half + middle :]))
    for place in range(row_count):
        block = lax.dot_general(
            adj_ref[:, place * BLK : (place + 1) * BLK],
            g,
            (((0,), (0,)), ((), ())),
            preferred_element_type=F32,
        )
        msg_ref[col_block(place, row_count), :BLK] = block.astype(BF16)
    for k in range(row_count):
        msg_ref[k, BLK : BLK + share] = grads[k * share : (k + 1) * share].astype(BF16)
        if share < PAD:
            msg_ref[k, BLK + share : BLK + PAD] = jnp.zeros((PAD - share, grads.shape[1]), BF16)
        msg_ref[k, BLK + PAD :] = bias_rows


def finish_kernel(msg_ref, self_ref, d_features_ref, share_ref, bias_ref):
    row_count = msg_ref.shape[0]
    total = msg_ref[0].astype(F32)
    for k in range(1, row_count):
        total = total + msg_ref[k].astype(F32)
    d_features_ref[...] = self_ref[...] + total[:BLK]
    share_ref[...] = total[BLK : BLK + PAD].astype(BF16)
    bias_ref[...] = total[BLK + PAD : BLK + PAD + 1] + total[BLK + PAD + 1 : BLK + PAD + 2]


def call(kernel, out_shape, specs, scratch=()):
    many = isinstance(out_shape, (list, tuple))
    return pl.pallas_call(
        kernel,
        out_shape=out_shape,
        in_specs=specs,
        out_specs=[VMEM] * len(out_shape) if many else VMEM,
        scratch_shapes=list(scratch),
        compiler_params=params(),
    )


def on_device(
    features, w_self, w_neigh, bias, d_out, tile_row, tile_col, tile_count, edge_src, edge_dst
):
    rows, width = features.shape
    row_count, rep_count = lax.axis_size("row"), lax.axis_size("rep")
    group, columns = rep_count * rows, row_count * rows
    half, middle = group // 2, width // 2
    shape = jax.ShapeDtypeStruct

    def swap(value, axis, bit):
        return lax.ppermute(value, axis, [(i, i ^ bit) for i in range(lax.axis_size(axis))])

    pair = jnp.concatenate([features, swap(features, "row", 1)], axis=0)
    pieces = [pair] + [
        lax.ppermute(pair, "row", [(i, (i + 2 * s) % row_count) for i in range(row_count)])
        for s in range(1, row_count // 2)
    ]
    own = jnp.concatenate([features, d_out], axis=0)
    near = swap(own, "rep", 2)
    adjacency = call(
        build_kernel,
        shape((group, columns), BF16),
        [SMEM, SMEM, SMEM, VMEM, VMEM],
        [pltpu.VMEM((rep_count, row_count, BLK, BLK), F32)],
    )(tile_row, tile_col, tile_count, edge_src, edge_dst)
    keep, send = call(
        gather_kernel,
        (shape((half + PAD, width), F32), shape((half + PAD, width), BF16)),
        [VMEM] * (1 + len(pieces)),
    )(adjacency, *pieces)
    pair_sum = call(pair_kernel, shape((half + PAD, width), BF16), [VMEM] * 2)(
        keep, swap(send, "rep", 1)
    )
    out, self_term, keep, send = call(
        node_kernel,
        (
            shape((rows, width), BF16),
            shape((rows, width), F32),
            shape((middle + PAD, width), F32),
            shape((half + middle + PAD, width), BF16),
        ),
        [VMEM] * 7,
    )(pair_sum, swap(pair_sum, "rep", 2), own, near, w_self, w_neigh, bias[None, :])
    message = call(
        spread_kernel, shape((row_count, BLK + 2 * PAD, width), BF16), [VMEM] * 4
    )(adjacency, send, swap(send, "rep", 1), keep)
    message = lax.all_to_all(message, "row", 0, 0, tiled=True)
    d_features, share, grad_bias = call(
        finish_kernel,
        (shape((rows, width), F32), shape((PAD, width), BF16), shape((1, width), F32)),
        [VMEM] * 2,
    )(message, self_term)
    share = share[: middle // row_count]
    quarter = lax.all_to_all(
        jnp.broadcast_to(share[None], (row_count,) + share.shape), "row", 0, 0, tiled=True
    ).reshape(middle, width)
    grads = lax.all_gather(quarter, "rep", axis=0, tiled=True).astype(F32)
    return (out, d_features, grads[:width], grads[width:], grad_bias[0])


def solution(mesh):
    return jax.shard_map(
        on_device,
        mesh=mesh,
        in_specs=(
            P(("row", "rep"), None),
            P(),
            P(),
            P(),
            P(("row", "rep"), None),
            P(("row", "rep")),
            P(("row", "rep")),
            P(("row", "rep")),
            P(("row", "rep"), None),
            P(("row", "rep"), None),
        ),
        out_specs=(P(("row", "rep"), None), P(("row", "rep"), None), P(), P(), P()),
        check_vma=False,
    )
```

```python
import math

import jax
import jax.numpy as jnp
from jax import lax
from jax.experimental import pallas as pl
from jax.experimental.pallas import tpu as pltpu
from jax.sharding import PartitionSpec as P

BLK = 128
PAD = 16
BF16 = jnp.bfloat16
F32 = jnp.float32
UNROLL = 32
VMEM = pl.BlockSpec(memory_space=pltpu.VMEM)
SMEM = pl.BlockSpec(memory_space=pltpu.SMEM)


def size_of(value):
    return math.prod(value.shape) * jnp.dtype(value.dtype).itemsize


def row_place(block):
    away = block ^ lax.axis_index("rep")
    return ((away & 1) << 1) | (away >> 1)


def col_place(block, row_count):
    me = lax.axis_index("row")
    half = row_count // 2
    return 2 * lax.rem((me >> 1) - (block >> 1) + half, half) + ((block ^ me) & 1)


def col_block(place, row_count):
    me = lax.axis_index("row")
    half = row_count // 2
    return 2 * lax.rem((me >> 1) - place // 2 + half, half) + ((me & 1) ^ (place & 1))


def split(value):
    high = value.astype(BF16).astype(F32)
    line = lax.broadcasted_iota(jnp.int32, (PAD, value.shape[1]), 0)
    return jnp.where(line == 0, high, jnp.where(line == 1, value - high, 0.0)).astype(BF16)


def joined(rows):
    rows = rows.astype(F32)
    return rows[0:1] + rows[1:2]


def build_kernel(row_ref, col_ref, count_ref, src_ref, dst_ref, adj_ref, acc_ref):
    tiles, slots = src_ref.shape
    row_blocks, col_blocks = acc_ref.shape[:2]
    acc_ref[...] = jnp.zeros_like(acc_ref)
    line = lax.broadcasted_iota(jnp.int32, (BLK, slots), 0).astype(BF16)
    slot = lax.broadcasted_iota(jnp.int32, (1, slots), 1)
    one, zero = jnp.ones((), BF16), jnp.zeros((), BF16)

    def step(i, carry):
        base = pl.multiple_of(i * UNROLL, UNROLL)
        dst, src = dst_ref[pl.ds(base, UNROLL), :], src_ref[pl.ds(base, UNROLL), :]
        for u in range(UNROLL):
            tile = base + u
            live = jnp.where(slot < count_ref[tile], dst[u : u + 1], -1)
            dst_hot = jnp.where(line == live.astype(BF16), one, zero)
            src_hot = jnp.where(line == src[u : u + 1].astype(BF16), one, zero)
            part = lax.dot_general(
                dst_hot, src_hot, (((1,), (1,)), ((), ())), preferred_element_type=F32
            )
            acc_ref[row_place(row_ref[tile]), col_place(col_ref[tile], col_blocks)] += part
        return carry

    lax.fori_loop(0, tiles // UNROLL, step, 0)
    for g in range(row_blocks):
        for c in range(col_blocks):
            adj_ref[g * BLK : (g + 1) * BLK, c * BLK : (c + 1) * BLK] = acc_ref[g, c].astype(BF16)


def gather_kernel(adj_ref, *refs):
    *feature_refs, keep_ref, send_ref = refs
    half = keep_ref.shape[0] - PAD
    total, at = None, 0
    for ref in feature_refs:
        size = ref.shape[0]
        part = jnp.dot(adj_ref[:, at : at + size], ref[...], preferred_element_type=F32)
        total = part if total is None else total + part
        at += size
    ones = jnp.ones((PAD, adj_ref.shape[1]), BF16)
    degree = lax.dot_general(
        ones, adj_ref[...], (((1,), (1,)), ((), ())), preferred_element_type=F32
    )
    keep_ref[:half] = total[:half]
    keep_ref[half:] = degree[:, :half]
    send_ref[:half] = total[half:].astype(BF16)
    send_ref[half:] = split(degree[:1, half:])


def pair_kernel(keep_ref, got_ref, pair_ref):
    half = keep_ref.shape[0] - PAD
    pair_ref[:half] = (keep_ref[:half] + got_ref[:half].astype(F32)).astype(BF16)
    pair_ref[half:] = split(keep_ref[half : half + 1] + joined(got_ref[half:]))


def node_kernel(
    pair_ref, got_ref, own_ref, near_ref, w_self_ref, w_neigh_ref, bias_ref,
    out_ref, self_ref, keep_ref, send_ref,
):
    rows, width = out_ref.shape
    half = 2 * rows
    swapped = jnp.concatenate([got_ref[rows:half], got_ref[:rows]], axis=0).astype(F32)
    sums = pair_ref[:half].astype(F32) + swapped
    far = joined(got_ref[half:])
    degree = joined(pair_ref[half:]) + jnp.concatenate([far[:, rows:], far[:, :rows]], axis=1)
    inverse_row = 1.0 / jnp.maximum(degree, 1.0)
    diagonal = lax.broadcasted_iota(jnp.int32, (half, half), 0) == lax.broadcasted_iota(
        jnp.int32, (half, half), 1
    )
    inverse = jnp.sum(jnp.where(diagonal, inverse_row, 0.0), axis=1, keepdims=True)
    agg = (sums * inverse).astype(BF16)
    features = jnp.concatenate([own_ref[:rows], near_ref[:rows]], axis=0)
    d_out = jnp.concatenate([own_ref[rows:], near_ref[rows:]], axis=0).astype(F32)
    pre = (
        jnp.dot(features, w_self_ref[...], preferred_element_type=F32)
        + jnp.dot(agg, w_neigh_ref[...], preferred_element_type=F32)
        + bias_ref[...]
    )
    square = pre * pre
    bend = jnp.tanh(0.7978845608 * pre * (1.0 + 0.044715 * square))
    out_ref[...] = (0.5 * pre[:rows] * (1.0 + bend[:rows])).astype(BF16)
    slope = 0.5 * (1.0 + bend) + 0.5 * pre * (1.0 - bend * bend) * (
        0.7978845608 * (1.0 + 3.0 * 0.044715 * square)
    )
    d_pre = (d_out * slope).astype(BF16)
    transposed = (((1,), (1,)), ((), ()))
    self_ref[...] = lax.dot_general(
        d_pre[:rows], w_self_ref[...], transposed, preferred_element_type=F32
    )
    back = lax.dot_general(d_pre, w_neigh_ref[...], transposed, preferred_element_type=F32)
    send_ref[:half] = (back * inverse).astype(BF16)
    me = lax.axis_index("rep")
    terms = jnp.where(me >> 1 == 0, features, agg)
    grads = lax.dot_general(terms, d_pre, (((0,), (0,)), ((), ())), preferred_element_type=F32)
    middle = width // 2
    low = me & 1 == 0
    bias_term = jnp.sum(d_pre.astype(F32), axis=0, keepdims=True)
    keep_ref[:middle] = jnp.where(low, grads[:middle], grads[middle:])
    keep_ref[middle:] = jnp.broadcast_to(bias_term, (PAD, width))
    send_ref[half : half + middle] = jnp.where(low, grads[middle:], grads[:middle]).astype(BF16)
    send_ref[half + middle :] = split(bias_term)


def spread_kernel(adj_ref, sent_ref, got_ref, keep_ref, msg_ref):
    row_count = msg_ref.shape[0]
    half = adj_ref.shape[0] // 2
    middle = keep_ref.shape[0] - PAD
    share = middle // row_count
    g = jnp.concatenate([sent_ref[:half], got_ref[:half]], axis=0)
    grads = keep_ref[:middle] + got_ref[half : half + middle].astype(F32)
    bias_rows = split(keep_ref[middle : middle + 1] + joined(got_ref[half + middle :]))
    for place in range(row_count):
        block = lax.dot_general(
            adj_ref[:, place * BLK : (place + 1) * BLK],
            g,
            (((0,), (0,)), ((), ())),
            preferred_element_type=F32,
        )
        msg_ref[col_block(place, row_count), :BLK] = block.astype(BF16)
    for k in range(row_count):
        msg_ref[k, BLK : BLK + share] = grads[k * share : (k + 1) * share].astype(BF16)
        if share < PAD:
            msg_ref[k, BLK + share : BLK + PAD] = jnp.zeros((PAD - share, grads.shape[1]), BF16)
        msg_ref[k, BLK + PAD :] = bias_rows


def finish_kernel(msg_ref, self_ref, d_features_ref, share_ref, bias_ref):
    row_count = msg_ref.shape[0]
    total = msg_ref[0].astype(F32)
    for k in range(1, row_count):
        total = total + msg_ref[k].astype(F32)
    d_features_ref[...] = self_ref[...] + total[:BLK]
    share_ref[...] = total[BLK : BLK + PAD].astype(BF16)
    bias_ref[...] = total[BLK + PAD : BLK + PAD + 1] + total[BLK + PAD + 1 : BLK + PAD + 2]


def call(kernel, out_shape, specs, args, scratch=()):
    outs = out_shape if isinstance(out_shape, (list, tuple)) else [out_shape]
    held = sum(size_of(v) for v in [*args, *outs, *scratch])
    return pl.pallas_call(
        kernel,
        out_shape=out_shape,
        in_specs=specs,
        out_specs=[VMEM] * len(outs) if outs is out_shape else VMEM,
        scratch_shapes=list(scratch),
        compiler_params=pltpu.CompilerParams(vmem_limit_bytes=2 * held + 4 * 1024 * 1024),
    )(*args)


def on_device(
    features, w_self, w_neigh, bias, d_out, tile_row, tile_col, tile_count, edge_src, edge_dst
):
    rows, width = features.shape
    row_count, rep_count = lax.axis_size("row"), lax.axis_size("rep")
    group, columns = rep_count * rows, row_count * rows
    half, middle = group // 2, width // 2
    shape = jax.ShapeDtypeStruct

    def swap(value, axis, bit):
        return lax.ppermute(value, axis, [(i, i ^ bit) for i in range(lax.axis_size(axis))])

    pair = jnp.concatenate([features, swap(features, "row", 1)], axis=0)
    pieces = [pair] + [
        lax.ppermute(pair, "row", [(i, (i + 2 * s) % row_count) for i in range(row_count)])
        for s in range(1, row_count // 2)
    ]
    own = jnp.concatenate([features, d_out], axis=0)
    near = swap(own, "rep", 2)
    adjacency = call(
        build_kernel,
        shape((group, columns), BF16),
        [SMEM, SMEM, SMEM, VMEM, VMEM],
        (tile_row, tile_col, tile_count, edge_src, edge_dst),
        [pltpu.VMEM((rep_count, row_count, BLK, BLK), F32)],
    )
    adjacency, near, pieces = lax.optimization_barrier((adjacency, near, pieces))
    keep, send = call(
        gather_kernel,
        (shape((half + PAD, width), F32), shape((half + PAD, width), BF16)),
        [VMEM] * (1 + len(pieces)),
        (adjacency, *pieces),
    )
    pair_sum = call(
        pair_kernel,
        shape((half + PAD, width), BF16),
        [VMEM] * 2,
        (keep, swap(send, "rep", 1)),
    )
    out, self_term, keep, send = call(
        node_kernel,
        (
            shape((rows, width), BF16),
            shape((rows, width), F32),
            shape((middle + PAD, width), F32),
            shape((half + middle + PAD, width), BF16),
        ),
        [VMEM] * 7,
        (pair_sum, swap(pair_sum, "rep", 2), own, near, w_self, w_neigh, bias[None, :]),
    )
    message = call(
        spread_kernel,
        shape((row_count, BLK + 2 * PAD, width), BF16),
        [VMEM] * 4,
        (adjacency, send, swap(send, "rep", 1), keep),
    )
    message = lax.all_to_all(message, "row", 0, 0, tiled=True)
    d_features, share, grad_bias = call(
        finish_kernel,
        (shape((rows, width), F32), shape((PAD, width), BF16), shape((1, width), F32)),
        [VMEM] * 2,
        (message, self_term),
    )
    share = share[: middle // row_count]
    quarter = lax.all_to_all(
        jnp.broadcast_to(share[None], (row_count,) + share.shape), "row", 0, 0, tiled=True
    ).reshape(middle, width)
    grads = lax.all_gather(quarter, "rep", axis=0, tiled=True).astype(F32)
    return (out, d_features, grads[:width], grads[width:], grad_bias[0])


def solution(mesh):
    return jax.shard_map(
        on_device,
        mesh=mesh,
        in_specs=(
            P(("row", "rep"), None),
            P(),
            P(),
            P(),
            P(("row", "rep"), None),
            P(("row", "rep")),
            P(("row", "rep")),
            P(("row", "rep")),
            P(("row", "rep"), None),
            P(("row", "rep"), None),
        ),
        out_specs=(P(("row", "rep"), None), P(("row", "rep"), None), P(), P(), P()),
        check_vma=False,
    )
```

```python
import math

import jax
import jax.numpy as jnp
from jax import lax
from jax.experimental import pallas as pl
from jax.experimental.pallas import tpu as pltpu
from jax.sharding import PartitionSpec as P

BLK = 128
PAD = 16
BF16 = jnp.bfloat16
F32 = jnp.float32
UNROLL = 32
VMEM = pl.BlockSpec(memory_space=pltpu.VMEM)
SMEM = pl.BlockSpec(memory_space=pltpu.SMEM)


def size_of(value):
    return math.prod(value.shape) * jnp.dtype(value.dtype).itemsize


def row_place(block):
    away = block ^ lax.axis_index("rep")
    return ((away & 1) << 1) | (away >> 1)


def col_place(block, row_count):
    away = block ^ lax.axis_index("row")
    return (away & 3) * (row_count // 4) + (away >> 2)


def tree(values):
    while len(values) > 1:
        values = [values[i] + values[i + 1] for i in range(0, len(values), 2)]
    return values[0]


def split(value):
    high = value.astype(BF16).astype(F32)
    line = lax.broadcasted_iota(jnp.int32, (PAD, value.shape[1]), 0)
    return jnp.where(line == 0, high, jnp.where(line == 1, value - high, 0.0)).astype(BF16)


def joined(rows):
    rows = rows.astype(F32)
    return rows[0:1] + rows[1:2]


def add_tiles(first, last, row_ref, col_ref, count_ref, src_ref, dst_ref, acc_ref):
    slots = src_ref.shape[1]
    col_blocks = acc_ref.shape[1]
    line = lax.broadcasted_iota(jnp.int32, (BLK, slots), 0).astype(BF16)
    slot = lax.broadcasted_iota(jnp.int32, (1, slots), 1)
    one, zero = jnp.ones((), BF16), jnp.zeros((), BF16)

    def step(i, carry):
        base = pl.multiple_of(first + i * UNROLL, UNROLL)
        dst, src = dst_ref[pl.ds(base, UNROLL), :], src_ref[pl.ds(base, UNROLL), :]
        for u in range(UNROLL):
            tile = base + u
            live = jnp.where(slot < count_ref[tile], dst[u : u + 1], -1)
            dst_hot = jnp.where(line == live.astype(BF16), one, zero)
            src_hot = jnp.where(line == src[u : u + 1].astype(BF16), one, zero)
            part = lax.dot_general(
                dst_hot, src_hot, (((1,), (1,)), ((), ())), preferred_element_type=F32
            )
            acc_ref[row_place(row_ref[tile]), col_place(col_ref[tile], col_blocks)] += part
        return carry

    lax.fori_loop(0, (last - first) // UNROLL, step, 0)


def first_build_kernel(row_ref, col_ref, count_ref, src_ref, dst_ref, acc_ref):
    acc_ref[...] = jnp.zeros_like(acc_ref)
    tiles = src_ref.shape[0]
    add_tiles(0, tiles // 2, row_ref, col_ref, count_ref, src_ref, dst_ref, acc_ref)


def last_build_kernel(row_ref, col_ref, count_ref, src_ref, dst_ref, half_ref, adj_ref, acc_ref):
    acc_ref[...] = half_ref[...]
    tiles = src_ref.shape[0]
    add_tiles(tiles // 2, tiles, row_ref, col_ref, count_ref, src_ref, dst_ref, acc_ref)
    row_blocks, col_blocks = acc_ref.shape[:2]
    for g in range(row_blocks):
        for c in range(col_blocks):
            adj_ref[g * BLK : (g + 1) * BLK, c * BLK : (c + 1) * BLK] = acc_ref[g, c].astype(BF16)


def gather_kernel(adj_ref, *refs):
    *feature_refs, keep_ref, send_ref = refs
    half = keep_ref.shape[0] - PAD
    total, at = None, 0
    for ref in feature_refs:
        size = ref.shape[0]
        part = jnp.dot(adj_ref[:, at : at + size], ref[...], preferred_element_type=F32)
        total = part if total is None else total + part
        at += size
    ones = jnp.ones((PAD, adj_ref.shape[1]), BF16)
    degree = lax.dot_general(
        ones, adj_ref[...], (((1,), (1,)), ((), ())), preferred_element_type=F32
    )
    keep_ref[:half] = total[:half]
    keep_ref[half:] = degree[:, :half]
    send_ref[:half] = total[half:].astype(BF16)
    send_ref[half:] = split(degree[:1, half:])


def pair_kernel(keep_ref, got_ref, pair_ref):
    half = keep_ref.shape[0] - PAD
    pair_ref[:half] = (keep_ref[:half] + got_ref[:half].astype(F32)).astype(BF16)
    pair_ref[half:] = split(keep_ref[half : half + 1] + joined(got_ref[half:]))


def node_kernel(
    pair_ref, got_ref, own_ref, near_ref, w_self_ref, w_neigh_ref, bias_ref,
    out_ref, self_ref, keep_ref, send_ref,
):
    rows, width = out_ref.shape
    half = 2 * rows
    swapped = jnp.concatenate([got_ref[rows:half], got_ref[:rows]], axis=0).astype(F32)
    sums = pair_ref[:half].astype(F32) + swapped
    far = joined(got_ref[half:])
    degree = joined(pair_ref[half:]) + jnp.concatenate([far[:, rows:], far[:, :rows]], axis=1)
    inverse_row = 1.0 / jnp.maximum(degree, 1.0)
    diagonal = lax.broadcasted_iota(jnp.int32, (half, half), 0) == lax.broadcasted_iota(
        jnp.int32, (half, half), 1
    )
    inverse = jnp.sum(jnp.where(diagonal, inverse_row, 0.0), axis=1, keepdims=True)
    agg = (sums * inverse).astype(BF16)
    features = jnp.concatenate([own_ref[:rows], near_ref[:rows]], axis=0)
    d_out = jnp.concatenate([own_ref[rows:], near_ref[rows:]], axis=0).astype(F32)
    pre = (
        jnp.dot(features, w_self_ref[...], preferred_element_type=F32)
        + jnp.dot(agg, w_neigh_ref[...], preferred_element_type=F32)
        + bias_ref[...]
    )
    square = pre * pre
    bend = jnp.tanh(0.7978845608 * pre * (1.0 + 0.044715 * square))
    out_ref[...] = (0.5 * pre[:rows] * (1.0 + bend[:rows])).astype(BF16)
    slope = 0.5 * (1.0 + bend) + 0.5 * pre * (1.0 - bend * bend) * (
        0.7978845608 * (1.0 + 3.0 * 0.044715 * square)
    )
    d_pre = (d_out * slope).astype(BF16)
    transposed = (((1,), (1,)), ((), ()))
    self_ref[...] = lax.dot_general(
        d_pre[:rows], w_self_ref[...], transposed, preferred_element_type=F32
    )
    back = lax.dot_general(d_pre, w_neigh_ref[...], transposed, preferred_element_type=F32)
    send_ref[:half] = (back * inverse).astype(BF16)
    me = lax.axis_index("rep")
    terms = jnp.where(me >> 1 == 0, features, agg)
    grads = lax.dot_general(terms, d_pre, (((0,), (0,)), ((), ())), preferred_element_type=F32)
    middle = width // 2
    low = me & 1 == 0
    bias_term = jnp.sum(d_pre[:rows].astype(F32), axis=0, keepdims=True) + jnp.sum(
        d_pre[rows:].astype(F32), axis=0, keepdims=True
    )
    keep_ref[:middle] = jnp.where(low, grads[:middle], grads[middle:])
    keep_ref[middle:] = split(bias_term).astype(F32)
    send_ref[half : half + middle] = jnp.where(low, grads[middle:], grads[:middle]).astype(BF16)
    send_ref[half + middle :] = split(bias_term)


def spread_kernel(adj_ref, sent_ref, got_ref, terms_ref, keep_ref, *msg_refs):
    half = adj_ref.shape[0] // 2
    middle = terms_ref.shape[0] - PAD
    size = adj_ref.shape[1] // 4
    g = jnp.concatenate([sent_ref[:half], got_ref[:half]], axis=0)
    grads = (terms_ref[:middle] + got_ref[half : half + middle].astype(F32)).astype(BF16)
    bias_rows = split(joined(terms_ref[middle:]) + joined(got_ref[half + middle :]))
    for m, ref in enumerate([keep_ref, *msg_refs]):
        blocks = lax.dot_general(
            adj_ref[:, m * size : (m + 1) * size],
            g,
            (((0,), (0,)), ((), ())),
            preferred_element_type=F32,
        )
        ref[:size] = blocks.astype(ref.dtype)
        ref[size : size + middle] = grads.astype(ref.dtype)
        ref[size + middle :] = bias_rows.astype(ref.dtype)


def near_sum_kernel(keep_ref, *refs):
    *got_refs, own_ref = refs[:4]
    msg_refs = refs[4:]
    size = (1 + len(msg_refs)) * BLK
    middle = keep_ref.shape[0] - size - PAD
    terms = [keep_ref, *got_refs]
    blocks = tree([ref[:size].astype(F32) for ref in terms])
    grads = tree([ref[size : size + middle].astype(F32) for ref in terms]).astype(BF16)
    bias_rows = split(tree([joined(ref[size + middle :]) for ref in terms]))
    for h, ref in enumerate([own_ref, *msg_refs]):
        ref[:BLK] = blocks[h * BLK : (h + 1) * BLK].astype(ref.dtype)
        ref[BLK : BLK + middle] = grads.astype(ref.dtype)
        ref[BLK + middle :] = bias_rows.astype(ref.dtype)


def finish_kernel(self_ref, own_ref, *refs):
    *got_refs, d_features_ref, quarter_ref, bias_ref = refs
    middle = own_ref.shape[0] - BLK - PAD
    terms = [own_ref, *got_refs]
    d_features_ref[...] = self_ref[...] + tree([ref[:BLK].astype(F32) for ref in terms])
    quarter_ref[...] = tree([ref[BLK : BLK + middle].astype(F32) for ref in terms]).astype(BF16)
    bias_ref[...] = tree([joined(ref[BLK + middle :]) for ref in terms])


def call(kernel, out_shape, specs, args, scratch=()):
    outs = out_shape if isinstance(out_shape, (list, tuple)) else [out_shape]
    held = sum(size_of(v) for v in [*args, *outs, *scratch])
    return pl.pallas_call(
        kernel,
        out_shape=out_shape,
        in_specs=specs,
        out_specs=[VMEM] * len(outs) if outs is out_shape else VMEM,
        scratch_shapes=list(scratch),
        compiler_params=pltpu.CompilerParams(vmem_limit_bytes=2 * held + 4 * 1024 * 1024),
    )(*args)


def on_device(
    features, w_self, w_neigh, bias, d_out, tile_row, tile_col, tile_count, edge_src, edge_dst
):
    rows, width = features.shape
    row_count, rep_count = lax.axis_size("row"), lax.axis_size("rep")
    group, columns = rep_count * rows, row_count * rows
    half, middle = group // 2, width // 2
    far = row_count // 4
    shape = jax.ShapeDtypeStruct

    def swap(value, axis, bits):
        return lax.ppermute(value, axis, [(i, i ^ bits) for i in range(lax.axis_size(axis))])

    far_pieces = [swap(features, "row", 4 * h) for h in range(1, far)]
    own = jnp.concatenate([features, d_out], axis=0)
    near = swap(own, "rep", 2)
    tiles = (tile_row, tile_col, tile_count, edge_src, edge_dst)
    tile_specs = [SMEM, SMEM, SMEM, VMEM, VMEM]
    acc_shape = (rep_count, row_count, BLK, BLK)
    acc = call(first_build_kernel, shape(acc_shape, F32), tile_specs, tiles)
    acc, far_pieces = lax.optimization_barrier((acc, far_pieces))
    line = jnp.concatenate([features, *far_pieces], axis=0)
    pieces = [line] + [swap(line, "row", m) for m in range(1, 4)]
    adjacency = call(
        last_build_kernel,
        shape((group, columns), BF16),
        tile_specs + [VMEM],
        (*tiles, acc),
        [pltpu.VMEM(acc_shape, F32)],
    )
    adjacency, near, pieces = lax.optimization_barrier((adjacency, near, pieces))
    keep, send = call(
        gather_kernel,
        (shape((half + PAD, width), F32), shape((half + PAD, width), BF16)),
        [VMEM] * (1 + len(pieces)),
        (adjacency, *pieces),
    )
    pair_sum = call(
        pair_kernel,
        shape((half + PAD, width), BF16),
        [VMEM] * 2,
        (keep, swap(send, "rep", 1)),
    )
    out, self_term, keep, send = call(
        node_kernel,
        (
            shape((rows, width), BF16),
            shape((rows, width), F32),
            shape((middle + PAD, width), F32),
            shape((half + middle + PAD, width), BF16),
        ),
        [VMEM] * 7,
        (pair_sum, swap(pair_sum, "rep", 2), own, near, w_self, w_neigh, bias[None, :]),
    )
    terms = middle + PAD
    keep, *near_msgs = call(
        spread_kernel,
        (shape((far * BLK + terms, width), F32),) + (shape((far * BLK + terms, width), BF16),) * 3,
        [VMEM] * 4,
        (adjacency, send, swap(send, "rep", 1), keep),
    )
    got = [swap(msg, "row", m + 1) for m, msg in enumerate(near_msgs)]
    keep, *far_msgs = call(
        near_sum_kernel,
        (shape((BLK + terms, width), F32),) + (shape((BLK + terms, width), BF16),) * (far - 1),
        [VMEM] * 4,
        (keep, *got),
    )
    got = [swap(msg, "row", 4 * (h + 1)) for h, msg in enumerate(far_msgs)]
    d_features, quarter, grad_bias = call(
        finish_kernel,
        (shape((rows, width), F32), shape((middle, width), BF16), shape((1, width), F32)),
        [VMEM] * (2 + len(got)),
        (self_term, keep, *got),
    )
    grads = lax.all_gather(quarter, "rep", axis=0, tiled=True).astype(F32)
    return (out, d_features, grads[:width], grads[width:], grad_bias[0])


def solution(mesh):
    return jax.shard_map(
        on_device,
        mesh=mesh,
        in_specs=(
            P(("row", "rep"), None),
            P(),
            P(),
            P(),
            P(("row", "rep"), None),
            P(("row", "rep")),
            P(("row", "rep")),
            P(("row", "rep")),
            P(("row", "rep"), None),
            P(("row", "rep"), None),
        ),
        out_specs=(P(("row", "rep"), None), P(("row", "rep"), None), P(), P(), P()),
        check_vma=False,
    )
```

```python
import math

import jax
import jax.numpy as jnp
from jax import lax
from jax.experimental import pallas as pl
from jax.experimental.pallas import tpu as pltpu
from jax.sharding import PartitionSpec as P

BLK = 128
PAD = 16
BF16 = jnp.bfloat16
F32 = jnp.float32
UNROLL = 64
VMEM = pl.BlockSpec(memory_space=pltpu.VMEM)
HBM = pl.BlockSpec(memory_space=pltpu.HBM)


def size_of(value):
    return math.prod(value.shape) * jnp.dtype(value.dtype).itemsize


def row_place(block):
    away = block ^ lax.axis_index("rep")
    return ((away & 1) << 1) | (away >> 1)


def col_place(block, row_count):
    away = block ^ lax.axis_index("row")
    return (away & 3) * (row_count // 4) + (away >> 2)


def tree(values):
    while len(values) > 1:
        values = [values[i] + values[i + 1] for i in range(0, len(values), 2)]
    return values[0]


def split(value):
    high = value.astype(BF16).astype(F32)
    line = lax.broadcasted_iota(jnp.int32, (PAD, value.shape[1]), 0)
    return jnp.where(line == 0, high, jnp.where(line == 1, value - high, 0.0)).astype(BF16)


def joined(rows):
    rows = rows.astype(F32)
    return rows[0:1] + rows[1:2]


def add_tiles(first, scalars, src_ref, dst_ref, acc_ref, ready):
    row_ref, col_ref, count_ref = scalars
    tiles, slots = src_ref.shape
    col_blocks = acc_ref.shape[1]
    line = lax.broadcasted_iota(jnp.int32, (BLK, slots), 0).astype(BF16)
    slot = lax.broadcasted_iota(jnp.int32, (1, slots), 1)
    one, zero = jnp.ones((), BF16), jnp.zeros((), BF16)

    def step(i, carry):
        base = pl.multiple_of(i * UNROLL, UNROLL)
        ready(i, pl.ds(base, UNROLL))
        dst, src = dst_ref[pl.ds(base, UNROLL), :], src_ref[pl.ds(base, UNROLL), :]
        for u in range(UNROLL):
            tile = first + base + u
            live = jnp.where(slot < count_ref[tile], dst[u : u + 1], -1)
            dst_hot = jnp.where(line == live.astype(BF16), one, zero)
            src_hot = jnp.where(line == src[u : u + 1].astype(BF16), one, zero)
            part = lax.dot_general(
                dst_hot, src_hot, (((1,), (1,)), ((), ())), preferred_element_type=F32
            )
            acc_ref[row_place(row_ref[tile]), col_place(col_ref[tile], col_blocks)] += part
        return carry

    lax.fori_loop(0, tiles // UNROLL, step, 0)


def first_build_kernel(
    row_ref, col_ref, count_ref, src_ref, dst_ref, features_ref, d_out_ref,
    acc_ref, own_ref, line_ref, late_src_ref, late_dst_ref,
    row_buf, col_buf, count_buf, src_buf, dst_buf, sems, src_sems, dst_sems,
):
    half, rows = src_buf.shape[0], features_ref.shape[0]
    scalars = [row_buf, col_buf, count_buf]
    copies = [
        pltpu.make_async_copy(ref, buf, sems.at[i])
        for i, (ref, buf) in enumerate(zip([row_ref, col_ref, count_ref], scalars))
    ]

    def edges(i, at):
        return (
            pltpu.make_async_copy(src_ref.at[at], src_buf.at[at], src_sems.at[i]),
            pltpu.make_async_copy(dst_ref.at[at], dst_buf.at[at], dst_sems.at[i]),
        )

    late = [
        pltpu.make_async_copy(src_ref.at[pl.ds(half, half)], late_src_ref, sems.at[3]),
        pltpu.make_async_copy(dst_ref.at[pl.ds(half, half)], late_dst_ref, sems.at[4]),
        pltpu.make_async_copy(features_ref, own_ref.at[pl.ds(0, rows)], sems.at[5]),
        pltpu.make_async_copy(d_out_ref, own_ref.at[pl.ds(rows, rows)], sems.at[6]),
        pltpu.make_async_copy(features_ref, line_ref.at[pl.ds(0, rows)], sems.at[7]),
    ]
    for copy in copies:
        copy.start()
    for i in range(half // UNROLL):
        for copy in edges(i, pl.ds(i * UNROLL, UNROLL)):
            copy.start()
    for copy in late:
        copy.start()
    acc_ref[...] = jnp.zeros_like(acc_ref)
    for copy in copies:
        copy.wait()

    def ready(i, at):
        for copy in edges(i, at):
            copy.wait()

    add_tiles(0, scalars, src_buf, dst_buf, acc_ref, ready)
    for copy in late:
        copy.wait()


def last_build_kernel(
    row_ref, col_ref, count_ref, src_ref, dst_ref, half_ref, adj_ref,
    acc_ref, row_buf, col_buf, count_buf, sems,
):
    scalars = [row_buf, col_buf, count_buf]
    copies = [
        pltpu.make_async_copy(ref, buf, sems.at[i])
        for i, (ref, buf) in enumerate(zip([row_ref, col_ref, count_ref], scalars))
    ]
    for copy in copies:
        copy.start()
    acc_ref[...] = half_ref[...]
    for copy in copies:
        copy.wait()
    add_tiles(src_ref.shape[0], scalars, src_ref, dst_ref, acc_ref, lambda i, at: None)
    row_blocks, col_blocks = acc_ref.shape[:2]
    for g in range(row_blocks):
        for c in range(col_blocks):
            adj_ref[g * BLK : (g + 1) * BLK, c * BLK : (c + 1) * BLK] = acc_ref[g, c].astype(BF16)


def gather_kernel(adj_ref, *refs):
    *feature_refs, keep_ref, send_ref = refs
    half = keep_ref.shape[0] - PAD
    total, at = None, 0
    for ref in feature_refs:
        size = ref.shape[0]
        part = jnp.dot(adj_ref[:, at : at + size], ref[...], preferred_element_type=F32)
        total = part if total is None else total + part
        at += size
    ones = jnp.ones((PAD, adj_ref.shape[1]), BF16)
    degree = lax.dot_general(
        ones, adj_ref[...], (((1,), (1,)), ((), ())), preferred_element_type=F32
    )
    keep_ref[:half] = total[:half]
    keep_ref[half:] = degree[:, :half]
    send_ref[:half] = total[half:].astype(BF16)
    send_ref[half:] = split(degree[:1, half:])


def pair_kernel(keep_ref, got_ref, pair_ref):
    half = keep_ref.shape[0] - PAD
    pair_ref[:half] = (keep_ref[:half] + got_ref[:half].astype(F32)).astype(BF16)
    pair_ref[half:] = split(keep_ref[half : half + 1] + joined(got_ref[half:]))


def node_kernel(
    pair_ref, got_ref, own_ref, near_ref, w_self_ref, w_neigh_ref, bias_ref,
    out_ref, self_ref, keep_ref, send_ref,
):
    rows, width = out_ref.shape
    half = 2 * rows
    swapped = jnp.concatenate([got_ref[rows:half], got_ref[:rows]], axis=0).astype(F32)
    sums = pair_ref[:half].astype(F32) + swapped
    far = joined(got_ref[half:])
    degree = joined(pair_ref[half:]) + jnp.concatenate([far[:, rows:], far[:, :rows]], axis=1)
    inverse_row = 1.0 / jnp.maximum(degree, 1.0)
    diagonal = lax.broadcasted_iota(jnp.int32, (half, half), 0) == lax.broadcasted_iota(
        jnp.int32, (half, half), 1
    )
    inverse = jnp.sum(jnp.where(diagonal, inverse_row, 0.0), axis=1, keepdims=True)
    agg = (sums * inverse).astype(BF16)
    features = jnp.concatenate([own_ref[:rows], near_ref[:rows]], axis=0)
    d_out = jnp.concatenate([own_ref[rows:], near_ref[rows:]], axis=0).astype(F32)
    pre = (
        jnp.dot(features, w_self_ref[...], preferred_element_type=F32)
        + jnp.dot(agg, w_neigh_ref[...], preferred_element_type=F32)
        + bias_ref[...]
    )
    square = pre * pre
    bend = jnp.tanh(0.7978845608 * pre * (1.0 + 0.044715 * square))
    out_ref[...] = (0.5 * pre[:rows] * (1.0 + bend[:rows])).astype(BF16)
    slope = 0.5 * (1.0 + bend) + 0.5 * pre * (1.0 - bend * bend) * (
        0.7978845608 * (1.0 + 3.0 * 0.044715 * square)
    )
    d_pre = (d_out * slope).astype(BF16)
    transposed = (((1,), (1,)), ((), ()))
    self_ref[...] = lax.dot_general(
        d_pre[:rows], w_self_ref[...], transposed, preferred_element_type=F32
    )
    back = lax.dot_general(d_pre, w_neigh_ref[...], transposed, preferred_element_type=F32)
    send_ref[:half] = (back * inverse).astype(BF16)
    me = lax.axis_index("rep")
    terms = jnp.where(me >> 1 == 0, features, agg)
    grads = lax.dot_general(terms, d_pre, (((0,), (0,)), ((), ())), preferred_element_type=F32)
    middle = width // 2
    low = me & 1 == 0
    bias_term = jnp.sum(d_pre[:rows].astype(F32), axis=0, keepdims=True) + jnp.sum(
        d_pre[rows:].astype(F32), axis=0, keepdims=True
    )
    keep_ref[:middle] = jnp.where(low, grads[:middle], grads[middle:])
    keep_ref[middle:] = split(bias_term).astype(F32)
    send_ref[half : half + middle] = jnp.where(low, grads[middle:], grads[:middle]).astype(BF16)
    send_ref[half + middle :] = split(bias_term)


def spread_kernel(adj_ref, sent_ref, got_ref, terms_ref, keep_ref, *msg_refs):
    half = adj_ref.shape[0] // 2
    middle = terms_ref.shape[0] - PAD
    size = adj_ref.shape[1] // 4
    g = jnp.concatenate([sent_ref[:half], got_ref[:half]], axis=0)
    grads = (terms_ref[:middle] + got_ref[half : half + middle].astype(F32)).astype(BF16)
    bias_rows = split(joined(terms_ref[middle:]) + joined(got_ref[half + middle :]))
    for m, ref in enumerate([keep_ref, *msg_refs]):
        blocks = lax.dot_general(
            adj_ref[:, m * size : (m + 1) * size],
            g,
            (((0,), (0,)), ((), ())),
            preferred_element_type=F32,
        )
        ref[:size] = blocks.astype(ref.dtype)
        ref[size : size + middle] = grads.astype(ref.dtype)
        ref[size + middle :] = bias_rows.astype(ref.dtype)


def near_sum_kernel(keep_ref, *refs):
    *got_refs, own_ref = refs[:4]
    msg_refs = refs[4:]
    size = (1 + len(msg_refs)) * BLK
    middle = keep_ref.shape[0] - size - PAD
    terms = [keep_ref, *got_refs]
    blocks = tree([ref[:size].astype(F32) for ref in terms])
    grads = tree([ref[size : size + middle].astype(F32) for ref in terms]).astype(BF16)
    bias_rows = split(tree([joined(ref[size + middle :]) for ref in terms]))
    for h, ref in enumerate([own_ref, *msg_refs]):
        ref[:BLK] = blocks[h * BLK : (h + 1) * BLK].astype(ref.dtype)
        ref[BLK : BLK + middle] = grads.astype(ref.dtype)
        ref[BLK + middle :] = bias_rows.astype(ref.dtype)


def finish_kernel(self_ref, own_ref, *refs):
    *got_refs, d_features_ref, quarter_ref, bias_ref = refs
    middle = own_ref.shape[0] - BLK - PAD
    terms = [own_ref, *got_refs]
    d_features_ref[...] = self_ref[...] + tree([ref[:BLK].astype(F32) for ref in terms])
    quarter_ref[...] = tree([ref[BLK : BLK + middle].astype(F32) for ref in terms]).astype(BF16)
    bias_ref[...] = tree([joined(ref[BLK + middle :]) for ref in terms])


def call(kernel, out_shape, specs, args, scratch=()):
    outs = out_shape if isinstance(out_shape, (list, tuple)) else [out_shape]
    held = sum(size_of(v) for v in [*args, *outs])
    held += sum(math.prod(v.shape) * 4 for v in scratch)
    return pl.pallas_call(
        kernel,
        out_shape=out_shape,
        in_specs=specs,
        out_specs=[VMEM] * len(outs) if outs is out_shape else VMEM,
        scratch_shapes=list(scratch),
        compiler_params=pltpu.CompilerParams(vmem_limit_bytes=2 * held + 4 * 1024 * 1024),
    )(*args)


def on_device(
    features, w_self, w_neigh, bias, d_out, tile_row, tile_col, tile_count, edge_src, edge_dst
):
    rows, width = features.shape
    row_count, rep_count = lax.axis_size("row"), lax.axis_size("rep")
    group, columns = rep_count * rows, row_count * rows
    half, middle = group // 2, width // 2
    far = row_count // 4
    shape = jax.ShapeDtypeStruct

    def swap(value, axis, bits):
        return lax.ppermute(value, axis, [(i, i ^ bits) for i in range(lax.axis_size(axis))])

    far_pieces = [swap(features, "row", 4 * h) for h in range(1, far)]
    tiles, slots = edge_src.shape
    early = tiles // 2
    tile_row, tile_col, tile_count, edge_src, edge_dst, held_features, d_out = (
        pltpu.with_memory_space_constraint(v, pltpu.HBM)
        for v in (tile_row, tile_col, tile_count, edge_src, edge_dst, features, d_out)
    )
    scalars = (tile_row, tile_col, tile_count)
    buffers = [pltpu.SMEM((tiles,), jnp.int32)] * 3
    acc_shape = (rep_count, row_count, BLK, BLK)
    chunk_sems = [pltpu.SemaphoreType.DMA((early // UNROLL,))] * 2
    acc, own, line, late_src, late_dst = call(
        first_build_kernel,
        (
            shape(acc_shape, F32),
            shape((2 * rows, width), BF16),
            shape((far * rows, width), BF16),
            shape((early, slots), jnp.int32),
            shape((early, slots), jnp.int32),
        ),
        [HBM] * 7,
        (*scalars, edge_src, edge_dst, held_features, d_out),
        buffers
        + [pltpu.VMEM((early, slots), jnp.int32)] * 2
        + [pltpu.SemaphoreType.DMA((8,))]
        + chunk_sems,
    )
    acc, line, far_pieces = lax.optimization_barrier((acc, line, far_pieces))
    for h, piece in enumerate(far_pieces):
        line = lax.dynamic_update_slice(line, piece, ((h + 1) * rows, 0))
    near = swap(own, "rep", 2)
    pieces = [line] + [swap(line, "row", m) for m in range(1, 4)]
    adjacency = call(
        last_build_kernel,
        shape((group, columns), BF16),
        [HBM] * 3 + [VMEM] * 3,
        (*scalars, late_src, late_dst, acc),
        [pltpu.VMEM(acc_shape, F32)] + buffers + [pltpu.SemaphoreType.DMA((3,))],
    )
    adjacency, near, pieces = lax.optimization_barrier((adjacency, near, pieces))
    keep, send = call(
        gather_kernel,
        (shape((half + PAD, width), F32), shape((half + PAD, width), BF16)),
        [VMEM] * (1 + len(pieces)),
        (adjacency, *pieces),
    )
    pair_sum = call(
        pair_kernel,
        shape((half + PAD, width), BF16),
        [VMEM] * 2,
        (keep, swap(send, "rep", 1)),
    )
    out, self_term, keep, send = call(
        node_kernel,
        (
            shape((rows, width), BF16),
            shape((rows, width), F32),
            shape((middle + PAD, width), F32),
            shape((half + middle + PAD, width), BF16),
        ),
        [VMEM] * 7,
        (pair_sum, swap(pair_sum, "rep", 2), own, near, w_self, w_neigh, bias[None, :]),
    )
    terms = middle + PAD
    keep, *near_msgs = call(
        spread_kernel,
        (shape((far * BLK + terms, width), F32),) + (shape((far * BLK + terms, width), BF16),) * 3,
        [VMEM] * 4,
        (adjacency, send, swap(send, "rep", 1), keep),
    )
    got = [swap(msg, "row", m + 1) for m, msg in enumerate(near_msgs)]
    keep, *far_msgs = call(
        near_sum_kernel,
        (shape((BLK + terms, width), F32),) + (shape((BLK + terms, width), BF16),) * (far - 1),
        [VMEM] * 4,
        (keep, *got),
    )
    got = [swap(msg, "row", 4 * (h + 1)) for h, msg in enumerate(far_msgs)]
    d_features, quarter, grad_bias = call(
        finish_kernel,
        (shape((rows, width), F32), shape((middle, width), BF16), shape((1, width), F32)),
        [VMEM] * (2 + len(got)),
        (self_term, keep, *got),
    )
    grads = lax.all_gather(quarter, "rep", axis=0, tiled=True).astype(F32)
    return (out, d_features, grads[:width], grads[width:], grad_bias[0])


def solution(mesh):
    return jax.shard_map(
        on_device,
        mesh=mesh,
        in_specs=(
            P(("row", "rep"), None),
            P(),
            P(),
            P(),
            P(("row", "rep"), None),
            P(("row", "rep")),
            P(("row", "rep")),
            P(("row", "rep")),
            P(("row", "rep"), None),
            P(("row", "rep"), None),
        ),
        out_specs=(P(("row", "rep"), None), P(("row", "rep"), None), P(), P(), P()),
        check_vma=False,
    )
```

```python
import math

import jax
import jax.numpy as jnp
from jax import lax
from jax.experimental import pallas as pl
from jax.experimental.pallas import tpu as pltpu
from jax.sharding import PartitionSpec as P

BLK = 128
PAD = 16
BF16 = jnp.bfloat16
F32 = jnp.float32
UNROLL = 64
VMEM = pl.BlockSpec(memory_space=pltpu.VMEM)
HBM = pl.BlockSpec(memory_space=pltpu.HBM)


def size_of(value):
    return math.prod(value.shape) * jnp.dtype(value.dtype).itemsize


def row_place(block):
    away = block ^ lax.axis_index("rep")
    return ((away & 1) << 1) | (away >> 1)


def col_place(block, row_count):
    away = block ^ lax.axis_index("row")
    return (away & 3) * (row_count // 4) + (away >> 2)


def tree(values):
    while len(values) > 1:
        values = [values[i] + values[i + 1] for i in range(0, len(values), 2)]
    return values[0]


def split(value):
    high = value.astype(BF16).astype(F32)
    line = lax.broadcasted_iota(jnp.int32, (PAD, value.shape[1]), 0)
    return jnp.where(line == 0, high, jnp.where(line == 1, value - high, 0.0)).astype(BF16)


def joined(rows):
    rows = rows.astype(F32)
    return rows[0:1] + rows[1:2]


def add_tiles(first, scalars, src_ref, dst_ref, acc_ref, ready):
    row_ref, col_ref, count_ref = scalars
    tiles, slots = src_ref.shape
    col_blocks = acc_ref.shape[1]
    line = lax.broadcasted_iota(jnp.int32, (BLK, slots), 0).astype(BF16)
    slot = lax.broadcasted_iota(jnp.int32, (1, slots), 1)
    one, zero = jnp.ones((), BF16), jnp.zeros((), BF16)

    def step(i, carry):
        base = pl.multiple_of(i * UNROLL, UNROLL)
        ready(i, pl.ds(base, UNROLL))
        dst, src = dst_ref[pl.ds(base, UNROLL), :], src_ref[pl.ds(base, UNROLL), :]
        for u in range(UNROLL):
            tile = first + base + u
            live = jnp.where(slot < count_ref[tile], dst[u : u + 1], -1)
            dst_hot = jnp.where(line == live.astype(BF16), one, zero)
            src_hot = jnp.where(line == src[u : u + 1].astype(BF16), one, zero)
            part = lax.dot_general(
                dst_hot, src_hot, (((1,), (1,)), ((), ())), preferred_element_type=F32
            )
            acc_ref[row_place(row_ref[tile]), col_place(col_ref[tile], col_blocks)] += part
        return carry

    lax.fori_loop(0, tiles // UNROLL, step, 0)


def first_build_kernel(
    row_ref, col_ref, count_ref, src_ref, dst_ref, features_ref, d_out_ref,
    acc_ref, own_ref, line_ref, late_src_ref, late_dst_ref,
    row_buf, col_buf, count_buf, src_buf, dst_buf, sems, src_sems, dst_sems,
):
    half, rows = src_buf.shape[0], features_ref.shape[0]
    scalars = [row_buf, col_buf, count_buf]
    copies = [
        pltpu.make_async_copy(ref, buf, sems.at[i])
        for i, (ref, buf) in enumerate(zip([row_ref, col_ref, count_ref], scalars))
    ]

    def edges(i, at):
        return (
            pltpu.make_async_copy(src_ref.at[at], src_buf.at[at], src_sems.at[i]),
            pltpu.make_async_copy(dst_ref.at[at], dst_buf.at[at], dst_sems.at[i]),
        )

    late = [
        pltpu.make_async_copy(src_ref.at[pl.ds(half, half)], late_src_ref, sems.at[3]),
        pltpu.make_async_copy(dst_ref.at[pl.ds(half, half)], late_dst_ref, sems.at[4]),
        pltpu.make_async_copy(features_ref, own_ref.at[pl.ds(0, rows)], sems.at[5]),
        pltpu.make_async_copy(d_out_ref, own_ref.at[pl.ds(rows, rows)], sems.at[6]),
        pltpu.make_async_copy(features_ref, line_ref.at[pl.ds(0, rows)], sems.at[7]),
    ]
    for copy in copies:
        copy.start()
    for i in range(half // UNROLL):
        for copy in edges(i, pl.ds(i * UNROLL, UNROLL)):
            copy.start()
    for copy in late:
        copy.start()
    acc_ref[...] = jnp.zeros_like(acc_ref)
    for copy in copies:
        copy.wait()

    def ready(i, at):
        for copy in edges(i, at):
            copy.wait()

    add_tiles(0, scalars, src_buf, dst_buf, acc_ref, ready)
    for copy in late:
        copy.wait()


def last_build_kernel(
    row_ref, col_ref, count_ref, src_ref, dst_ref, half_ref, adj_ref,
    acc_ref, row_buf, col_buf, count_buf, sems,
):
    scalars = [row_buf, col_buf, count_buf]
    copies = [
        pltpu.make_async_copy(ref, buf, sems.at[i])
        for i, (ref, buf) in enumerate(zip([row_ref, col_ref, count_ref], scalars))
    ]
    for copy in copies:
        copy.start()
    acc_ref[...] = half_ref[...]
    for copy in copies:
        copy.wait()
    add_tiles(src_ref.shape[0], scalars, src_ref, dst_ref, acc_ref, lambda i, at: None)
    row_blocks, col_blocks = acc_ref.shape[:2]
    for g in range(row_blocks):
        for c in range(col_blocks):
            adj_ref[g * BLK : (g + 1) * BLK, c * BLK : (c + 1) * BLK] = acc_ref[g, c].astype(BF16)


def gather_kernel(adj_ref, *refs):
    *feature_refs, keep_ref, send_ref = refs
    half = keep_ref.shape[0] - PAD
    total, at = None, 0
    for ref in feature_refs:
        size = ref.shape[0]
        part = jnp.dot(adj_ref[:, at : at + size], ref[...], preferred_element_type=F32)
        total = part if total is None else total + part
        at += size
    ones = jnp.ones((PAD, adj_ref.shape[1]), BF16)
    degree = lax.dot_general(
        ones, adj_ref[...], (((1,), (1,)), ((), ())), preferred_element_type=F32
    )
    keep_ref[:half] = total[:half]
    keep_ref[half:] = degree[:, :half]
    send_ref[:half] = total[half:].astype(BF16)
    send_ref[half:] = split(degree[:1, half:])


def pair_kernel(keep_ref, got_ref, pair_ref):
    half = keep_ref.shape[0] - PAD
    pair_ref[:half] = (keep_ref[:half] + got_ref[:half].astype(F32)).astype(BF16)
    pair_ref[half:] = split(keep_ref[half : half + 1] + joined(got_ref[half:]))


def node_kernel(
    pair_ref, got_ref, own_ref, near_ref, w_self_ref, w_neigh_ref, bias_ref,
    out_ref, self_ref, keep_ref, send_ref,
):
    rows, width = out_ref.shape
    half = 2 * rows
    swapped = jnp.concatenate([got_ref[rows:half], got_ref[:rows]], axis=0).astype(F32)
    sums = pair_ref[:half].astype(F32) + swapped
    far = joined(got_ref[half:])
    degree = joined(pair_ref[half:]) + jnp.concatenate([far[:, rows:], far[:, :rows]], axis=1)
    inverse_row = 1.0 / jnp.maximum(degree, 1.0)
    diagonal = lax.broadcasted_iota(jnp.int32, (half, half), 0) == lax.broadcasted_iota(
        jnp.int32, (half, half), 1
    )
    inverse = jnp.sum(jnp.where(diagonal, inverse_row, 0.0), axis=1, keepdims=True)
    agg = (sums * inverse).astype(BF16)
    features = jnp.concatenate([own_ref[:rows], near_ref[:rows]], axis=0)
    d_out = jnp.concatenate([own_ref[rows:], near_ref[rows:]], axis=0).astype(F32)
    pre = (
        jnp.dot(features, w_self_ref[...], preferred_element_type=F32)
        + jnp.dot(agg, w_neigh_ref[...], preferred_element_type=F32)
        + bias_ref[...]
    )
    square = pre * pre
    bend = jnp.tanh(0.7978845608 * pre * (1.0 + 0.044715 * square))
    out_ref[...] = (0.5 * pre[:rows] * (1.0 + bend[:rows])).astype(BF16)
    slope = 0.5 * (1.0 + bend) + 0.5 * pre * (1.0 - bend * bend) * (
        0.7978845608 * (1.0 + 3.0 * 0.044715 * square)
    )
    d_pre = (d_out * slope).astype(BF16)
    transposed = (((1,), (1,)), ((), ()))
    self_ref[...] = lax.dot_general(
        d_pre[:rows], w_self_ref[...], transposed, preferred_element_type=F32
    )
    back = lax.dot_general(d_pre, w_neigh_ref[...], transposed, preferred_element_type=F32)
    send_ref[:half] = (back * inverse).astype(BF16)
    me = lax.axis_index("rep")
    terms = jnp.where(me >> 1 == 0, features, agg)
    grads = lax.dot_general(terms, d_pre, (((0,), (0,)), ((), ())), preferred_element_type=F32)
    middle = width // 2
    low = me & 1 == 0
    bias_term = jnp.sum(d_pre[:rows].astype(F32), axis=0, keepdims=True) + jnp.sum(
        d_pre[rows:].astype(F32), axis=0, keepdims=True
    )
    keep_ref[:middle] = jnp.where(low, grads[:middle], grads[middle:])
    keep_ref[middle:] = split(bias_term).astype(F32)
    send_ref[half : half + middle] = jnp.where(low, grads[middle:], grads[:middle]).astype(BF16)
    send_ref[half + middle :] = split(bias_term)


def spread_kernel(adj_ref, sent_ref, got_ref, keep_ref, *msg_refs):
    half = adj_ref.shape[0] // 2
    size = adj_ref.shape[1] // 4
    g = jnp.concatenate([sent_ref[:half], got_ref[:half]], axis=0)
    for m, ref in enumerate([keep_ref, *msg_refs]):
        blocks = lax.dot_general(
            adj_ref[:, m * size : (m + 1) * size],
            g,
            (((0,), (0,)), ((), ())),
            preferred_element_type=F32,
        )
        ref[...] = blocks.astype(ref.dtype)


def near_sum_kernel(keep_ref, *refs):
    blocks = tree([ref[...].astype(F32) for ref in (keep_ref, *refs[:3])])
    for h, ref in enumerate(refs[3:]):
        ref[...] = blocks[h * BLK : (h + 1) * BLK].astype(ref.dtype)


def finish_kernel(self_ref, *refs):
    *terms, d_features_ref = refs
    d_features_ref[...] = self_ref[...] + tree([ref[...].astype(F32) for ref in terms])


def core_terms_kernel(keep_ref, got_ref, terms_ref):
    middle = keep_ref.shape[0] - PAD
    at = got_ref.shape[0] - PAD
    grads = keep_ref[:middle] + got_ref[at - middle : at].astype(F32)
    terms_ref[:middle] = grads.astype(BF16)
    terms_ref[middle:] = split(joined(keep_ref[middle:]) + joined(got_ref[at:]))


def add_terms(refs):
    middle = refs[0].shape[0] - PAD
    grads = tree([ref[:middle].astype(F32) for ref in refs]).astype(BF16)
    return grads, tree([joined(ref[middle:]) for ref in refs])


def far_terms_kernel(*refs):
    *terms, sum_ref = refs
    middle = sum_ref.shape[0] - PAD
    grads, bias_term = add_terms(terms)
    sum_ref[:middle] = grads
    sum_ref[middle:] = split(bias_term)


def near_terms_kernel(*refs):
    *terms, quarter_ref, bias_ref = refs
    quarter_ref[...], bias_ref[...] = add_terms(terms)


def call(kernel, out_shape, specs, args, scratch=()):
    outs = out_shape if isinstance(out_shape, (list, tuple)) else [out_shape]
    held = sum(size_of(v) for v in [*args, *outs])
    held += sum(math.prod(v.shape) * 4 for v in scratch)
    return pl.pallas_call(
        kernel,
        out_shape=out_shape,
        in_specs=specs,
        out_specs=[VMEM] * len(outs) if outs is out_shape else VMEM,
        scratch_shapes=list(scratch),
        compiler_params=pltpu.CompilerParams(vmem_limit_bytes=2 * held + 4 * 1024 * 1024),
    )(*args)


def on_device(
    features, w_self, w_neigh, bias, d_out, tile_row, tile_col, tile_count, edge_src, edge_dst
):
    rows, width = features.shape
    row_count, rep_count = lax.axis_size("row"), lax.axis_size("rep")
    group, columns = rep_count * rows, row_count * rows
    half, middle = group // 2, width // 2
    far = row_count // 4
    shape = jax.ShapeDtypeStruct

    def swap(value, axis, bits):
        return lax.ppermute(value, axis, [(i, i ^ bits) for i in range(lax.axis_size(axis))])

    far_pieces = [swap(features, "row", 4 * h) for h in range(1, far)]
    tiles, slots = edge_src.shape
    early = tiles // 2
    tile_row, tile_col, tile_count, edge_src, edge_dst, held_features, d_out = (
        pltpu.with_memory_space_constraint(v, pltpu.HBM)
        for v in (tile_row, tile_col, tile_count, edge_src, edge_dst, features, d_out)
    )
    scalars = (tile_row, tile_col, tile_count)
    buffers = [pltpu.SMEM((tiles,), jnp.int32)] * 3
    acc_shape = (rep_count, row_count, BLK, BLK)
    chunk_sems = [pltpu.SemaphoreType.DMA((early // UNROLL,))] * 2
    acc, own, line, late_src, late_dst = call(
        first_build_kernel,
        (
            shape(acc_shape, F32),
            shape((2 * rows, width), BF16),
            shape((far * rows, width), BF16),
            shape((early, slots), jnp.int32),
            shape((early, slots), jnp.int32),
        ),
        [HBM] * 7,
        (*scalars, edge_src, edge_dst, held_features, d_out),
        buffers
        + [pltpu.VMEM((early, slots), jnp.int32)] * 2
        + [pltpu.SemaphoreType.DMA((8,))]
        + chunk_sems,
    )
    acc, line, far_pieces = lax.optimization_barrier((acc, line, far_pieces))
    for h, piece in enumerate(far_pieces):
        line = lax.dynamic_update_slice(line, piece, ((h + 1) * rows, 0))
    near = swap(own, "rep", 2)
    pieces = [line] + [swap(line, "row", m) for m in range(1, 4)]
    adjacency = call(
        last_build_kernel,
        shape((group, columns), BF16),
        [HBM] * 3 + [VMEM] * 3,
        (*scalars, late_src, late_dst, acc),
        [pltpu.VMEM(acc_shape, F32)] + buffers + [pltpu.SemaphoreType.DMA((3,))],
    )
    adjacency, near, pieces = lax.optimization_barrier((adjacency, near, pieces))
    keep, send = call(
        gather_kernel,
        (shape((half + PAD, width), F32), shape((half + PAD, width), BF16)),
        [VMEM] * (1 + len(pieces)),
        (adjacency, *pieces),
    )
    pair_sum = call(
        pair_kernel,
        shape((half + PAD, width), BF16),
        [VMEM] * 2,
        (keep, swap(send, "rep", 1)),
    )
    out, self_term, keep, send = call(
        node_kernel,
        (
            shape((rows, width), BF16),
            shape((rows, width), F32),
            shape((middle + PAD, width), F32),
            shape((half + middle + PAD, width), BF16),
        ),
        [VMEM] * 7,
        (pair_sum, swap(pair_sum, "rep", 2), own, near, w_self, w_neigh, bias[None, :]),
    )
    back = swap(send, "rep", 1)
    keep_blocks, *near_msgs = call(
        spread_kernel,
        (shape((far * BLK, width), F32),) + (shape((far * BLK, width), BF16),) * 3,
        [VMEM] * 3,
        (adjacency, send, back),
    )
    got = [swap(msg, "row", m + 1) for m, msg in enumerate(near_msgs)]
    terms_shape = shape((middle + PAD, width), BF16)
    terms = call(core_terms_kernel, terms_shape, [VMEM] * 2, (keep, back))
    far_terms = [terms] + [swap(terms, "row", 4 * h) for h in range(1, far)]
    terms = call(far_terms_kernel, terms_shape, [VMEM] * far, far_terms)
    near_terms = [terms] + [swap(terms, "row", m) for m in range(1, 4)]
    quarter, grad_bias = call(
        near_terms_kernel,
        (shape((middle, width), BF16), shape((1, width), F32)),
        [VMEM] * 4,
        near_terms,
    )
    keep_block, *far_msgs = call(
        near_sum_kernel,
        (shape((BLK, width), F32),) + (shape((BLK, width), BF16),) * (far - 1),
        [VMEM] * 4,
        (keep_blocks, *got),
    )
    got = [swap(msg, "row", 4 * (h + 1)) for h, msg in enumerate(far_msgs)]
    d_features = call(
        finish_kernel,
        shape((rows, width), F32),
        [VMEM] * (2 + len(got)),
        (self_term, keep_block, *got),
    )
    grads = lax.all_gather(quarter, "rep", axis=0, tiled=True).astype(F32)
    return (out, d_features, grads[:width], grads[width:], grad_bias[0])


def solution(mesh):
    return jax.shard_map(
        on_device,
        mesh=mesh,
        in_specs=(
            P(("row", "rep"), None),
            P(),
            P(),
            P(),
            P(("row", "rep"), None),
            P(("row", "rep")),
            P(("row", "rep")),
            P(("row", "rep")),
            P(("row", "rep"), None),
            P(("row", "rep"), None),
        ),
        out_specs=(P(("row", "rep"), None), P(("row", "rep"), None), P(), P(), P()),
        check_vma=False,
    )
```

```python
import math

import jax
import jax.numpy as jnp
from jax import lax
from jax.experimental import pallas as pl
from jax.experimental.pallas import tpu as pltpu
from jax.sharding import PartitionSpec as P

BLK = 128
PAD = 16
BF16 = jnp.bfloat16
F32 = jnp.float32
UNROLL = 64
VMEM = pl.BlockSpec(memory_space=pltpu.VMEM)
HBM = pl.BlockSpec(memory_space=pltpu.HBM)


def size_of(value):
    return math.prod(value.shape) * jnp.dtype(value.dtype).itemsize


def row_place(block):
    away = block ^ lax.axis_index("rep")
    return ((away & 1) << 1) | (away >> 1)


def col_place(block, row_count):
    away = block ^ lax.axis_index("row")
    return (away & 3) * (row_count // 4) + (away >> 2)


def tree(values):
    while len(values) > 1:
        values = [values[i] + values[i + 1] for i in range(0, len(values), 2)]
    return values[0]


def split(value):
    high = value.astype(BF16).astype(F32)
    line = lax.broadcasted_iota(jnp.int32, (PAD, value.shape[1]), 0)
    return jnp.where(line == 0, high, jnp.where(line == 1, value - high, 0.0)).astype(BF16)


def joined(rows):
    rows = rows.astype(F32)
    return rows[0:1] + rows[1:2]


def add_tiles(first, scalars, src_ref, dst_ref, acc_ref, ready):
    row_ref, col_ref, count_ref = scalars
    tiles, slots = src_ref.shape
    col_blocks = acc_ref.shape[1]
    line = lax.broadcasted_iota(jnp.int32, (BLK, slots), 0).astype(BF16)
    slot = lax.broadcasted_iota(jnp.int32, (1, slots), 1)
    one, zero = jnp.ones((), BF16), jnp.zeros((), BF16)

    def step(i, carry):
        base = pl.multiple_of(i * UNROLL, UNROLL)
        ready(i, pl.ds(base, UNROLL))
        dst, src = dst_ref[pl.ds(base, UNROLL), :], src_ref[pl.ds(base, UNROLL), :]
        for u in range(UNROLL):
            tile = first + base + u
            live = jnp.where(slot < count_ref[tile], dst[u : u + 1], -1)
            dst_hot = jnp.where(line == live.astype(BF16), one, zero)
            src_hot = jnp.where(line == src[u : u + 1].astype(BF16), one, zero)
            part = lax.dot_general(
                dst_hot, src_hot, (((1,), (1,)), ((), ())), preferred_element_type=F32
            )
            acc_ref[row_place(row_ref[tile]), col_place(col_ref[tile], col_blocks)] += part
        return carry

    lax.fori_loop(0, tiles // UNROLL, step, 0)


def first_build_kernel(
    row_ref, col_ref, count_ref, src_ref, dst_ref, features_ref,
    acc_ref, line_ref, late_src_ref, late_dst_ref,
    row_buf, col_buf, count_buf, src_buf, dst_buf, sems, src_sems, dst_sems,
):
    half, rows = src_buf.shape[0], features_ref.shape[0]
    scalars = [row_buf, col_buf, count_buf]
    copies = [
        pltpu.make_async_copy(ref, buf, sems.at[i])
        for i, (ref, buf) in enumerate(zip([row_ref, col_ref, count_ref], scalars))
    ]

    def edges(i, at):
        return (
            pltpu.make_async_copy(src_ref.at[at], src_buf.at[at], src_sems.at[i]),
            pltpu.make_async_copy(dst_ref.at[at], dst_buf.at[at], dst_sems.at[i]),
        )

    late = [
        pltpu.make_async_copy(src_ref.at[pl.ds(half, half)], late_src_ref, sems.at[3]),
        pltpu.make_async_copy(dst_ref.at[pl.ds(half, half)], late_dst_ref, sems.at[4]),
        pltpu.make_async_copy(features_ref, line_ref.at[pl.ds(0, rows)], sems.at[5]),
    ]
    for copy in copies:
        copy.start()
    for i in range(half // UNROLL):
        for copy in edges(i, pl.ds(i * UNROLL, UNROLL)):
            copy.start()
    for copy in late:
        copy.start()
    acc_ref[...] = jnp.zeros_like(acc_ref)
    for copy in copies:
        copy.wait()

    def ready(i, at):
        for copy in edges(i, at):
            copy.wait()

    add_tiles(0, scalars, src_buf, dst_buf, acc_ref, ready)
    for copy in late:
        copy.wait()


def last_build_kernel(
    row_ref, col_ref, count_ref, src_ref, dst_ref, half_ref, adj_ref,
    acc_ref, row_buf, col_buf, count_buf, sems,
):
    scalars = [row_buf, col_buf, count_buf]
    copies = [
        pltpu.make_async_copy(ref, buf, sems.at[i])
        for i, (ref, buf) in enumerate(zip([row_ref, col_ref, count_ref], scalars))
    ]
    for copy in copies:
        copy.start()
    acc_ref[...] = half_ref[...]
    for copy in copies:
        copy.wait()
    add_tiles(src_ref.shape[0], scalars, src_ref, dst_ref, acc_ref, lambda i, at: None)
    row_blocks, col_blocks = acc_ref.shape[:2]
    for g in range(row_blocks):
        for c in range(col_blocks):
            adj_ref[g * BLK : (g + 1) * BLK, c * BLK : (c + 1) * BLK] = acc_ref[g, c].astype(BF16)


def gather_kernel(adj_ref, *refs):
    *feature_refs, keep_ref, send_ref = refs
    half = keep_ref.shape[0] - PAD
    total, at = None, 0
    for ref in feature_refs:
        size = ref.shape[0]
        part = jnp.dot(adj_ref[:, at : at + size], ref[...], preferred_element_type=F32)
        total = part if total is None else total + part
        at += size
    ones = jnp.ones((PAD, adj_ref.shape[1]), BF16)
    degree = lax.dot_general(
        ones, adj_ref[...], (((1,), (1,)), ((), ())), preferred_element_type=F32
    )
    keep_ref[:half] = total[:half]
    keep_ref[half:] = degree[:, :half]
    send_ref[:half] = total[half:].astype(BF16)
    send_ref[half:] = split(degree[:1, half:])


def pair_kernel(keep_ref, got_ref, pair_ref):
    half = keep_ref.shape[0] - PAD
    pair_ref[:half] = (keep_ref[:half] + got_ref[:half].astype(F32)).astype(BF16)
    pair_ref[half:] = split(keep_ref[half : half + 1] + joined(got_ref[half:]))


def node_kernel(
    pair_ref, got_ref, features_ref, near_features_ref, d_out_ref, near_d_out_ref,
    w_self_ref, w_neigh_ref, bias_ref,
    out_ref, self_ref, keep_ref, send_ref,
):
    rows, width = out_ref.shape
    half = 2 * rows
    swapped = jnp.concatenate([got_ref[rows:half], got_ref[:rows]], axis=0).astype(F32)
    sums = pair_ref[:half].astype(F32) + swapped
    far = joined(got_ref[half:])
    degree = joined(pair_ref[half:]) + jnp.concatenate([far[:, rows:], far[:, :rows]], axis=1)
    inverse_row = 1.0 / jnp.maximum(degree, 1.0)
    diagonal = lax.broadcasted_iota(jnp.int32, (half, half), 0) == lax.broadcasted_iota(
        jnp.int32, (half, half), 1
    )
    inverse = jnp.sum(jnp.where(diagonal, inverse_row, 0.0), axis=1, keepdims=True)
    agg = (sums * inverse).astype(BF16)
    features = jnp.concatenate([features_ref[...], near_features_ref[...]], axis=0)
    d_out = jnp.concatenate([d_out_ref[...], near_d_out_ref[...]], axis=0).astype(F32)
    pre = (
        jnp.dot(features, w_self_ref[...], preferred_element_type=F32)
        + jnp.dot(agg, w_neigh_ref[...], preferred_element_type=F32)
        + bias_ref[...]
    )
    square = pre * pre
    bend = jnp.tanh(0.7978845608 * pre * (1.0 + 0.044715 * square))
    out_ref[...] = (0.5 * pre[:rows] * (1.0 + bend[:rows])).astype(BF16)
    slope = 0.5 * (1.0 + bend) + 0.5 * pre * (1.0 - bend * bend) * (
        0.7978845608 * (1.0 + 3.0 * 0.044715 * square)
    )
    d_pre = (d_out * slope).astype(BF16)
    transposed = (((1,), (1,)), ((), ()))
    self_ref[...] = lax.dot_general(
        d_pre[:rows], w_self_ref[...], transposed, preferred_element_type=F32
    )
    back = lax.dot_general(d_pre, w_neigh_ref[...], transposed, preferred_element_type=F32)
    send_ref[:half] = (back * inverse).astype(BF16)
    me = lax.axis_index("rep")
    terms = jnp.where(me >> 1 == 0, features, agg)
    grads = lax.dot_general(terms, d_pre, (((0,), (0,)), ((), ())), preferred_element_type=F32)
    middle = width // 2
    low = me & 1 == 0
    bias_term = jnp.sum(d_pre[:rows].astype(F32), axis=0, keepdims=True) + jnp.sum(
        d_pre[rows:].astype(F32), axis=0, keepdims=True
    )
    keep_ref[:middle] = jnp.where(low, grads[:middle], grads[middle:])
    keep_ref[middle:] = split(bias_term).astype(F32)
    send_ref[half : half + middle] = jnp.where(low, grads[middle:], grads[:middle]).astype(BF16)
    send_ref[half + middle :] = split(bias_term)


def spread_kernel(adj_ref, sent_ref, got_ref, keep_ref, *msg_refs):
    half = adj_ref.shape[0] // 2
    size = adj_ref.shape[1] // 4
    g = jnp.concatenate([sent_ref[:half], got_ref[:half]], axis=0)
    for m, ref in enumerate([keep_ref, *msg_refs]):
        blocks = lax.dot_general(
            adj_ref[:, m * size : (m + 1) * size],
            g,
            (((0,), (0,)), ((), ())),
            preferred_element_type=F32,
        )
        ref[...] = blocks.astype(ref.dtype)


def near_sum_kernel(keep_ref, *refs):
    blocks = tree([ref[...].astype(F32) for ref in (keep_ref, *refs[:3])])
    for h, ref in enumerate(refs[3:]):
        ref[...] = blocks[h * BLK : (h + 1) * BLK].astype(ref.dtype)


def finish_kernel(self_ref, *refs):
    *terms, d_features_ref, grad_self_ref, grad_neigh_ref = refs
    quarters, terms = terms[:4], terms[4:]
    d_features_ref[...] = self_ref[...] + tree([ref[...].astype(F32) for ref in terms])
    me = lax.axis_index("rep")
    low = me >> 1 == 0
    for h in range(2):
        same, other = quarters[h][...].astype(F32), quarters[2 + h][...].astype(F32)
        grad_self_ref[(me & 1) ^ h] = jnp.where(low, same, other)
        grad_neigh_ref[(me & 1) ^ h] = jnp.where(low, other, same)


def core_terms_kernel(keep_ref, got_ref, terms_ref):
    middle = keep_ref.shape[0] - PAD
    at = got_ref.shape[0] - PAD
    grads = keep_ref[:middle] + got_ref[at - middle : at].astype(F32)
    terms_ref[:middle] = grads.astype(BF16)
    terms_ref[middle:] = split(joined(keep_ref[middle:]) + joined(got_ref[at:]))


def add_terms(refs):
    middle = refs[0].shape[0] - PAD
    grads = tree([ref[:middle].astype(F32) for ref in refs]).astype(BF16)
    return grads, tree([joined(ref[middle:]) for ref in refs])


def far_terms_kernel(*refs):
    *terms, sum_ref = refs
    middle = sum_ref.shape[0] - PAD
    grads, bias_term = add_terms(terms)
    sum_ref[:middle] = grads
    sum_ref[middle:] = split(bias_term)


def near_terms_kernel(*refs):
    *terms, quarter_ref, bias_ref = refs
    quarter_ref[...], bias_ref[...] = add_terms(terms)


def call(kernel, out_shape, specs, args, scratch=()):
    outs = out_shape if isinstance(out_shape, (list, tuple)) else [out_shape]
    held = sum(size_of(v) for v in [*args, *outs])
    held += sum(math.prod(v.shape) * 4 for v in scratch)
    return pl.pallas_call(
        kernel,
        out_shape=out_shape,
        in_specs=specs,
        out_specs=[VMEM] * len(outs) if outs is out_shape else VMEM,
        scratch_shapes=list(scratch),
        compiler_params=pltpu.CompilerParams(vmem_limit_bytes=2 * held + 4 * 1024 * 1024),
    )(*args)


def on_device(
    features, w_self, w_neigh, bias, d_out, tile_row, tile_col, tile_count, edge_src, edge_dst
):
    rows, width = features.shape
    row_count, rep_count = lax.axis_size("row"), lax.axis_size("rep")
    group, columns = rep_count * rows, row_count * rows
    half, middle = group // 2, width // 2
    far = row_count // 4
    shape = jax.ShapeDtypeStruct

    def swap(value, axis, bits):
        return lax.ppermute(value, axis, [(i, i ^ bits) for i in range(lax.axis_size(axis))])

    far_pieces = [swap(features, "row", 4 * h) for h in range(1, far)]
    near = [swap(features, "rep", 2), swap(d_out, "rep", 2)]
    tiles, slots = edge_src.shape
    early = tiles // 2
    tile_row, tile_col, tile_count, edge_src, edge_dst, held_features = (
        pltpu.with_memory_space_constraint(v, pltpu.HBM)
        for v in (tile_row, tile_col, tile_count, edge_src, edge_dst, features)
    )
    scalars = (tile_row, tile_col, tile_count)
    buffers = [pltpu.SMEM((tiles,), jnp.int32)] * 3
    acc_shape = (rep_count, row_count, BLK, BLK)
    chunk_sems = [pltpu.SemaphoreType.DMA((early // UNROLL,))] * 2
    acc, line, late_src, late_dst = call(
        first_build_kernel,
        (
            shape(acc_shape, F32),
            shape((far * rows, width), BF16),
            shape((early, slots), jnp.int32),
            shape((early, slots), jnp.int32),
        ),
        [HBM] * 6,
        (*scalars, edge_src, edge_dst, held_features),
        buffers
        + [pltpu.VMEM((early, slots), jnp.int32)] * 2
        + [pltpu.SemaphoreType.DMA((6,))]
        + chunk_sems,
    )
    acc, line, near, far_pieces = lax.optimization_barrier((acc, line, near, far_pieces))
    for h, piece in enumerate(far_pieces):
        line = lax.dynamic_update_slice(line, piece, ((h + 1) * rows, 0))
    pieces = [line] + [swap(line, "row", m) for m in range(1, 4)]
    adjacency = call(
        last_build_kernel,
        shape((group, columns), BF16),
        [HBM] * 3 + [VMEM] * 3,
        (*scalars, late_src, late_dst, acc),
        [pltpu.VMEM(acc_shape, F32)] + buffers + [pltpu.SemaphoreType.DMA((3,))],
    )
    keep, send = call(
        gather_kernel,
        (shape((half + PAD, width), F32), shape((half + PAD, width), BF16)),
        [VMEM] * (1 + len(pieces)),
        (adjacency, *pieces),
    )
    pair_sum = call(
        pair_kernel,
        shape((half + PAD, width), BF16),
        [VMEM] * 2,
        (keep, swap(send, "rep", 1)),
    )
    out, self_term, keep, send = call(
        node_kernel,
        (
            shape((rows, width), BF16),
            shape((rows, width), F32),
            shape((middle + PAD, width), F32),
            shape((half + middle + PAD, width), BF16),
        ),
        [VMEM] * 9,
        (
            pair_sum,
            swap(pair_sum, "rep", 2),
            features,
            near[0],
            d_out,
            near[1],
            w_self,
            w_neigh,
            bias[None, :],
        ),
    )
    back = swap(send, "rep", 1)
    terms_shape = shape((middle + PAD, width), BF16)
    terms = call(core_terms_kernel, terms_shape, [VMEM] * 2, (keep, back))
    terms, back = lax.optimization_barrier((terms, back))
    far_terms = [terms] + [swap(terms, "row", 4 * h) for h in range(1, far)]
    keep_blocks, *near_msgs = call(
        spread_kernel,
        (shape((far * BLK, width), F32),) + (shape((far * BLK, width), BF16),) * 3,
        [VMEM] * 3,
        (adjacency, send, back),
    )
    got = [swap(msg, "row", m + 1) for m, msg in enumerate(near_msgs)]
    terms = call(far_terms_kernel, terms_shape, [VMEM] * far, far_terms)
    near_terms = [terms] + [swap(terms, "row", m) for m in range(1, 4)]
    quarter, grad_bias = call(
        near_terms_kernel,
        (shape((middle, width), BF16), shape((1, width), F32)),
        [VMEM] * 4,
        near_terms,
    )
    keep_block, *far_msgs = call(
        near_sum_kernel,
        (shape((BLK, width), F32),) + (shape((BLK, width), BF16),) * (far - 1),
        [VMEM] * 4,
        (keep_blocks, *got),
    )
    got = [swap(msg, "row", 4 * (h + 1)) for h, msg in enumerate(far_msgs)]
    quarters = [quarter] + [swap(quarter, "rep", m) for m in range(1, 4)]
    d_features, grad_self, grad_neigh = call(
        finish_kernel,
        (shape((rows, width), F32),) + (shape((2, middle, width), F32),) * 2,
        [VMEM] * (6 + len(got)),
        (self_term, *quarters, keep_block, *got),
    )
    grad_self, grad_neigh = (v.reshape(width, width) for v in (grad_self, grad_neigh))
    return (out, d_features, grad_self, grad_neigh, grad_bias[0])


def solution(mesh):
    return jax.shard_map(
        on_device,
        mesh=mesh,
        in_specs=(
            P(("row", "rep"), None),
            P(),
            P(),
            P(),
            P(("row", "rep"), None),
            P(("row", "rep")),
            P(("row", "rep")),
            P(("row", "rep")),
            P(("row", "rep"), None),
            P(("row", "rep"), None),
        ),
        out_specs=(P(("row", "rep"), None), P(("row", "rep"), None), P(), P(), P()),
        check_vma=False,
    )
```

```python
import math

import jax
import jax.numpy as jnp
from jax import lax
from jax.experimental import pallas as pl
from jax.experimental.pallas import tpu as pltpu
from jax.sharding import PartitionSpec as P

BLK = 128
PAD = 16
BF16 = jnp.bfloat16
F32 = jnp.float32
HOT = jnp.float8_e4m3fn
UNROLL = 64
VMEM = pl.BlockSpec(memory_space=pltpu.VMEM)
HBM = pl.BlockSpec(memory_space=pltpu.HBM)


def size_of(value):
    return math.prod(value.shape) * jnp.dtype(value.dtype).itemsize


def row_place(block):
    away = block ^ lax.axis_index("rep")
    return ((away & 1) << 1) | (away >> 1)


def col_place(block, row_count):
    away = block ^ lax.axis_index("row")
    return (away & 3) * (row_count // 4) + (away >> 2)


def tree(values):
    while len(values) > 1:
        values = [values[i] + values[i + 1] for i in range(0, len(values), 2)]
    return values[0]


def split(value):
    high = value.astype(BF16).astype(F32)
    line = lax.broadcasted_iota(jnp.int32, (PAD, value.shape[1]), 0)
    return jnp.where(line == 0, high, jnp.where(line == 1, value - high, 0.0)).astype(BF16)


def joined(rows):
    rows = rows.astype(F32)
    return rows[0:1] + rows[1:2]


def add_tiles(first, scalars, src_ref, dst_ref, acc_ref, ready):
    row_ref, col_ref, count_ref = scalars
    tiles, slots = src_ref.shape
    col_blocks = acc_ref.shape[1]
    line = lax.broadcasted_iota(jnp.int32, (BLK, slots), 0).astype(BF16)
    slot = lax.broadcasted_iota(jnp.int32, (1, slots), 1)
    one, zero = jnp.ones((), BF16), jnp.zeros((), BF16)

    def step(i, carry):
        base = pl.multiple_of(i * UNROLL, UNROLL)
        ready(i, pl.ds(base, UNROLL))
        dst, src = dst_ref[pl.ds(base, UNROLL), :], src_ref[pl.ds(base, UNROLL), :]
        for u in range(UNROLL):
            tile = first + base + u
            live = jnp.where(slot < count_ref[tile], dst[u : u + 1], -1)
            dst_hot = jnp.where(line == live.astype(BF16), one, zero).astype(HOT)
            src_hot = jnp.where(line == src[u : u + 1].astype(BF16), one, zero).astype(HOT)
            part = lax.dot_general(
                dst_hot, src_hot, (((1,), (1,)), ((), ())), preferred_element_type=F32
            )
            acc_ref[row_place(row_ref[tile]), col_place(col_ref[tile], col_blocks)] += part
        return carry

    lax.fori_loop(0, tiles // UNROLL, step, 0)


def first_build_kernel(
    row_ref, col_ref, count_ref, src_ref, dst_ref, features_ref,
    acc_ref, line_ref, late_src_ref, late_dst_ref,
    row_buf, col_buf, count_buf, src_buf, dst_buf, sems, src_sems, dst_sems,
):
    half, rows = src_buf.shape[0], features_ref.shape[0]
    scalars = [row_buf, col_buf, count_buf]
    copies = [
        pltpu.make_async_copy(ref, buf, sems.at[i])
        for i, (ref, buf) in enumerate(zip([row_ref, col_ref, count_ref], scalars))
    ]

    def edges(i, at):
        return (
            pltpu.make_async_copy(src_ref.at[at], src_buf.at[at], src_sems.at[i]),
            pltpu.make_async_copy(dst_ref.at[at], dst_buf.at[at], dst_sems.at[i]),
        )

    late = [
        pltpu.make_async_copy(src_ref.at[pl.ds(half, half)], late_src_ref, sems.at[3]),
        pltpu.make_async_copy(dst_ref.at[pl.ds(half, half)], late_dst_ref, sems.at[4]),
        pltpu.make_async_copy(features_ref, line_ref.at[pl.ds(0, rows)], sems.at[5]),
    ]
    for copy in copies:
        copy.start()
    for i in range(half // UNROLL):
        for copy in edges(i, pl.ds(i * UNROLL, UNROLL)):
            copy.start()
    for copy in late:
        copy.start()
    acc_ref[...] = jnp.zeros_like(acc_ref)
    for copy in copies:
        copy.wait()

    def ready(i, at):
        for copy in edges(i, at):
            copy.wait()

    add_tiles(0, scalars, src_buf, dst_buf, acc_ref, ready)
    for copy in late:
        copy.wait()


def last_build_kernel(
    row_ref, col_ref, count_ref, src_ref, dst_ref, half_ref, adj_ref,
    acc_ref, row_buf, col_buf, count_buf, sems,
):
    scalars = [row_buf, col_buf, count_buf]
    copies = [
        pltpu.make_async_copy(ref, buf, sems.at[i])
        for i, (ref, buf) in enumerate(zip([row_ref, col_ref, count_ref], scalars))
    ]
    for copy in copies:
        copy.start()
    acc_ref[...] = half_ref[...]
    for copy in copies:
        copy.wait()
    add_tiles(src_ref.shape[0], scalars, src_ref, dst_ref, acc_ref, lambda i, at: None)
    row_blocks, col_blocks = acc_ref.shape[:2]
    for g in range(row_blocks):
        for c in range(col_blocks):
            adj_ref[g * BLK : (g + 1) * BLK, c * BLK : (c + 1) * BLK] = acc_ref[g, c].astype(BF16)


def gather_kernel(adj_ref, *refs):
    *feature_refs, keep_ref, send_ref = refs
    half = keep_ref.shape[0] - PAD
    total, at = None, 0
    for ref in feature_refs:
        size = ref.shape[0]
        part = jnp.dot(adj_ref[:, at : at + size], ref[...], preferred_element_type=F32)
        total = part if total is None else total + part
        at += size
    ones = jnp.ones((PAD, adj_ref.shape[1]), BF16)
    degree = lax.dot_general(
        ones, adj_ref[...], (((1,), (1,)), ((), ())), preferred_element_type=F32
    )
    keep_ref[:half] = total[:half]
    keep_ref[half:] = degree[:, :half]
    send_ref[:half] = total[half:].astype(BF16)
    send_ref[half:] = split(degree[:1, half:])


def pair_kernel(keep_ref, got_ref, pair_ref):
    half = keep_ref.shape[0] - PAD
    pair_ref[:half] = (keep_ref[:half] + got_ref[:half].astype(F32)).astype(BF16)
    pair_ref[half:] = split(keep_ref[half : half + 1] + joined(got_ref[half:]))


def node_kernel(
    pair_ref, got_ref, features_ref, near_features_ref, d_out_ref, near_d_out_ref,
    w_self_ref, w_neigh_ref, bias_ref,
    out_ref, self_ref, keep_ref, send_ref,
):
    rows, width = out_ref.shape
    half = 2 * rows
    swapped = jnp.concatenate([got_ref[rows:half], got_ref[:rows]], axis=0).astype(F32)
    sums = pair_ref[:half].astype(F32) + swapped
    far = joined(got_ref[half:])
    degree = joined(pair_ref[half:]) + jnp.concatenate([far[:, rows:], far[:, :rows]], axis=1)
    inverse_row = 1.0 / jnp.maximum(degree, 1.0)
    diagonal = lax.broadcasted_iota(jnp.int32, (half, half), 0) == lax.broadcasted_iota(
        jnp.int32, (half, half), 1
    )
    inverse = jnp.sum(jnp.where(diagonal, inverse_row, 0.0), axis=1, keepdims=True)
    agg = (sums * inverse).astype(BF16)
    features = jnp.concatenate([features_ref[...], near_features_ref[...]], axis=0)
    d_out = jnp.concatenate([d_out_ref[...], near_d_out_ref[...]], axis=0).astype(F32)
    pre = (
        jnp.dot(features, w_self_ref[...], preferred_element_type=F32)
        + jnp.dot(agg, w_neigh_ref[...], preferred_element_type=F32)
        + bias_ref[...]
    )
    square = pre * pre
    bend = jnp.tanh(0.7978845608 * pre * (1.0 + 0.044715 * square))
    out_ref[...] = (0.5 * pre[:rows] * (1.0 + bend[:rows])).astype(BF16)
    slope = 0.5 * (1.0 + bend) + 0.5 * pre * (1.0 - bend * bend) * (
        0.7978845608 * (1.0 + 3.0 * 0.044715 * square)
    )
    d_pre = (d_out * slope).astype(BF16)
    transposed = (((1,), (1,)), ((), ()))
    self_ref[...] = lax.dot_general(
        d_pre[:rows], w_self_ref[...], transposed, preferred_element_type=F32
    )
    back = lax.dot_general(d_pre, w_neigh_ref[...], transposed, preferred_element_type=F32)
    send_ref[:half] = (back * inverse).astype(BF16)
    me = lax.axis_index("rep")
    terms = jnp.where(me >> 1 == 0, features, agg)
    grads = lax.dot_general(terms, d_pre, (((0,), (0,)), ((), ())), preferred_element_type=F32)
    middle = width // 2
    low = me & 1 == 0
    bias_term = jnp.sum(d_pre[:rows].astype(F32), axis=0, keepdims=True) + jnp.sum(
        d_pre[rows:].astype(F32), axis=0, keepdims=True
    )
    keep_ref[:middle] = jnp.where(low, grads[:middle], grads[middle:])
    keep_ref[middle:] = split(bias_term).astype(F32)
    send_ref[half : half + middle] = jnp.where(low, grads[middle:], grads[:middle]).astype(BF16)
    send_ref[half + middle :] = split(bias_term)


def spread_kernel(adj_ref, sent_ref, got_ref, keep_ref, *msg_refs):
    half = adj_ref.shape[0] // 2
    size = adj_ref.shape[1] // 4
    g = jnp.concatenate([sent_ref[:half], got_ref[:half]], axis=0)
    for m, ref in enumerate([keep_ref, *msg_refs]):
        blocks = lax.dot_general(
            adj_ref[:, m * size : (m + 1) * size],
            g,
            (((0,), (0,)), ((), ())),
            preferred_element_type=F32,
        )
        ref[...] = blocks.astype(ref.dtype)


def near_sum_kernel(keep_ref, *refs):
    blocks = tree([ref[...].astype(F32) for ref in (keep_ref, *refs[:3])])
    for h, ref in enumerate(refs[3:]):
        ref[...] = blocks[h * BLK : (h + 1) * BLK].astype(ref.dtype)


def finish_kernel(self_ref, *refs):
    *terms, d_features_ref, grad_self_ref, grad_neigh_ref = refs
    quarters, terms = terms[:4], terms[4:]
    d_features_ref[...] = self_ref[...] + tree([ref[...].astype(F32) for ref in terms])
    me = lax.axis_index("rep")
    low = me >> 1 == 0
    for h in range(2):
        same, other = quarters[h][...].astype(F32), quarters[2 + h][...].astype(F32)
        grad_self_ref[(me & 1) ^ h] = jnp.where(low, same, other)
        grad_neigh_ref[(me & 1) ^ h] = jnp.where(low, other, same)


def core_terms_kernel(keep_ref, got_ref, terms_ref):
    middle = keep_ref.shape[0] - PAD
    at = got_ref.shape[0] - PAD
    grads = keep_ref[:middle] + got_ref[at - middle : at].astype(F32)
    terms_ref[:middle] = grads.astype(BF16)
    terms_ref[middle:] = split(joined(keep_ref[middle:]) + joined(got_ref[at:]))


def add_terms(refs):
    middle = refs[0].shape[0] - PAD
    grads = tree([ref[:middle].astype(F32) for ref in refs]).astype(BF16)
    return grads, tree([joined(ref[middle:]) for ref in refs])


def far_terms_kernel(*refs):
    *terms, sum_ref = refs
    middle = sum_ref.shape[0] - PAD
    grads, bias_term = add_terms(terms)
    sum_ref[:middle] = grads
    sum_ref[middle:] = split(bias_term)


def near_terms_kernel(*refs):
    *terms, quarter_ref, bias_ref = refs
    quarter_ref[...], bias_ref[...] = add_terms(terms)


def call(kernel, out_shape, specs, args, scratch=()):
    outs = out_shape if isinstance(out_shape, (list, tuple)) else [out_shape]
    held = sum(size_of(v) for v in [*args, *outs])
    held += sum(math.prod(v.shape) * 4 for v in scratch)
    return pl.pallas_call(
        kernel,
        out_shape=out_shape,
        in_specs=specs,
        out_specs=[VMEM] * len(outs) if outs is out_shape else VMEM,
        scratch_shapes=list(scratch),
        compiler_params=pltpu.CompilerParams(vmem_limit_bytes=2 * held + 4 * 1024 * 1024),
    )(*args)


def on_device(
    features, w_self, w_neigh, bias, d_out, tile_row, tile_col, tile_count, edge_src, edge_dst
):
    rows, width = features.shape
    row_count, rep_count = lax.axis_size("row"), lax.axis_size("rep")
    group, columns = rep_count * rows, row_count * rows
    half, middle = group // 2, width // 2
    far = row_count // 4
    shape = jax.ShapeDtypeStruct

    def swap(value, axis, bits):
        return lax.ppermute(value, axis, [(i, i ^ bits) for i in range(lax.axis_size(axis))])

    far_pieces = [swap(features, "row", 4 * h) for h in range(1, far)]
    near = [swap(features, "rep", 2), swap(d_out, "rep", 2)]
    tiles, slots = edge_src.shape
    early = tiles // 2
    tile_row, tile_col, tile_count, edge_src, edge_dst, held_features = (
        pltpu.with_memory_space_constraint(v, pltpu.HBM)
        for v in (tile_row, tile_col, tile_count, edge_src, edge_dst, features)
    )
    scalars = (tile_row, tile_col, tile_count)
    buffers = [pltpu.SMEM((tiles,), jnp.int32)] * 3
    acc_shape = (rep_count, row_count, BLK, BLK)
    chunk_sems = [pltpu.SemaphoreType.DMA((early // UNROLL,))] * 2
    acc, line, late_src, late_dst = call(
        first_build_kernel,
        (
            shape(acc_shape, F32),
            shape((far * rows, width), BF16),
            shape((early, slots), jnp.int32),
            shape((early, slots), jnp.int32),
        ),
        [HBM] * 6,
        (*scalars, edge_src, edge_dst, held_features),
        buffers
        + [pltpu.VMEM((early, slots), jnp.int32)] * 2
        + [pltpu.SemaphoreType.DMA((6,))]
        + chunk_sems,
    )
    acc, line, near, far_pieces = lax.optimization_barrier((acc, line, near, far_pieces))
    for h, piece in enumerate(far_pieces):
        line = lax.dynamic_update_slice(line, piece, ((h + 1) * rows, 0))
    pieces = [line] + [swap(line, "row", m) for m in range(1, 4)]
    adjacency = call(
        last_build_kernel,
        shape((group, columns), BF16),
        [HBM] * 3 + [VMEM] * 3,
        (*scalars, late_src, late_dst, acc),
        [pltpu.VMEM(acc_shape, F32)] + buffers + [pltpu.SemaphoreType.DMA((3,))],
    )
    keep, send = call(
        gather_kernel,
        (shape((half + PAD, width), F32), shape((half + PAD, width), BF16)),
        [VMEM] * (1 + len(pieces)),
        (adjacency, *pieces),
    )
    pair_sum = call(
        pair_kernel,
        shape((half + PAD, width), BF16),
        [VMEM] * 2,
        (keep, swap(send, "rep", 1)),
    )
    out, self_term, keep, send = call(
        node_kernel,
        (
            shape((rows, width), BF16),
            shape((rows, width), F32),
            shape((middle + PAD, width), F32),
            shape((half + middle + PAD, width), BF16),
        ),
        [VMEM] * 9,
        (
            pair_sum,
            swap(pair_sum, "rep", 2),
            features,
            near[0],
            d_out,
            near[1],
            w_self,
            w_neigh,
            bias[None, :],
        ),
    )
    back = swap(send, "rep", 1)
    terms_shape = shape((middle + PAD, width), BF16)
    terms = call(core_terms_kernel, terms_shape, [VMEM] * 2, (keep, back))
    terms, back = lax.optimization_barrier((terms, back))
    far_terms = [terms] + [swap(terms, "row", 4 * h) for h in range(1, far)]
    keep_blocks, *near_msgs = call(
        spread_kernel,
        (shape((far * BLK, width), F32),) + (shape((far * BLK, width), BF16),) * 3,
        [VMEM] * 3,
        (adjacency, send, back),
    )
    got = [swap(msg, "row", m + 1) for m, msg in enumerate(near_msgs)][::-1]
    terms = call(far_terms_kernel, terms_shape, [VMEM] * far, far_terms)
    near_terms = [terms] + [swap(terms, "row", m) for m in range(1, 4)]
    quarter, grad_bias = call(
        near_terms_kernel,
        (shape((middle, width), BF16), shape((1, width), F32)),
        [VMEM] * 4,
        near_terms,
    )
    keep_block, *far_msgs = call(
        near_sum_kernel,
        (shape((BLK, width), F32),) + (shape((BLK, width), BF16),) * (far - 1),
        [VMEM] * 4,
        (keep_blocks, *got),
    )
    got = [swap(msg, "row", 4 * (h + 1)) for h, msg in enumerate(far_msgs)]
    quarters = [quarter] + [swap(quarter, "rep", m) for m in range(1, 4)]
    d_features, grad_self, grad_neigh = call(
        finish_kernel,
        (shape((rows, width), F32),) + (shape((2, middle, width), F32),) * 2,
        [VMEM] * (6 + len(got)),
        (self_term, *quarters, keep_block, *got),
    )
    grad_self, grad_neigh = (v.reshape(width, width) for v in (grad_self, grad_neigh))
    return (out, d_features, grad_self, grad_neigh, grad_bias[0])


def solution(mesh):
    return jax.shard_map(
        on_device,
        mesh=mesh,
        in_specs=(
            P(("row", "rep"), None),
            P(),
            P(),
            P(),
            P(("row", "rep"), None),
            P(("row", "rep")),
            P(("row", "rep")),
            P(("row", "rep")),
            P(("row", "rep"), None),
            P(("row", "rep"), None),
        ),
        out_specs=(P(("row", "rep"), None), P(("row", "rep"), None), P(), P(), P()),
        check_vma=False,
    )
```

```python
import math

import jax
import jax.numpy as jnp
from jax import lax
from jax.experimental import pallas as pl
from jax.experimental.pallas import tpu as pltpu
from jax.sharding import PartitionSpec as P

BLK = 128
PAD = 16
BF16 = jnp.bfloat16
F32 = jnp.float32
HOT = jnp.float8_e4m3fn
UNROLL = 64
VMEM = pl.BlockSpec(memory_space=pltpu.VMEM)
HBM = pl.BlockSpec(memory_space=pltpu.HBM)


def size_of(value):
    return math.prod(value.shape) * jnp.dtype(value.dtype).itemsize


def row_place(block):
    away = block ^ lax.axis_index("rep")
    return ((away & 1) << 1) | (away >> 1)


def col_place(block, row_count):
    away = block ^ lax.axis_index("row")
    return (away & 3) * (row_count // 4) + (away >> 2)


def tree(values):
    while len(values) > 1:
        values = [values[i] + values[i + 1] for i in range(0, len(values), 2)]
    return values[0]


def split(value):
    high = value.astype(BF16).astype(F32)
    line = lax.broadcasted_iota(jnp.int32, (PAD, value.shape[1]), 0)
    return jnp.where(line == 0, high, jnp.where(line == 1, value - high, 0.0)).astype(BF16)


def joined(rows):
    rows = rows.astype(F32)
    return rows[0:1] + rows[1:2]


def add_tiles(first, scalars, src_ref, dst_ref, acc_ref, ready):
    row_ref, col_ref, count_ref = scalars
    tiles, slots = src_ref.shape
    col_blocks = acc_ref.shape[1]
    line = lax.broadcasted_iota(jnp.int32, (BLK, slots), 0).astype(BF16)
    slot = lax.broadcasted_iota(jnp.int32, (1, slots), 1)
    one, zero = jnp.ones((), BF16), jnp.zeros((), BF16)

    def step(i, carry):
        base = pl.multiple_of(i * UNROLL, UNROLL)
        ready(i, pl.ds(base, UNROLL))
        dst, src = dst_ref[pl.ds(base, UNROLL), :], src_ref[pl.ds(base, UNROLL), :]
        for u in range(UNROLL):
            tile = first + base + u
            live = jnp.where(slot < count_ref[tile], dst[u : u + 1], -1)
            dst_hot = jnp.where(line == live.astype(BF16), one, zero).astype(HOT)
            src_hot = jnp.where(line == src[u : u + 1].astype(BF16), one, zero).astype(HOT)
            part = lax.dot_general(
                dst_hot, src_hot, (((1,), (1,)), ((), ())), preferred_element_type=F32
            )
            acc_ref[row_place(row_ref[tile]), col_place(col_ref[tile], col_blocks)] += part
        return carry

    lax.fori_loop(0, tiles // UNROLL, step, 0)


def first_build_kernel(
    row_ref, col_ref, count_ref, src_ref, dst_ref, features_ref,
    acc_ref, line_ref, late_src_ref, late_dst_ref,
    row_buf, col_buf, count_buf, src_buf, dst_buf, sems, src_sems, dst_sems,
):
    half, rows = src_buf.shape[0], features_ref.shape[0]
    scalars = [row_buf, col_buf, count_buf]
    copies = [
        pltpu.make_async_copy(ref, buf, sems.at[i])
        for i, (ref, buf) in enumerate(zip([row_ref, col_ref, count_ref], scalars))
    ]

    def edges(i, at):
        return (
            pltpu.make_async_copy(src_ref.at[at], src_buf.at[at], src_sems.at[i]),
            pltpu.make_async_copy(dst_ref.at[at], dst_buf.at[at], dst_sems.at[i]),
        )

    late = [
        pltpu.make_async_copy(src_ref.at[pl.ds(half, half)], late_src_ref, sems.at[3]),
        pltpu.make_async_copy(dst_ref.at[pl.ds(half, half)], late_dst_ref, sems.at[4]),
        pltpu.make_async_copy(features_ref, line_ref.at[pl.ds(0, rows)], sems.at[5]),
    ]
    for copy in copies:
        copy.start()
    for i in range(half // UNROLL):
        for copy in edges(i, pl.ds(i * UNROLL, UNROLL)):
            copy.start()
    for copy in late:
        copy.start()
    acc_ref[...] = jnp.zeros_like(acc_ref)
    for copy in copies:
        copy.wait()

    def ready(i, at):
        for copy in edges(i, at):
            copy.wait()

    add_tiles(0, scalars, src_buf, dst_buf, acc_ref, ready)
    for copy in late:
        copy.wait()


def last_build_kernel(
    row_ref, col_ref, count_ref, src_ref, dst_ref, half_ref, adj_ref,
    acc_ref, row_buf, col_buf, count_buf, sems,
):
    scalars = [row_buf, col_buf, count_buf]
    copies = [
        pltpu.make_async_copy(ref, buf, sems.at[i])
        for i, (ref, buf) in enumerate(zip([row_ref, col_ref, count_ref], scalars))
    ]
    for copy in copies:
        copy.start()
    acc_ref[...] = half_ref[...]
    for copy in copies:
        copy.wait()
    add_tiles(src_ref.shape[0], scalars, src_ref, dst_ref, acc_ref, lambda i, at: None)
    row_blocks, col_blocks = acc_ref.shape[:2]
    for g in range(row_blocks):
        for c in range(col_blocks):
            adj_ref[g * BLK : (g + 1) * BLK, c * BLK : (c + 1) * BLK] = acc_ref[g, c].astype(BF16)


def gather_kernel(adj_ref, *refs):
    *feature_refs, keep_ref, send_ref = refs
    half = keep_ref.shape[0] - PAD
    total, at = None, 0
    for ref in feature_refs:
        size = ref.shape[0]
        part = jnp.dot(adj_ref[:, at : at + size], ref[...], preferred_element_type=F32)
        total = part if total is None else total + part
        at += size
    ones = jnp.ones((PAD, adj_ref.shape[1]), BF16)
    degree = lax.dot_general(
        ones, adj_ref[...], (((1,), (1,)), ((), ())), preferred_element_type=F32
    )
    keep_ref[:half] = total[:half]
    keep_ref[half:] = degree[:, :half]
    send_ref[:half] = total[half:].astype(BF16)
    send_ref[half:] = split(degree[:1, half:])


def pair_kernel(keep_ref, got_ref, pair_ref):
    half = keep_ref.shape[0] - PAD
    pair_ref[:half] = (keep_ref[:half] + got_ref[:half].astype(F32)).astype(BF16)
    pair_ref[half:] = split(keep_ref[half : half + 1] + joined(got_ref[half:]))


def node_kernel(
    pair_ref, got_ref, features_ref, near_features_ref, d_out_ref, near_d_out_ref,
    w_self_ref, w_neigh_ref, bias_ref,
    out_ref, self_ref, keep_ref, send_ref,
):
    rows, width = out_ref.shape
    half = 2 * rows
    swapped = jnp.concatenate([got_ref[rows:half], got_ref[:rows]], axis=0).astype(F32)
    sums = pair_ref[:half].astype(F32) + swapped
    far = joined(got_ref[half:])
    degree = joined(pair_ref[half:]) + jnp.concatenate([far[:, rows:], far[:, :rows]], axis=1)
    inverse_row = 1.0 / jnp.maximum(degree, 1.0)
    diagonal = lax.broadcasted_iota(jnp.int32, (half, half), 0) == lax.broadcasted_iota(
        jnp.int32, (half, half), 1
    )
    inverse = jnp.sum(jnp.where(diagonal, inverse_row, 0.0), axis=1, keepdims=True)
    agg = (sums * inverse).astype(BF16)
    features = jnp.concatenate([features_ref[...], near_features_ref[...]], axis=0)
    d_out = jnp.concatenate([d_out_ref[...], near_d_out_ref[...]], axis=0).astype(F32)
    pre = (
        jnp.dot(features, w_self_ref[...], preferred_element_type=F32)
        + jnp.dot(agg, w_neigh_ref[...], preferred_element_type=F32)
        + bias_ref[...]
    )
    square = pre * pre
    bend = jnp.tanh(0.7978845608 * pre * (1.0 + 0.044715 * square))
    out_ref[...] = (0.5 * pre[:rows] * (1.0 + bend[:rows])).astype(BF16)
    slope = 0.5 * (1.0 + bend) + 0.5 * pre * (1.0 - bend * bend) * (
        0.7978845608 * (1.0 + 3.0 * 0.044715 * square)
    )
    d_pre = (d_out * slope).astype(BF16)
    transposed = (((1,), (1,)), ((), ()))
    self_ref[...] = lax.dot_general(
        d_pre[:rows], w_self_ref[...], transposed, preferred_element_type=F32
    )
    back = lax.dot_general(d_pre, w_neigh_ref[...], transposed, preferred_element_type=F32)
    send_ref[:half] = (back * inverse).astype(BF16)
    me = lax.axis_index("rep")
    terms = jnp.where(me >> 1 == 0, features, agg)
    grads = lax.dot_general(terms, d_pre, (((0,), (0,)), ((), ())), preferred_element_type=F32)
    middle = width // 2
    low = me & 1 == 0
    bias_term = jnp.sum(d_pre[:rows].astype(F32), axis=0, keepdims=True) + jnp.sum(
        d_pre[rows:].astype(F32), axis=0, keepdims=True
    )
    keep_ref[:middle] = jnp.where(low, grads[:middle], grads[middle:])
    keep_ref[middle:] = split(bias_term).astype(F32)
    send_ref[half : half + middle] = jnp.where(low, grads[middle:], grads[:middle]).astype(BF16)
    send_ref[half + middle :] = split(bias_term)


def spread_kernel(adj_ref, sent_ref, got_ref, keep_ref, *msg_refs):
    half = adj_ref.shape[0] // 2
    size = adj_ref.shape[1] // 4
    g = jnp.concatenate([sent_ref[:half], got_ref[:half]], axis=0)
    for m, ref in enumerate([keep_ref, *msg_refs]):
        blocks = lax.dot_general(
            adj_ref[:, m * size : (m + 1) * size],
            g,
            (((0,), (0,)), ((), ())),
            preferred_element_type=F32,
        )
        ref[...] = blocks.astype(ref.dtype)


def near_sum_kernel(keep_ref, *refs):
    blocks = tree([ref[...].astype(F32) for ref in (keep_ref, *refs[:3])])
    for h, ref in enumerate(refs[3:]):
        ref[...] = blocks[h * BLK : (h + 1) * BLK].astype(ref.dtype)


def finish_kernel(self_ref, *refs):
    *terms, d_features_ref, grad_self_ref, grad_neigh_ref = refs
    quarters, terms = terms[:4], terms[4:]
    d_features_ref[...] = self_ref[...] + tree([ref[...].astype(F32) for ref in terms])
    me = lax.axis_index("rep")
    low = me >> 1 == 0
    for h in range(2):
        same, other = quarters[h][...].astype(F32), quarters[2 + h][...].astype(F32)
        grad_self_ref[(me & 1) ^ h] = jnp.where(low, same, other)
        grad_neigh_ref[(me & 1) ^ h] = jnp.where(low, other, same)


def core_terms_kernel(keep_ref, got_ref, terms_ref):
    middle = keep_ref.shape[0] - PAD
    at = got_ref.shape[0] - PAD
    grads = keep_ref[:middle] + got_ref[at - middle : at].astype(F32)
    terms_ref[:middle] = grads.astype(BF16)
    terms_ref[middle:] = split(joined(keep_ref[middle:]) + joined(got_ref[at:]))


def add_terms(refs):
    middle = refs[0].shape[0] - PAD
    grads = tree([ref[:middle].astype(F32) for ref in refs]).astype(BF16)
    return grads, tree([joined(ref[middle:]) for ref in refs])


def far_terms_kernel(*refs):
    *terms, sum_ref = refs
    middle = sum_ref.shape[0] - PAD
    grads, bias_term = add_terms(terms)
    sum_ref[:middle] = grads
    sum_ref[middle:] = split(bias_term)


def near_terms_kernel(*refs):
    *terms, quarter_ref, bias_ref = refs
    quarter_ref[...], bias_ref[...] = add_terms(terms)


def call(kernel, out_shape, specs, args, scratch=()):
    outs = out_shape if isinstance(out_shape, (list, tuple)) else [out_shape]
    held = sum(size_of(v) for v in [*args, *outs])
    held += sum(math.prod(v.shape) * 4 for v in scratch)
    return pl.pallas_call(
        kernel,
        out_shape=out_shape,
        in_specs=specs,
        out_specs=[VMEM] * len(outs) if outs is out_shape else VMEM,
        scratch_shapes=list(scratch),
        compiler_params=pltpu.CompilerParams(vmem_limit_bytes=2 * held + 4 * 1024 * 1024),
    )(*args)


def on_device(
    features, w_self, w_neigh, bias, d_out, tile_row, tile_col, tile_count, edge_src, edge_dst
):
    rows, width = features.shape
    row_count, rep_count = lax.axis_size("row"), lax.axis_size("rep")
    group, columns = rep_count * rows, row_count * rows
    half, middle = group // 2, width // 2
    far = row_count // 4
    shape = jax.ShapeDtypeStruct

    def swap(value, axis, bits):
        return lax.ppermute(value, axis, [(i, i ^ bits) for i in range(lax.axis_size(axis))])

    far_pieces = [swap(features, "row", 4 * h) for h in range(1, far)]
    tiles, slots = edge_src.shape
    early = tiles // 2
    tile_row, tile_col, tile_count, edge_src, edge_dst, held_features = (
        pltpu.with_memory_space_constraint(v, pltpu.HBM)
        for v in (tile_row, tile_col, tile_count, edge_src, edge_dst, features)
    )
    scalars = (tile_row, tile_col, tile_count)
    buffers = [pltpu.SMEM((tiles,), jnp.int32)] * 3
    acc_shape = (rep_count, row_count, BLK, BLK)
    chunk_sems = [pltpu.SemaphoreType.DMA((early // UNROLL,))] * 2
    acc, line, late_src, late_dst = call(
        first_build_kernel,
        (
            shape(acc_shape, F32),
            shape((far * rows, width), BF16),
            shape((early, slots), jnp.int32),
            shape((early, slots), jnp.int32),
        ),
        [HBM] * 6,
        (*scalars, edge_src, edge_dst, held_features),
        buffers
        + [pltpu.VMEM((early, slots), jnp.int32)] * 2
        + [pltpu.SemaphoreType.DMA((6,))]
        + chunk_sems,
    )
    acc, line, far_pieces = lax.optimization_barrier((acc, line, far_pieces))
    for h, piece in enumerate(far_pieces):
        line = lax.dynamic_update_slice(line, piece, ((h + 1) * rows, 0))
    pieces = [line] + [swap(line, "row", m) for m in range(1, 4)]
    near_features, near_d_out, acc = lax.optimization_barrier((features, d_out, acc))
    near = [swap(near_features, "rep", 2), swap(near_d_out, "rep", 2)]
    adjacency = call(
        last_build_kernel,
        shape((group, columns), BF16),
        [HBM] * 3 + [VMEM] * 3,
        (*scalars, late_src, late_dst, acc),
        [pltpu.VMEM(acc_shape, F32)] + buffers + [pltpu.SemaphoreType.DMA((3,))],
    )
    adjacency, near, pieces = lax.optimization_barrier((adjacency, near, pieces))
    keep, send = call(
        gather_kernel,
        (shape((half + PAD, width), F32), shape((half + PAD, width), BF16)),
        [VMEM] * (1 + len(pieces)),
        (adjacency, *pieces),
    )
    pair_sum = call(
        pair_kernel,
        shape((half + PAD, width), BF16),
        [VMEM] * 2,
        (keep, swap(send, "rep", 1)),
    )
    out, self_term, keep, send = call(
        node_kernel,
        (
            shape((rows, width), BF16),
            shape((rows, width), F32),
            shape((middle + PAD, width), F32),
            shape((half + middle + PAD, width), BF16),
        ),
        [VMEM] * 9,
        (
            pair_sum,
            swap(pair_sum, "rep", 2),
            features,
            near[0],
            d_out,
            near[1],
            w_self,
            w_neigh,
            bias[None, :],
        ),
    )
    back = swap(send, "rep", 1)
    terms_shape = shape((middle + PAD, width), BF16)
    terms = call(core_terms_kernel, terms_shape, [VMEM] * 2, (keep, back))
    terms, back = lax.optimization_barrier((terms, back))
    far_terms = [terms] + [swap(terms, "row", 4 * h) for h in range(1, far)]
    keep_blocks, *near_msgs = call(
        spread_kernel,
        (shape((far * BLK, width), F32),) + (shape((far * BLK, width), BF16),) * 3,
        [VMEM] * 3,
        (adjacency, send, back),
    )
    got = [swap(msg, "row", m + 1) for m, msg in enumerate(near_msgs)][::-1]
    terms = call(far_terms_kernel, terms_shape, [VMEM] * far, far_terms)
    near_terms = [terms] + [swap(terms, "row", m) for m in range(1, 4)]
    quarter, grad_bias = call(
        near_terms_kernel,
        (shape((middle, width), BF16), shape((1, width), F32)),
        [VMEM] * 4,
        near_terms,
    )
    keep_block, *far_msgs = call(
        near_sum_kernel,
        (shape((BLK, width), F32),) + (shape((BLK, width), BF16),) * (far - 1),
        [VMEM] * 4,
        (keep_blocks, *got),
    )
    got = [swap(msg, "row", 4 * (h + 1)) for h, msg in enumerate(far_msgs)]
    quarters = [quarter] + [swap(quarter, "rep", m) for m in range(1, 4)]
    d_features, grad_self, grad_neigh = call(
        finish_kernel,
        (shape((rows, width), F32),) + (shape((2, middle, width), F32),) * 2,
        [VMEM] * (6 + len(got)),
        (self_term, *quarters, keep_block, *got),
    )
    grad_self, grad_neigh = (v.reshape(width, width) for v in (grad_self, grad_neigh))
    return (out, d_features, grad_self, grad_neigh, grad_bias[0])


def solution(mesh):
    return jax.shard_map(
        on_device,
        mesh=mesh,
        in_specs=(
            P(("row", "rep"), None),
            P(),
            P(),
            P(),
            P(("row", "rep"), None),
            P(("row", "rep")),
            P(("row", "rep")),
            P(("row", "rep")),
            P(("row", "rep"), None),
            P(("row", "rep"), None),
        ),
        out_specs=(P(("row", "rep"), None), P(("row", "rep"), None), P(), P(), P()),
        check_vma=False,
    )
```

```python
import math

import jax
import jax.numpy as jnp
from jax import lax
from jax.experimental import pallas as pl
from jax.experimental.pallas import tpu as pltpu
from jax.sharding import PartitionSpec as P

BLK = 128
PAD = 16
BF16 = jnp.bfloat16
F32 = jnp.float32
HOT = jnp.float8_e4m3fn
UNROLL = 64
VMEM = pl.BlockSpec(memory_space=pltpu.VMEM)
HBM = pl.BlockSpec(memory_space=pltpu.HBM)


def size_of(value):
    return math.prod(value.shape) * jnp.dtype(value.dtype).itemsize


def row_place(block):
    away = block ^ lax.axis_index("rep")
    return ((away & 1) << 1) | (away >> 1)


def col_place(block, row_count):
    away = block ^ lax.axis_index("row")
    return (away & 3) * (row_count // 4) + (away >> 2)


def tree(values):
    while len(values) > 1:
        values = [values[i] + values[i + 1] for i in range(0, len(values), 2)]
    return values[0]


def split(value):
    high = value.astype(BF16).astype(F32)
    line = lax.broadcasted_iota(jnp.int32, (PAD, value.shape[1]), 0)
    return jnp.where(line == 0, high, jnp.where(line == 1, value - high, 0.0)).astype(BF16)


def joined(rows):
    rows = rows.astype(F32)
    return rows[0:1] + rows[1:2]


def add_tiles(first, scalars, src_ref, dst_ref, acc_ref, ready):
    row_ref, col_ref, count_ref = scalars
    tiles, slots = src_ref.shape
    col_blocks = acc_ref.shape[1]
    line = lax.broadcasted_iota(jnp.int32, (BLK, slots), 0).astype(BF16)
    slot = lax.broadcasted_iota(jnp.int32, (1, slots), 1)
    one, zero = jnp.ones((), BF16), jnp.zeros((), BF16)

    def step(i, carry):
        base = pl.multiple_of(i * UNROLL, UNROLL)
        ready(i, pl.ds(base, UNROLL))
        dst, src = dst_ref[pl.ds(base, UNROLL), :], src_ref[pl.ds(base, UNROLL), :]
        for u in range(UNROLL):
            tile = first + base + u
            live = jnp.where(slot < count_ref[tile], dst[u : u + 1], -1)
            dst_hot = jnp.where(line == live.astype(BF16), one, zero).astype(HOT)
            src_hot = jnp.where(line == src[u : u + 1].astype(BF16), one, zero).astype(HOT)
            part = lax.dot_general(
                dst_hot, src_hot, (((1,), (1,)), ((), ())), preferred_element_type=F32
            )
            acc_ref[row_place(row_ref[tile]), col_place(col_ref[tile], col_blocks)] += part
        return carry

    lax.fori_loop(0, tiles // UNROLL, step, 0)


def first_build_kernel(
    row_ref, col_ref, count_ref, src_ref, dst_ref, features_ref,
    acc_ref, line_ref, late_src_ref, late_dst_ref,
    row_buf, col_buf, count_buf, src_buf, dst_buf, sems, src_sems, dst_sems,
):
    half, rows = src_buf.shape[0], features_ref.shape[0]
    scalars = [row_buf, col_buf, count_buf]
    copies = [
        pltpu.make_async_copy(ref, buf, sems.at[i])
        for i, (ref, buf) in enumerate(zip([row_ref, col_ref, count_ref], scalars))
    ]

    def edges(i, at):
        return (
            pltpu.make_async_copy(src_ref.at[at], src_buf.at[at], src_sems.at[i]),
            pltpu.make_async_copy(dst_ref.at[at], dst_buf.at[at], dst_sems.at[i]),
        )

    late = [
        pltpu.make_async_copy(src_ref.at[pl.ds(half, half)], late_src_ref, sems.at[3]),
        pltpu.make_async_copy(dst_ref.at[pl.ds(half, half)], late_dst_ref, sems.at[4]),
        pltpu.make_async_copy(features_ref, line_ref.at[pl.ds(0, rows)], sems.at[5]),
    ]
    for copy in copies:
        copy.start()
    for i in range(half // UNROLL):
        for copy in edges(i, pl.ds(i * UNROLL, UNROLL)):
            copy.start()
    for copy in late:
        copy.start()
    acc_ref[...] = jnp.zeros_like(acc_ref)
    for copy in copies:
        copy.wait()

    def ready(i, at):
        for copy in edges(i, at):
            copy.wait()

    add_tiles(0, scalars, src_buf, dst_buf, acc_ref, ready)
    for copy in late:
        copy.wait()


def last_build_kernel(
    row_ref, col_ref, count_ref, src_ref, dst_ref, half_ref, adj_ref,
    acc_ref, row_buf, col_buf, count_buf, sems,
):
    scalars = [row_buf, col_buf, count_buf]
    copies = [
        pltpu.make_async_copy(ref, buf, sems.at[i])
        for i, (ref, buf) in enumerate(zip([row_ref, col_ref, count_ref], scalars))
    ]
    for copy in copies:
        copy.start()
    acc_ref[...] = half_ref[...]
    for copy in copies:
        copy.wait()
    add_tiles(src_ref.shape[0], scalars, src_ref, dst_ref, acc_ref, lambda i, at: None)
    row_blocks, col_blocks = acc_ref.shape[:2]
    for g in range(row_blocks):
        for c in range(col_blocks):
            adj_ref[g * BLK : (g + 1) * BLK, c * BLK : (c + 1) * BLK] = acc_ref[g, c].astype(BF16)


def gather_kernel(adj_ref, *refs):
    *feature_refs, keep_ref, send_ref = refs
    half = keep_ref.shape[0] - PAD
    total, at = None, 0
    for ref in feature_refs:
        size = ref.shape[0]
        part = jnp.dot(adj_ref[:, at : at + size], ref[...], preferred_element_type=F32)
        total = part if total is None else total + part
        at += size
    ones = jnp.ones((PAD, adj_ref.shape[1]), BF16)
    degree = lax.dot_general(
        ones, adj_ref[...], (((1,), (1,)), ((), ())), preferred_element_type=F32
    )
    keep_ref[:half] = total[:half]
    keep_ref[half:] = degree[:, :half]
    send_ref[:half] = total[half:].astype(BF16)
    send_ref[half:] = split(degree[:1, half:])


def pair_kernel(keep_ref, got_ref, pair_ref):
    half = keep_ref.shape[0] - PAD
    pair_ref[:half] = (keep_ref[:half] + got_ref[:half].astype(F32)).astype(BF16)
    pair_ref[half:] = split(keep_ref[half : half + 1] + joined(got_ref[half:]))


def node_kernel(
    pair_ref, got_ref, features_ref, near_features_ref, d_out_ref, near_d_out_ref,
    w_self_ref, w_neigh_ref, bias_ref,
    out_ref, self_ref, keep_ref, send_ref,
):
    rows, width = out_ref.shape
    half = 2 * rows
    swapped = jnp.concatenate([got_ref[rows:half], got_ref[:rows]], axis=0).astype(F32)
    sums = pair_ref[:half].astype(F32) + swapped
    far = joined(got_ref[half:])
    degree = joined(pair_ref[half:]) + jnp.concatenate([far[:, rows:], far[:, :rows]], axis=1)
    inverse_row = 1.0 / jnp.maximum(degree, 1.0)
    diagonal = lax.broadcasted_iota(jnp.int32, (half, half), 0) == lax.broadcasted_iota(
        jnp.int32, (half, half), 1
    )
    inverse = jnp.sum(jnp.where(diagonal, inverse_row, 0.0), axis=1, keepdims=True)
    agg = (sums * inverse).astype(BF16)
    features = jnp.concatenate([features_ref[...], near_features_ref[...]], axis=0)
    d_out = jnp.concatenate([d_out_ref[...], near_d_out_ref[...]], axis=0).astype(F32)
    pre = (
        jnp.dot(features, w_self_ref[...], preferred_element_type=F32)
        + jnp.dot(agg, w_neigh_ref[...], preferred_element_type=F32)
        + bias_ref[...]
    )
    square = pre * pre
    bend = jnp.tanh(0.7978845608 * pre * (1.0 + 0.044715 * square))
    out_ref[...] = (0.5 * pre[:rows] * (1.0 + bend[:rows])).astype(BF16)
    slope = 0.5 * (1.0 + bend) + 0.5 * pre * (1.0 - bend * bend) * (
        0.7978845608 * (1.0 + 3.0 * 0.044715 * square)
    )
    d_pre = (d_out * slope).astype(BF16)
    transposed = (((1,), (1,)), ((), ()))
    self_ref[...] = lax.dot_general(
        d_pre[:rows], w_self_ref[...], transposed, preferred_element_type=F32
    )
    back = lax.dot_general(d_pre, w_neigh_ref[...], transposed, preferred_element_type=F32)
    send_ref[:half] = (back * inverse).astype(BF16)
    me = lax.axis_index("rep")
    terms = jnp.where(me >> 1 == 0, features, agg)
    grads = lax.dot_general(terms, d_pre, (((0,), (0,)), ((), ())), preferred_element_type=F32)
    middle = width // 2
    low = me & 1 == 0
    bias_term = jnp.sum(d_pre[:rows].astype(F32), axis=0, keepdims=True) + jnp.sum(
        d_pre[rows:].astype(F32), axis=0, keepdims=True
    )
    keep_ref[:middle] = jnp.where(low, grads[:middle], grads[middle:])
    keep_ref[middle:] = split(bias_term).astype(F32)
    send_ref[half : half + middle] = jnp.where(low, grads[middle:], grads[:middle]).astype(BF16)
    send_ref[half + middle :] = split(bias_term)


def spread_kernel(adj_ref, sent_ref, got_ref, keep_ref, *msg_refs):
    half = adj_ref.shape[0] // 2
    size = adj_ref.shape[1] // 4
    g = jnp.concatenate([sent_ref[:half], got_ref[:half]], axis=0)
    for m, ref in enumerate([keep_ref, *msg_refs]):
        blocks = lax.dot_general(
            adj_ref[:, m * size : (m + 1) * size],
            g,
            (((0,), (0,)), ((), ())),
            preferred_element_type=F32,
        )
        ref[...] = blocks.astype(ref.dtype)


def near_sum_kernel(keep_ref, *refs):
    *sums, out_ref = refs[4:]
    blocks = tree([ref[...].astype(F32) for ref in (keep_ref, *refs[:3])])
    for h, ref in enumerate(sums):
        ref[...] = blocks[h * BLK : (h + 1) * BLK].astype(ref.dtype)
    out_ref[...] = refs[3][...]


def finish_kernel(self_ref, bias_term_ref, *refs):
    *terms, d_features_ref, grad_self_ref, grad_neigh_ref, bias_ref = refs
    quarters, terms = terms[:4], terms[4:]
    d_features_ref[...] = self_ref[...] + tree([ref[...].astype(F32) for ref in terms])
    bias_ref[...] = bias_term_ref[...]
    me = lax.axis_index("rep")
    low = me >> 1 == 0
    for h in range(2):
        same, other = quarters[h][...].astype(F32), quarters[2 + h][...].astype(F32)
        grad_self_ref[(me & 1) ^ h] = jnp.where(low, same, other)
        grad_neigh_ref[(me & 1) ^ h] = jnp.where(low, other, same)


def core_terms_kernel(keep_ref, got_ref, terms_ref):
    middle = keep_ref.shape[0] - PAD
    at = got_ref.shape[0] - PAD
    grads = keep_ref[:middle] + got_ref[at - middle : at].astype(F32)
    terms_ref[:middle] = grads.astype(BF16)
    terms_ref[middle:] = split(joined(keep_ref[middle:]) + joined(got_ref[at:]))


def add_terms(refs):
    middle = refs[0].shape[0] - PAD
    grads = tree([ref[:middle].astype(F32) for ref in refs]).astype(BF16)
    return grads, tree([joined(ref[middle:]) for ref in refs])


def part_terms_kernel(*refs):
    *terms, sum_ref = refs
    middle = sum_ref.shape[0] - PAD
    grads, bias_term = add_terms(terms)
    sum_ref[:middle] = grads
    sum_ref[middle:] = split(bias_term)


def all_terms_kernel(*refs):
    *terms, quarter_ref, bias_ref = refs
    quarter_ref[...], bias_ref[...] = add_terms(terms)


def call(kernel, out_shape, specs, args, scratch=()):
    outs = out_shape if isinstance(out_shape, (list, tuple)) else [out_shape]
    held = sum(size_of(v) for v in [*args, *outs])
    held += sum(math.prod(v.shape) * 4 for v in scratch)
    return pl.pallas_call(
        kernel,
        out_shape=out_shape,
        in_specs=specs,
        out_specs=[VMEM] * len(outs) if outs is out_shape else VMEM,
        scratch_shapes=list(scratch),
        compiler_params=pltpu.CompilerParams(vmem_limit_bytes=2 * held + 4 * 1024 * 1024),
    )(*args)


def on_device(
    features, w_self, w_neigh, bias, d_out, tile_row, tile_col, tile_count, edge_src, edge_dst
):
    rows, width = features.shape
    row_count, rep_count = lax.axis_size("row"), lax.axis_size("rep")
    group, columns = rep_count * rows, row_count * rows
    half, middle = group // 2, width // 2
    far = row_count // 4
    shape = jax.ShapeDtypeStruct

    def swap(value, axis, bits):
        return lax.ppermute(value, axis, [(i, i ^ bits) for i in range(lax.axis_size(axis))])

    far_pieces = [swap(features, "row", 4 * h) for h in range(1, far)]
    tiles, slots = edge_src.shape
    early = tiles // 2
    tile_row, tile_col, tile_count, edge_src, edge_dst, held_features = (
        pltpu.with_memory_space_constraint(v, pltpu.HBM)
        for v in (tile_row, tile_col, tile_count, edge_src, edge_dst, features)
    )
    scalars = (tile_row, tile_col, tile_count)
    buffers = [pltpu.SMEM((tiles,), jnp.int32)] * 3
    acc_shape = (rep_count, row_count, BLK, BLK)
    chunk_sems = [pltpu.SemaphoreType.DMA((early // UNROLL,))] * 2
    acc, line, late_src, late_dst = call(
        first_build_kernel,
        (
            shape(acc_shape, F32),
            shape((far * rows, width), BF16),
            shape((early, slots), jnp.int32),
            shape((early, slots), jnp.int32),
        ),
        [HBM] * 6,
        (*scalars, edge_src, edge_dst, held_features),
        buffers
        + [pltpu.VMEM((early, slots), jnp.int32)] * 2
        + [pltpu.SemaphoreType.DMA((6,))]
        + chunk_sems,
    )
    acc, line, far_pieces = lax.optimization_barrier((acc, line, far_pieces))
    for h, piece in enumerate(far_pieces):
        line = lax.dynamic_update_slice(line, piece, ((h + 1) * rows, 0))
    pieces = [line] + [swap(line, "row", m) for m in range(1, 4)]
    near_features, near_d_out, acc = lax.optimization_barrier((features, d_out, acc))
    near = [swap(near_features, "rep", 2), swap(near_d_out, "rep", 2)]
    adjacency = call(
        last_build_kernel,
        shape((group, columns), BF16),
        [HBM] * 3 + [VMEM] * 3,
        (*scalars, late_src, late_dst, acc),
        [pltpu.VMEM(acc_shape, F32)] + buffers + [pltpu.SemaphoreType.DMA((3,))],
    )
    adjacency, near, pieces = lax.optimization_barrier((adjacency, near, pieces))
    keep, send = call(
        gather_kernel,
        (shape((half + PAD, width), F32), shape((half + PAD, width), BF16)),
        [VMEM] * (1 + len(pieces)),
        (adjacency, *pieces),
    )
    pair_sum = call(
        pair_kernel,
        shape((half + PAD, width), BF16),
        [VMEM] * 2,
        (keep, swap(send, "rep", 1)),
    )
    out, self_term, keep, send = call(
        node_kernel,
        (
            shape((rows, width), BF16),
            shape((rows, width), F32),
            shape((middle + PAD, width), F32),
            shape((half + middle + PAD, width), BF16),
        ),
        [VMEM] * 9,
        (
            pair_sum,
            swap(pair_sum, "rep", 2),
            features,
            near[0],
            d_out,
            near[1],
            w_self,
            w_neigh,
            bias[None, :],
        ),
    )
    back = swap(send, "rep", 1)
    terms_shape = shape((middle + PAD, width), BF16)
    terms = call(core_terms_kernel, terms_shape, [VMEM] * 2, (keep, back))
    terms, back = lax.optimization_barrier((terms, back))
    keep_blocks, *near_msgs = call(
        spread_kernel,
        (shape((far * BLK, width), F32),) + (shape((far * BLK, width), BF16),) * 3,
        [VMEM] * 3,
        (adjacency, send, back),
    )
    near_terms = [terms] + [swap(terms, "row", m) for m in range(1, 4)]
    got = [swap(msg, "row", m + 1) for m, msg in enumerate(near_msgs)]
    terms = call(part_terms_kernel, terms_shape, [VMEM] * 4, near_terms)
    far_terms = [terms] + [swap(terms, "row", 4 * h) for h in range(1, far)]
    quarter, bias_term = call(
        all_terms_kernel,
        (shape((middle, width), BF16), shape((1, width), F32)),
        [VMEM] * far,
        far_terms,
    )
    keep_block, *far_msgs, out = call(
        near_sum_kernel,
        (shape((BLK, width), F32),)
        + (shape((BLK, width), BF16),) * (far - 1)
        + (shape((rows, width), BF16),),
        [VMEM] * 5,
        (keep_blocks, *got, out),
    )
    got = [swap(msg, "row", 4 * (h + 1)) for h, msg in enumerate(far_msgs)]
    quarters = [quarter] + [swap(quarter, "rep", m) for m in range(1, 4)]
    d_features, grad_self, grad_neigh, grad_bias = call(
        finish_kernel,
        (shape((rows, width), F32),)
        + (shape((2, middle, width), F32),) * 2
        + (shape((1, width), F32),),
        [VMEM] * (7 + len(got)),
        (self_term, bias_term, *quarters, keep_block, *got),
    )
    grad_self, grad_neigh = (v.reshape(width, width) for v in (grad_self, grad_neigh))
    return (out, d_features, grad_self, grad_neigh, grad_bias[0])


def solution(mesh):
    return jax.shard_map(
        on_device,
        mesh=mesh,
        in_specs=(
            P(("row", "rep"), None),
            P(),
            P(),
            P(),
            P(("row", "rep"), None),
            P(("row", "rep")),
            P(("row", "rep")),
            P(("row", "rep")),
            P(("row", "rep"), None),
            P(("row", "rep"), None),
        ),
        out_specs=(P(("row", "rep"), None), P(("row", "rep"), None), P(), P(), P()),
        check_vma=False,
    )
```

```python
import math

import jax
import jax.numpy as jnp
from jax import lax
from jax.experimental import pallas as pl
from jax.experimental.pallas import tpu as pltpu
from jax.sharding import PartitionSpec as P

BLK = 128
PAD = 16
BF16 = jnp.bfloat16
F32 = jnp.float32
HOT = jnp.float8_e4m3fn
UNROLL = 64
VMEM = pl.BlockSpec(memory_space=pltpu.VMEM)
HBM = pl.BlockSpec(memory_space=pltpu.HBM)


def size_of(value):
    return math.prod(value.shape) * jnp.dtype(value.dtype).itemsize


def row_place(block):
    away = block ^ lax.axis_index("rep")
    return ((away & 1) << 1) | (away >> 1)


def col_place(block, row_count):
    away = block ^ lax.axis_index("row")
    return (away & 3) * (row_count // 4) + (away >> 2)


def tree(values):
    while len(values) > 1:
        values = [values[i] + values[i + 1] for i in range(0, len(values), 2)]
    return values[0]


def split(value):
    high = value.astype(BF16).astype(F32)
    line = lax.broadcasted_iota(jnp.int32, (PAD, value.shape[1]), 0)
    return jnp.where(line == 0, high, jnp.where(line == 1, value - high, 0.0)).astype(BF16)


def joined(rows):
    rows = rows.astype(F32)
    return rows[0:1] + rows[1:2]


def add_tiles(first, scalars, src_ref, dst_ref, acc_ref, ready):
    row_ref, col_ref, count_ref = scalars
    tiles, slots = src_ref.shape
    col_blocks = acc_ref.shape[1]
    line = lax.broadcasted_iota(jnp.int32, (BLK, slots), 0).astype(BF16)
    slot = lax.broadcasted_iota(jnp.int32, (1, slots), 1)
    one, zero = jnp.ones((), BF16), jnp.zeros((), BF16)

    def step(i, carry):
        base = pl.multiple_of(i * UNROLL, UNROLL)
        ready(i, pl.ds(base, UNROLL))
        dst, src = dst_ref[pl.ds(base, UNROLL), :], src_ref[pl.ds(base, UNROLL), :]
        for u in range(UNROLL):
            tile = first + base + u
            live = jnp.where(slot < count_ref[tile], dst[u : u + 1], -1)
            dst_hot = jnp.where(line == live.astype(BF16), one, zero).astype(HOT)
            src_hot = jnp.where(line == src[u : u + 1].astype(BF16), one, zero).astype(HOT)
            part = lax.dot_general(
                dst_hot, src_hot, (((1,), (1,)), ((), ())), preferred_element_type=F32
            )
            acc_ref[row_place(row_ref[tile]), col_place(col_ref[tile], col_blocks)] += part
        return carry

    lax.fori_loop(0, tiles // UNROLL, step, 0)


def first_build_kernel(
    row_ref, col_ref, count_ref, src_ref, dst_ref, features_ref,
    acc_ref, line_ref, late_src_ref, late_dst_ref,
    row_buf, col_buf, count_buf, src_buf, dst_buf, sems, src_sems, dst_sems,
):
    half, rows = src_buf.shape[0], features_ref.shape[0]
    scalars = [row_buf, col_buf, count_buf]
    copies = [
        pltpu.make_async_copy(ref, buf, sems.at[i])
        for i, (ref, buf) in enumerate(zip([row_ref, col_ref, count_ref], scalars))
    ]

    def edges(i, at):
        return (
            pltpu.make_async_copy(src_ref.at[at], src_buf.at[at], src_sems.at[i]),
            pltpu.make_async_copy(dst_ref.at[at], dst_buf.at[at], dst_sems.at[i]),
        )

    late = [
        pltpu.make_async_copy(src_ref.at[pl.ds(half, half)], late_src_ref, sems.at[3]),
        pltpu.make_async_copy(dst_ref.at[pl.ds(half, half)], late_dst_ref, sems.at[4]),
        pltpu.make_async_copy(features_ref, line_ref.at[pl.ds(0, rows)], sems.at[5]),
    ]
    for copy in copies:
        copy.start()
    for i in range(half // UNROLL):
        for copy in edges(i, pl.ds(i * UNROLL, UNROLL)):
            copy.start()
    for copy in late:
        copy.start()
    acc_ref[...] = jnp.zeros_like(acc_ref)
    for copy in copies:
        copy.wait()

    def ready(i, at):
        for copy in edges(i, at):
            copy.wait()

    add_tiles(0, scalars, src_buf, dst_buf, acc_ref, ready)
    for copy in late:
        copy.wait()


def last_build_kernel(
    row_ref, col_ref, count_ref, src_ref, dst_ref, half_ref, adj_ref,
    acc_ref, row_buf, col_buf, count_buf, sems,
):
    scalars = [row_buf, col_buf, count_buf]
    copies = [
        pltpu.make_async_copy(ref, buf, sems.at[i])
        for i, (ref, buf) in enumerate(zip([row_ref, col_ref, count_ref], scalars))
    ]
    for copy in copies:
        copy.start()
    acc_ref[...] = half_ref[...]
    for copy in copies:
        copy.wait()
    add_tiles(src_ref.shape[0], scalars, src_ref, dst_ref, acc_ref, lambda i, at: None)
    row_blocks, col_blocks = acc_ref.shape[:2]
    for g in range(row_blocks):
        for c in range(col_blocks):
            adj_ref[g * BLK : (g + 1) * BLK, c * BLK : (c + 1) * BLK] = acc_ref[g, c].astype(BF16)


def gather_kernel(adj_ref, *refs):
    *feature_refs, keep_ref, send_ref = refs
    half = keep_ref.shape[0] - PAD
    total, at = None, 0
    for ref in feature_refs:
        size = ref.shape[0]
        part = jnp.dot(adj_ref[:, at : at + size], ref[...], preferred_element_type=F32)
        total = part if total is None else total + part
        at += size
    ones = jnp.ones((PAD, adj_ref.shape[1]), BF16)
    degree = lax.dot_general(
        ones, adj_ref[...], (((1,), (1,)), ((), ())), preferred_element_type=F32
    )
    keep_ref[:half] = total[:half]
    keep_ref[half:] = degree[:, :half]
    send_ref[:half] = total[half:].astype(BF16)
    send_ref[half:] = split(degree[:1, half:])


def pair_kernel(keep_ref, got_ref, pair_ref):
    half = keep_ref.shape[0] - PAD
    pair_ref[:half] = (keep_ref[:half] + got_ref[:half].astype(F32)).astype(BF16)
    pair_ref[half:] = split(keep_ref[half : half + 1] + joined(got_ref[half:]))


def node_kernel(
    pair_ref, got_ref, features_ref, near_features_ref, d_out_ref, near_d_out_ref,
    w_self_ref, w_neigh_ref, bias_ref,
    out_ref, self_ref, keep_ref, send_ref,
):
    rows, width = out_ref.shape
    half = 2 * rows
    swapped = jnp.concatenate([got_ref[rows:half], got_ref[:rows]], axis=0).astype(F32)
    sums = pair_ref[:half].astype(F32) + swapped
    far = joined(got_ref[half:])
    degree = joined(pair_ref[half:]) + jnp.concatenate([far[:, rows:], far[:, :rows]], axis=1)
    inverse_row = 1.0 / jnp.maximum(degree, 1.0)
    diagonal = lax.broadcasted_iota(jnp.int32, (half, half), 0) == lax.broadcasted_iota(
        jnp.int32, (half, half), 1
    )
    inverse = jnp.sum(jnp.where(diagonal, inverse_row, 0.0), axis=1, keepdims=True)
    agg = (sums * inverse).astype(BF16)
    features = jnp.concatenate([features_ref[...], near_features_ref[...]], axis=0)
    d_out = jnp.concatenate([d_out_ref[...], near_d_out_ref[...]], axis=0).astype(F32)
    pre = (
        jnp.dot(features, w_self_ref[...], preferred_element_type=F32)
        + jnp.dot(agg, w_neigh_ref[...], preferred_element_type=F32)
        + bias_ref[...]
    )
    square = pre * pre
    bend = jnp.tanh(0.7978845608 * pre * (1.0 + 0.044715 * square))
    out_ref[...] = (0.5 * pre[:rows] * (1.0 + bend[:rows])).astype(BF16)
    slope = 0.5 * (1.0 + bend) + 0.5 * pre * (1.0 - bend * bend) * (
        0.7978845608 * (1.0 + 3.0 * 0.044715 * square)
    )
    d_pre = (d_out * slope).astype(BF16)
    transposed = (((1,), (1,)), ((), ()))
    self_ref[...] = lax.dot_general(
        d_pre[:rows], w_self_ref[...], transposed, preferred_element_type=F32
    )
    back = lax.dot_general(d_pre, w_neigh_ref[...], transposed, preferred_element_type=F32)
    send_ref[:half] = (back * inverse).astype(BF16)
    me = lax.axis_index("rep")
    terms = jnp.where(me >> 1 == 0, features, agg)
    grads = lax.dot_general(terms, d_pre, (((0,), (0,)), ((), ())), preferred_element_type=F32)
    middle = width // 2
    low = me & 1 == 0
    bias_term = jnp.sum(d_pre[:rows].astype(F32), axis=0, keepdims=True) + jnp.sum(
        d_pre[rows:].astype(F32), axis=0, keepdims=True
    )
    keep_ref[:middle] = jnp.where(low, grads[:middle], grads[middle:])
    keep_ref[middle:] = split(bias_term).astype(F32)
    send_ref[half : half + middle] = jnp.where(low, grads[middle:], grads[:middle]).astype(BF16)
    send_ref[half + middle :] = split(bias_term)


def spread_kernel(adj_ref, sent_ref, got_ref, keep_ref, *msg_refs):
    half = adj_ref.shape[0] // 2
    size = adj_ref.shape[1] // 4
    g = jnp.concatenate([sent_ref[:half], got_ref[:half]], axis=0)
    for m, ref in enumerate([keep_ref, *msg_refs]):
        blocks = lax.dot_general(
            adj_ref[:, m * size : (m + 1) * size],
            g,
            (((0,), (0,)), ((), ())),
            preferred_element_type=F32,
        )
        ref[...] = blocks.astype(ref.dtype)


def near_sum_kernel(keep_ref, *refs):
    *sums, out_ref = refs[4:]
    blocks = tree([ref[...].astype(F32) for ref in (keep_ref, *refs[:3])])
    for h, ref in enumerate(sums):
        ref[...] = blocks[h * BLK : (h + 1) * BLK].astype(ref.dtype)
    out_ref[...] = refs[3][...]


def finish_kernel(self_ref, bias_term_ref, *refs):
    *terms, d_features_ref, grad_self_ref, grad_neigh_ref, bias_ref = refs
    quarters, terms = terms[:4], terms[4:]
    d_features_ref[...] = self_ref[...] + tree([ref[...].astype(F32) for ref in terms])
    bias_ref[...] = bias_term_ref[...]
    me = lax.axis_index("rep")
    low = me >> 1 == 0
    for h in range(2):
        same, other = quarters[h][...].astype(F32), quarters[2 + h][...].astype(F32)
        grad_self_ref[(me & 1) ^ h] = jnp.where(low, same, other)
        grad_neigh_ref[(me & 1) ^ h] = jnp.where(low, other, same)


def core_terms_kernel(keep_ref, got_ref, terms_ref):
    middle = keep_ref.shape[0] - PAD
    at = got_ref.shape[0] - PAD
    grads = keep_ref[:middle] + got_ref[at - middle : at].astype(F32)
    terms_ref[:middle] = grads.astype(BF16)
    terms_ref[middle:] = split(joined(keep_ref[middle:]) + joined(got_ref[at:]))


def add_terms(refs):
    middle = refs[0].shape[0] - PAD
    grads = tree([ref[:middle].astype(F32) for ref in refs]).astype(BF16)
    return grads, tree([joined(ref[middle:]) for ref in refs])


def part_terms_kernel(*refs):
    *terms, sum_ref = refs
    middle = sum_ref.shape[0] - PAD
    grads, bias_term = add_terms(terms)
    sum_ref[:middle] = grads
    sum_ref[middle:] = split(bias_term)


def all_terms_kernel(*refs):
    *terms, quarter_ref, bias_ref = refs
    quarter_ref[...], bias_ref[...] = add_terms(terms)


def call(kernel, out_shape, specs, args, scratch=()):
    outs = out_shape if isinstance(out_shape, (list, tuple)) else [out_shape]
    held = sum(size_of(v) for v in [*args, *outs])
    held += sum(math.prod(v.shape) * 4 for v in scratch)
    return pl.pallas_call(
        kernel,
        out_shape=out_shape,
        in_specs=specs,
        out_specs=[VMEM] * len(outs) if outs is out_shape else VMEM,
        scratch_shapes=list(scratch),
        compiler_params=pltpu.CompilerParams(vmem_limit_bytes=2 * held + 4 * 1024 * 1024),
    )(*args)


def on_device(
    features, w_self, w_neigh, bias, d_out, tile_row, tile_col, tile_count, edge_src, edge_dst
):
    rows, width = features.shape
    row_count, rep_count = lax.axis_size("row"), lax.axis_size("rep")
    group, columns = rep_count * rows, row_count * rows
    half, middle = group // 2, width // 2
    far = row_count // 4
    shape = jax.ShapeDtypeStruct

    def swap(value, axis, bits):
        return lax.ppermute(value, axis, [(i, i ^ bits) for i in range(lax.axis_size(axis))])

    far_pieces = [swap(features, "row", 4 * h) for h in range(1, far)]
    tiles, slots = edge_src.shape
    early = tiles // 2
    tile_row, tile_col, tile_count, edge_src, edge_dst, held_features = (
        pltpu.with_memory_space_constraint(v, pltpu.HBM)
        for v in (tile_row, tile_col, tile_count, edge_src, edge_dst, features)
    )
    scalars = (tile_row, tile_col, tile_count)
    buffers = [pltpu.SMEM((tiles,), jnp.int32)] * 3
    acc_shape = (rep_count, row_count, BLK, BLK)
    chunk_sems = [pltpu.SemaphoreType.DMA((early // UNROLL,))] * 2
    acc, line, late_src, late_dst = call(
        first_build_kernel,
        (
            shape(acc_shape, F32),
            shape((far * rows, width), BF16),
            shape((early, slots), jnp.int32),
            shape((early, slots), jnp.int32),
        ),
        [HBM] * 6,
        (*scalars, edge_src, edge_dst, held_features),
        buffers
        + [pltpu.VMEM((early, slots), jnp.int32)] * 2
        + [pltpu.SemaphoreType.DMA((6,))]
        + chunk_sems,
    )
    acc, line, far_pieces = lax.optimization_barrier((acc, line, far_pieces))
    for h, piece in enumerate(far_pieces):
        line = lax.dynamic_update_slice(line, piece, ((h + 1) * rows, 0))
    pieces = [line] + [swap(line, "row", m) for m in range(1, 4)]
    near_features, near_d_out, acc = lax.optimization_barrier((features, d_out, acc))
    near = [swap(near_features, "rep", 2), swap(near_d_out, "rep", 2)]
    adjacency = call(
        last_build_kernel,
        shape((group, columns), BF16),
        [HBM] * 3 + [VMEM] * 3,
        (*scalars, late_src, late_dst, acc),
        [pltpu.VMEM(acc_shape, F32)] + buffers + [pltpu.SemaphoreType.DMA((3,))],
    )
    adjacency, near, pieces = lax.optimization_barrier((adjacency, near, pieces))
    keep, send = call(
        gather_kernel,
        (shape((half + PAD, width), F32), shape((half + PAD, width), BF16)),
        [VMEM] * (1 + len(pieces)),
        (adjacency, *pieces),
    )
    pair_sum = call(
        pair_kernel,
        shape((half + PAD, width), BF16),
        [VMEM] * 2,
        (keep, swap(send, "rep", 1)),
    )
    out, self_term, keep, send = call(
        node_kernel,
        (
            shape((rows, width), BF16),
            shape((rows, width), F32),
            shape((middle + PAD, width), F32),
            shape((half + middle + PAD, width), BF16),
        ),
        [VMEM] * 9,
        (
            pair_sum,
            swap(pair_sum, "rep", 2),
            features,
            near[0],
            d_out,
            near[1],
            w_self,
            w_neigh,
            bias[None, :],
        ),
    )
    back = swap(send, "rep", 1)
    terms_shape = shape((middle + PAD, width), BF16)
    terms = call(core_terms_kernel, terms_shape, [VMEM] * 2, (keep, back))
    terms, back = lax.optimization_barrier((terms, back))
    keep_blocks, *near_msgs = call(
        spread_kernel,
        (shape((far * BLK, width), F32),) + (shape((far * BLK, width), BF16),) * 3,
        [VMEM] * 3,
        (adjacency, send, back),
    )
    near_terms = [terms] + [swap(terms, "row", m) for m in range(1, 4)]
    got = [swap(msg, "row", m + 1) for m, msg in enumerate(near_msgs)][::-1]
    terms = call(part_terms_kernel, terms_shape, [VMEM] * 4, near_terms)
    far_terms = [terms] + [swap(terms, "row", 4 * h) for h in range(1, far)]
    quarter, bias_term = call(
        all_terms_kernel,
        (shape((middle, width), BF16), shape((1, width), F32)),
        [VMEM] * far,
        far_terms,
    )
    keep_block, *far_msgs, out = call(
        near_sum_kernel,
        (shape((BLK, width), F32),)
        + (shape((BLK, width), BF16),) * (far - 1)
        + (shape((rows, width), BF16),),
        [VMEM] * 5,
        (keep_blocks, *got, out),
    )
    got = [swap(msg, "row", 4 * (h + 1)) for h, msg in enumerate(far_msgs)]
    quarters = [quarter] + [swap(quarter, "rep", m) for m in range(1, 4)]
    d_features, grad_self, grad_neigh, grad_bias = call(
        finish_kernel,
        (shape((rows, width), F32),)
        + (shape((2, middle, width), F32),) * 2
        + (shape((1, width), F32),),
        [VMEM] * (7 + len(got)),
        (self_term, bias_term, *quarters, keep_block, *got),
    )
    grad_self, grad_neigh = (v.reshape(width, width) for v in (grad_self, grad_neigh))
    return (out, d_features, grad_self, grad_neigh, grad_bias[0])


def solution(mesh):
    return jax.shard_map(
        on_device,
        mesh=mesh,
        in_specs=(
            P(("row", "rep"), None),
            P(),
            P(),
            P(),
            P(("row", "rep"), None),
            P(("row", "rep")),
            P(("row", "rep")),
            P(("row", "rep")),
            P(("row", "rep"), None),
            P(("row", "rep"), None),
        ),
        out_specs=(P(("row", "rep"), None), P(("row", "rep"), None), P(), P(), P()),
        check_vma=False,
    )
```

```python
import math

import jax
import jax.numpy as jnp
from jax import lax
from jax.experimental import pallas as pl
from jax.experimental.pallas import tpu as pltpu
from jax.sharding import PartitionSpec as P

BLK = 128
PAD = 16
BF16 = jnp.bfloat16
F32 = jnp.float32
HOT = jnp.float8_e4m3fn
VMEM = pl.BlockSpec(memory_space=pltpu.VMEM)
HBM = pl.BlockSpec(memory_space=pltpu.HBM)


def size_of(value):
    return math.prod(value.shape) * jnp.dtype(value.dtype).itemsize


def row_place(block):
    away = block ^ lax.axis_index("rep")
    return ((away & 1) << 1) | (away >> 1)


def col_place(block, row_count):
    away = block ^ lax.axis_index("row")
    return (away & 3) * (row_count // 4) + (away >> 2)


def tree(values):
    while len(values) > 1:
        values = [values[i] + values[i + 1] for i in range(0, len(values), 2)]
    return values[0]


def split(value):
    high = value.astype(BF16).astype(F32)
    line = lax.broadcasted_iota(jnp.int32, (PAD, value.shape[1]), 0)
    return jnp.where(line == 0, high, jnp.where(line == 1, value - high, 0.0)).astype(BF16)


def joined(rows):
    rows = rows.astype(F32)
    return rows[0:1] + rows[1:2]


def add_tiles(first, scalars, src_ref, dst_ref, acc_ref, ready):
    row_ref, col_ref, count_ref = scalars
    tiles, slots = src_ref.shape
    unroll = tiles // 2
    col_blocks = acc_ref.shape[1]
    line = lax.broadcasted_iota(jnp.int32, (BLK, slots), 0).astype(BF16)
    slot = lax.broadcasted_iota(jnp.int32, (1, slots), 1)
    one, zero = jnp.ones((), BF16), jnp.zeros((), BF16)

    def step(i, carry):
        base = pl.multiple_of(i * unroll, unroll)
        ready(i, pl.ds(base, unroll))
        dst, src = dst_ref[pl.ds(base, unroll), :], src_ref[pl.ds(base, unroll), :]
        for u in range(unroll):
            tile = first + base + u
            live = jnp.where(slot < count_ref[tile], dst[u : u + 1], -1)
            dst_hot = jnp.where(line == live.astype(BF16), one, zero).astype(HOT)
            src_hot = jnp.where(line == src[u : u + 1].astype(BF16), one, zero).astype(HOT)
            part = lax.dot_general(
                dst_hot, src_hot, (((1,), (1,)), ((), ())), preferred_element_type=F32
            )
            acc_ref[row_place(row_ref[tile]), col_place(col_ref[tile], col_blocks)] += part
        return carry

    lax.fori_loop(0, tiles // unroll, step, 0)


def first_build_kernel(
    row_ref, col_ref, count_ref, src_ref, dst_ref, features_ref,
    acc_ref, line_ref, late_src_ref, late_dst_ref,
    row_buf, col_buf, count_buf, src_buf, dst_buf, sems, src_sems, dst_sems,
):
    early, late_tiles = src_buf.shape[0], late_src_ref.shape[0]
    rows = features_ref.shape[0]
    unroll = early // 2
    scalars = [row_buf, col_buf, count_buf]
    copies = [
        pltpu.make_async_copy(ref, buf, sems.at[i])
        for i, (ref, buf) in enumerate(zip([row_ref, col_ref, count_ref], scalars))
    ]

    def edges(i, at):
        return (
            pltpu.make_async_copy(src_ref.at[at], src_buf.at[at], src_sems.at[i]),
            pltpu.make_async_copy(dst_ref.at[at], dst_buf.at[at], dst_sems.at[i]),
        )

    late = [
        pltpu.make_async_copy(src_ref.at[pl.ds(early, late_tiles)], late_src_ref, sems.at[3]),
        pltpu.make_async_copy(dst_ref.at[pl.ds(early, late_tiles)], late_dst_ref, sems.at[4]),
        pltpu.make_async_copy(features_ref, line_ref.at[pl.ds(0, rows)], sems.at[5]),
    ]
    for copy in copies:
        copy.start()
    for i in range(2):
        for copy in edges(i, pl.ds(i * unroll, unroll)):
            copy.start()
    for copy in late:
        copy.start()
    acc_ref[...] = jnp.zeros_like(acc_ref)
    for copy in copies:
        copy.wait()

    def ready(i, at):
        for copy in edges(i, at):
            copy.wait()

    add_tiles(0, scalars, src_buf, dst_buf, acc_ref, ready)
    for copy in late:
        copy.wait()


def last_build_kernel(
    row_ref, col_ref, count_ref, src_ref, dst_ref, half_ref, adj_ref,
    acc_ref, row_buf, col_buf, count_buf, sems,
):
    scalars = [row_buf, col_buf, count_buf]
    copies = [
        pltpu.make_async_copy(ref, buf, sems.at[i])
        for i, (ref, buf) in enumerate(zip([row_ref, col_ref, count_ref], scalars))
    ]
    for copy in copies:
        copy.start()
    acc_ref[...] = half_ref[...]
    for copy in copies:
        copy.wait()
    first = row_ref.shape[0] - src_ref.shape[0]
    add_tiles(first, scalars, src_ref, dst_ref, acc_ref, lambda i, at: None)
    row_blocks, col_blocks = acc_ref.shape[:2]
    for g in range(row_blocks):
        for c in range(col_blocks):
            adj_ref[g * BLK : (g + 1) * BLK, c * BLK : (c + 1) * BLK] = acc_ref[g, c].astype(BF16)


def gather_kernel(adj_ref, *refs):
    *feature_refs, keep_ref, send_ref = refs
    half = keep_ref.shape[0] - PAD
    total, at = None, 0
    for ref in feature_refs:
        size = ref.shape[0]
        part = jnp.dot(adj_ref[:, at : at + size], ref[...], preferred_element_type=F32)
        total = part if total is None else total + part
        at += size
    ones = jnp.ones((PAD, adj_ref.shape[1]), BF16)
    degree = lax.dot_general(
        ones, adj_ref[...], (((1,), (1,)), ((), ())), preferred_element_type=F32
    )
    keep_ref[:half] = total[:half]
    keep_ref[half:] = degree[:, :half]
    send_ref[:half] = total[half:].astype(BF16)
    send_ref[half:] = split(degree[:1, half:])


def pair_kernel(keep_ref, got_ref, pair_ref):
    half = keep_ref.shape[0] - PAD
    pair_ref[:half] = (keep_ref[:half] + got_ref[:half].astype(F32)).astype(BF16)
    pair_ref[half:] = split(keep_ref[half : half + 1] + joined(got_ref[half:]))


def node_kernel(
    pair_ref, got_ref, features_ref, near_features_ref, d_out_ref, near_d_out_ref,
    w_self_ref, w_neigh_ref, bias_ref,
    out_ref, self_ref, keep_ref, send_ref,
):
    rows, width = out_ref.shape
    half = 2 * rows
    swapped = jnp.concatenate([got_ref[rows:half], got_ref[:rows]], axis=0).astype(F32)
    sums = pair_ref[:half].astype(F32) + swapped
    far = joined(got_ref[half:])
    degree = joined(pair_ref[half:]) + jnp.concatenate([far[:, rows:], far[:, :rows]], axis=1)
    inverse_row = 1.0 / jnp.maximum(degree, 1.0)
    diagonal = lax.broadcasted_iota(jnp.int32, (half, half), 0) == lax.broadcasted_iota(
        jnp.int32, (half, half), 1
    )
    inverse = jnp.sum(jnp.where(diagonal, inverse_row, 0.0), axis=1, keepdims=True)
    agg = (sums * inverse).astype(BF16)
    features = jnp.concatenate([features_ref[...], near_features_ref[...]], axis=0)
    d_out = jnp.concatenate([d_out_ref[...], near_d_out_ref[...]], axis=0).astype(F32)
    pre = (
        jnp.dot(features, w_self_ref[...], preferred_element_type=F32)
        + jnp.dot(agg, w_neigh_ref[...], preferred_element_type=F32)
        + bias_ref[...]
    )
    square = pre * pre
    bend = jnp.tanh(0.7978845608 * pre * (1.0 + 0.044715 * square))
    out_ref[...] = (0.5 * pre[:rows] * (1.0 + bend[:rows])).astype(BF16)
    slope = 0.5 * (1.0 + bend) + 0.5 * pre * (1.0 - bend * bend) * (
        0.7978845608 * (1.0 + 3.0 * 0.044715 * square)
    )
    d_pre = (d_out * slope).astype(BF16)
    transposed = (((1,), (1,)), ((), ()))
    self_ref[...] = lax.dot_general(
        d_pre[:rows], w_self_ref[...], transposed, preferred_element_type=F32
    )
    back = lax.dot_general(d_pre, w_neigh_ref[...], transposed, preferred_element_type=F32)
    send_ref[:half] = (back * inverse).astype(BF16)
    me = lax.axis_index("rep")
    terms = jnp.where(me >> 1 == 0, features, agg)
    grads = lax.dot_general(terms, d_pre, (((0,), (0,)), ((), ())), preferred_element_type=F32)
    middle = width // 2
    low = me & 1 == 0
    bias_term = jnp.sum(d_pre[:rows].astype(F32), axis=0, keepdims=True) + jnp.sum(
        d_pre[rows:].astype(F32), axis=0, keepdims=True
    )
    keep_ref[:middle] = jnp.where(low, grads[:middle], grads[middle:])
    keep_ref[middle:] = split(bias_term).astype(F32)
    send_ref[half : half + middle] = jnp.where(low, grads[middle:], grads[:middle]).astype(BF16)
    send_ref[half + middle :] = split(bias_term)


def spread_kernel(adj_ref, sent_ref, got_ref, keep_ref, *msg_refs):
    half = adj_ref.shape[0] // 2
    size = adj_ref.shape[1] // 4
    g = jnp.concatenate([sent_ref[:half], got_ref[:half]], axis=0)
    for m, ref in enumerate([keep_ref, *msg_refs]):
        blocks = lax.dot_general(
            adj_ref[:, m * size : (m + 1) * size],
            g,
            (((0,), (0,)), ((), ())),
            preferred_element_type=F32,
        )
        ref[...] = blocks.astype(ref.dtype)


def near_sum_kernel(keep_ref, *refs):
    blocks = tree([ref[...].astype(F32) for ref in (keep_ref, *refs[:3])])
    for h, ref in enumerate(refs[3:]):
        ref[...] = blocks[h * BLK : (h + 1) * BLK].astype(ref.dtype)


def finish_kernel(own_out_ref, self_ref, bias_term_ref, *refs):
    *terms, out_ref, d_features_ref, grad_self_ref, grad_neigh_ref, bias_ref = refs
    quarters, terms = terms[:4], terms[4:]
    d_features_ref[...] = self_ref[...] + tree([ref[...].astype(F32) for ref in terms])
    out_ref[...] = own_out_ref[...]
    bias_ref[...] = bias_term_ref[...]
    me = lax.axis_index("rep")
    low = me >> 1 == 0
    for h in range(2):
        same, other = quarters[h][...].astype(F32), quarters[2 + h][...].astype(F32)
        grad_self_ref[(me & 1) ^ h] = jnp.where(low, same, other)
        grad_neigh_ref[(me & 1) ^ h] = jnp.where(low, other, same)


def core_terms_kernel(keep_ref, got_ref, terms_ref):
    middle = keep_ref.shape[0] - PAD
    at = got_ref.shape[0] - PAD
    grads = keep_ref[:middle] + got_ref[at - middle : at].astype(F32)
    terms_ref[:middle] = grads.astype(BF16)
    terms_ref[middle:] = split(joined(keep_ref[middle:]) + joined(got_ref[at:]))


def add_terms(refs):
    middle = refs[0].shape[0] - PAD
    grads = tree([ref[:middle].astype(F32) for ref in refs]).astype(BF16)
    return grads, tree([joined(ref[middle:]) for ref in refs])


def part_terms_kernel(*refs):
    *terms, sum_ref = refs
    middle = sum_ref.shape[0] - PAD
    grads, bias_term = add_terms(terms)
    sum_ref[:middle] = grads
    sum_ref[middle:] = split(bias_term)


def all_terms_kernel(*refs):
    *terms, quarter_ref, bias_ref = refs
    quarter_ref[...], bias_ref[...] = add_terms(terms)


def call(kernel, out_shape, specs, args, scratch=()):
    outs = out_shape if isinstance(out_shape, (list, tuple)) else [out_shape]
    held = sum(size_of(v) for v in [*args, *outs])
    held += sum(math.prod(v.shape) * 4 for v in scratch)
    return pl.pallas_call(
        kernel,
        out_shape=out_shape,
        in_specs=specs,
        out_specs=[VMEM] * len(outs) if outs is out_shape else VMEM,
        scratch_shapes=list(scratch),
        compiler_params=pltpu.CompilerParams(vmem_limit_bytes=2 * held + 4 * 1024 * 1024),
    )(*args)


def on_device(
    features, w_self, w_neigh, bias, d_out, tile_row, tile_col, tile_count, edge_src, edge_dst
):
    rows, width = features.shape
    row_count, rep_count = lax.axis_size("row"), lax.axis_size("rep")
    group, columns = rep_count * rows, row_count * rows
    half, middle = group // 2, width // 2
    far = row_count // 4
    shape = jax.ShapeDtypeStruct

    def swap(value, axis, bits):
        return lax.ppermute(value, axis, [(i, i ^ bits) for i in range(lax.axis_size(axis))])

    far_pieces = [swap(features, "row", 4 * h) for h in range(1, far)]
    tiles, slots = edge_src.shape
    early = tiles * 7 // 16
    late = tiles - early
    tile_row, tile_col, tile_count, edge_src, edge_dst, held_features = (
        pltpu.with_memory_space_constraint(v, pltpu.HBM)
        for v in (tile_row, tile_col, tile_count, edge_src, edge_dst, features)
    )
    scalars = (tile_row, tile_col, tile_count)
    buffers = [pltpu.SMEM((tiles,), jnp.int32)] * 3
    acc_shape = (rep_count, row_count, BLK, BLK)
    chunk_sems = [pltpu.SemaphoreType.DMA((2,))] * 2
    acc, line, late_src, late_dst = call(
        first_build_kernel,
        (
            shape(acc_shape, F32),
            shape((far * rows, width), BF16),
            shape((late, slots), jnp.int32),
            shape((late, slots), jnp.int32),
        ),
        [HBM] * 6,
        (*scalars, edge_src, edge_dst, held_features),
        buffers
        + [pltpu.VMEM((early, slots), jnp.int32)] * 2
        + [pltpu.SemaphoreType.DMA((6,))]
        + chunk_sems,
    )
    acc, line, far_pieces = lax.optimization_barrier((acc, line, far_pieces))
    for h, piece in enumerate(far_pieces):
        line = lax.dynamic_update_slice(line, piece, ((h + 1) * rows, 0))
    pieces = [line] + [swap(line, "row", m) for m in range(1, 4)]
    near_features, near_d_out, acc = lax.optimization_barrier((features, d_out, acc))
    near = [swap(near_features, "rep", 2), swap(near_d_out, "rep", 2)]
    adjacency = call(
        last_build_kernel,
        shape((group, columns), BF16),
        [HBM] * 3 + [VMEM] * 3,
        (*scalars, late_src, late_dst, acc),
        [pltpu.VMEM(acc_shape, F32)] + buffers + [pltpu.SemaphoreType.DMA((3,))],
    )
    adjacency, near, pieces = lax.optimization_barrier((adjacency, near, pieces))
    keep, send = call(
        gather_kernel,
        (shape((half + PAD, width), F32), shape((half + PAD, width), BF16)),
        [VMEM] * (1 + len(pieces)),
        (adjacency, *pieces),
    )
    pair_sum = call(
        pair_kernel,
        shape((half + PAD, width), BF16),
        [VMEM] * 2,
        (keep, swap(send, "rep", 1)),
    )
    out, self_term, keep, send = call(
        node_kernel,
        (
            shape((rows, width), BF16),
            shape((rows, width), F32),
            shape((middle + PAD, width), F32),
            shape((half + middle + PAD, width), BF16),
        ),
        [VMEM] * 9,
        (
            pair_sum,
            swap(pair_sum, "rep", 2),
            features,
            near[0],
            d_out,
            near[1],
            w_self,
            w_neigh,
            bias[None, :],
        ),
    )
    back = swap(send, "rep", 1)
    terms_shape = shape((middle + PAD, width), BF16)
    terms = call(core_terms_kernel, terms_shape, [VMEM] * 2, (keep, back))
    terms, back = lax.optimization_barrier((terms, back))
    keep_blocks, *near_msgs = call(
        spread_kernel,
        (shape((far * BLK, width), F32),) + (shape((far * BLK, width), BF16),) * 3,
        [VMEM] * 3,
        (adjacency, send, back),
    )
    near_terms = [terms] + [swap(terms, "row", m) for m in range(1, 4)]
    got = [swap(msg, "row", m + 1) for m, msg in enumerate(near_msgs)][::-1]
    terms = call(part_terms_kernel, terms_shape, [VMEM] * 4, near_terms)
    far_terms = [terms] + [swap(terms, "row", 4 * h) for h in range(1, far)]
    quarter, bias_term = call(
        all_terms_kernel,
        (shape((middle, width), BF16), shape((1, width), F32)),
        [VMEM] * far,
        far_terms,
    )
    keep_block, *far_msgs = call(
        near_sum_kernel,
        (shape((BLK, width), F32),) + (shape((BLK, width), BF16),) * (far - 1),
        [VMEM] * 4,
        (keep_blocks, *got),
    )
    got = [swap(msg, "row", 4 * (h + 1)) for h, msg in enumerate(far_msgs)]
    quarters = [quarter] + [swap(quarter, "rep", m) for m in range(1, 4)]
    out, d_features, grad_self, grad_neigh, grad_bias = call(
        finish_kernel,
        (shape((rows, width), BF16), shape((rows, width), F32))
        + (shape((2, middle, width), F32),) * 2
        + (shape((1, width), F32),),
        [VMEM] * (8 + len(got)),
        (out, self_term, bias_term, *quarters, keep_block, *got),
    )
    grad_self, grad_neigh = (v.reshape(width, width) for v in (grad_self, grad_neigh))
    return (out, d_features, grad_self, grad_neigh, grad_bias[0])


def solution(mesh):
    return jax.shard_map(
        on_device,
        mesh=mesh,
        in_specs=(
            P(("row", "rep"), None),
            P(),
            P(),
            P(),
            P(("row", "rep"), None),
            P(("row", "rep")),
            P(("row", "rep")),
            P(("row", "rep")),
            P(("row", "rep"), None),
            P(("row", "rep"), None),
        ),
        out_specs=(P(("row", "rep"), None), P(("row", "rep"), None), P(), P(), P()),
        check_vma=False,
    )
```

```python
import functools
import math

import jax
import jax.numpy as jnp
from jax import lax
from jax.experimental import pallas as pl
from jax.experimental.pallas import tpu as pltpu
from jax.sharding import PartitionSpec as P

BLK = 128
PAD = 16
BF16 = jnp.bfloat16
F32 = jnp.float32
HOT = jnp.float8_e4m3fn
VMEM = pl.BlockSpec(memory_space=pltpu.VMEM)
HBM = pl.BlockSpec(memory_space=pltpu.HBM)


def size_of(value):
    return math.prod(value.shape) * jnp.dtype(value.dtype).itemsize


def row_place(block):
    away = block ^ lax.axis_index("rep")
    return ((away & 1) << 1) | (away >> 1)


def col_place(block, row_count):
    away = block ^ lax.axis_index("row")
    return (away & 3) * (row_count // 4) + (away >> 2)


def tree(values):
    while len(values) > 1:
        values = [values[i] + values[i + 1] for i in range(0, len(values), 2)]
    return values[0]


def split(value):
    high = value.astype(BF16).astype(F32)
    line = lax.broadcasted_iota(jnp.int32, (PAD, value.shape[1]), 0)
    return jnp.where(line == 0, high, jnp.where(line == 1, value - high, 0.0)).astype(BF16)


def joined(rows):
    rows = rows.astype(F32)
    return rows[0:1] + rows[1:2]


def add_tiles(first, scalars, src_ref, dst_ref, acc_ref, ready):
    row_ref, col_ref, count_ref = scalars
    tiles, slots = src_ref.shape
    unroll = tiles // 2
    col_blocks = acc_ref.shape[1]
    line = lax.broadcasted_iota(jnp.int32, (BLK, slots), 0).astype(BF16)
    slot = lax.broadcasted_iota(jnp.int32, (1, slots), 1)
    one, zero = jnp.ones((), BF16), jnp.zeros((), BF16)

    def step(i, carry):
        base = pl.multiple_of(i * unroll, unroll)
        ready(i, pl.ds(base, unroll))
        dst, src = dst_ref[pl.ds(base, unroll), :], src_ref[pl.ds(base, unroll), :]
        for u in range(unroll):
            tile = first + base + u
            live = jnp.where(slot < count_ref[tile], dst[u : u + 1], -1)
            dst_hot = jnp.where(line == live.astype(BF16), one, zero).astype(HOT)
            src_hot = jnp.where(line == src[u : u + 1].astype(BF16), one, zero).astype(HOT)
            part = lax.dot_general(
                dst_hot, src_hot, (((1,), (1,)), ((), ())), preferred_element_type=F32
            )
            acc_ref[row_place(row_ref[tile]), col_place(col_ref[tile], col_blocks)] += part
        return carry

    lax.fori_loop(0, tiles // unroll, step, 0)


def first_build_kernel(
    row_ref, col_ref, count_ref, src_ref, dst_ref, features_ref,
    acc_ref, line_ref, late_src_ref, late_dst_ref,
    row_buf, col_buf, count_buf, src_buf, dst_buf, sems, src_sems, dst_sems,
):
    early, late_tiles = src_buf.shape[0], late_src_ref.shape[0]
    rows = features_ref.shape[0]
    unroll = early // 2
    scalars = [row_buf, col_buf, count_buf]
    copies = [
        pltpu.make_async_copy(ref, buf, sems.at[i])
        for i, (ref, buf) in enumerate(zip([row_ref, col_ref, count_ref], scalars))
    ]

    def edges(i, at):
        return (
            pltpu.make_async_copy(src_ref.at[at], src_buf.at[at], src_sems.at[i]),
            pltpu.make_async_copy(dst_ref.at[at], dst_buf.at[at], dst_sems.at[i]),
        )

    late = [
        pltpu.make_async_copy(src_ref.at[pl.ds(early, late_tiles)], late_src_ref, sems.at[3]),
        pltpu.make_async_copy(dst_ref.at[pl.ds(early, late_tiles)], late_dst_ref, sems.at[4]),
        pltpu.make_async_copy(features_ref, line_ref.at[pl.ds(0, rows)], sems.at[5]),
    ]
    for copy in copies:
        copy.start()
    for i in range(2):
        for copy in edges(i, pl.ds(i * unroll, unroll)):
            copy.start()
    for copy in late:
        copy.start()
    acc_ref[...] = jnp.zeros_like(acc_ref)
    for copy in copies:
        copy.wait()

    def ready(i, at):
        for copy in edges(i, at):
            copy.wait()

    add_tiles(0, scalars, src_buf, dst_buf, acc_ref, ready)
    for copy in late:
        copy.wait()


def last_build_kernel(
    row_ref, col_ref, count_ref, src_ref, dst_ref, half_ref, adj_ref,
    acc_ref, row_buf, col_buf, count_buf, sems,
):
    scalars = [row_buf, col_buf, count_buf]
    copies = [
        pltpu.make_async_copy(ref, buf, sems.at[i])
        for i, (ref, buf) in enumerate(zip([row_ref, col_ref, count_ref], scalars))
    ]
    for copy in copies:
        copy.start()
    acc_ref[...] = half_ref[...]
    for copy in copies:
        copy.wait()
    first = row_ref.shape[0] - src_ref.shape[0]
    add_tiles(first, scalars, src_ref, dst_ref, acc_ref, lambda i, at: None)
    row_blocks, col_blocks = acc_ref.shape[:2]
    for g in range(row_blocks):
        for c in range(col_blocks):
            adj_ref[g * BLK : (g + 1) * BLK, c * BLK : (c + 1) * BLK] = acc_ref[g, c].astype(BF16)


def gather_kernel(keep, adj_ref, *refs):
    *feature_refs, sum_ref = refs
    half = sum_ref.shape[0] - PAD
    rows = slice(0, half) if keep else slice(half, 2 * half)
    total, at = None, 0
    for ref in feature_refs:
        size = ref.shape[0]
        part = jnp.dot(adj_ref[rows, at : at + size], ref[...], preferred_element_type=F32)
        total = part if total is None else total + part
        at += size
    ones = jnp.ones((PAD, adj_ref.shape[1]), BF16)
    degree = lax.dot_general(
        ones, adj_ref[rows, :], (((1,), (1,)), ((), ())), preferred_element_type=F32
    )
    sum_ref[:half] = total.astype(sum_ref.dtype)
    sum_ref[half:] = degree if keep else split(degree[:1])


def pair_kernel(keep_ref, got_ref, pair_ref):
    half = keep_ref.shape[0] - PAD
    pair_ref[:half] = (keep_ref[:half] + got_ref[:half].astype(F32)).astype(BF16)
    pair_ref[half:] = split(keep_ref[half : half + 1] + joined(got_ref[half:]))


def node_kernel(
    pair_ref, got_ref, features_ref, near_features_ref, d_out_ref, near_d_out_ref,
    w_self_ref, w_neigh_ref, bias_ref,
    out_ref, self_ref, keep_ref, send_ref,
):
    rows, width = out_ref.shape
    half = 2 * rows
    swapped = jnp.concatenate([got_ref[rows:half], got_ref[:rows]], axis=0).astype(F32)
    sums = pair_ref[:half].astype(F32) + swapped
    far = joined(got_ref[half:])
    degree = joined(pair_ref[half:]) + jnp.concatenate([far[:, rows:], far[:, :rows]], axis=1)
    inverse_row = 1.0 / jnp.maximum(degree, 1.0)
    diagonal = lax.broadcasted_iota(jnp.int32, (half, half), 0) == lax.broadcasted_iota(
        jnp.int32, (half, half), 1
    )
    inverse = jnp.sum(jnp.where(diagonal, inverse_row, 0.0), axis=1, keepdims=True)
    agg = (sums * inverse).astype(BF16)
    features = jnp.concatenate([features_ref[...], near_features_ref[...]], axis=0)
    d_out = jnp.concatenate([d_out_ref[...], near_d_out_ref[...]], axis=0).astype(F32)
    pre = (
        jnp.dot(features, w_self_ref[...], preferred_element_type=F32)
        + jnp.dot(agg, w_neigh_ref[...], preferred_element_type=F32)
        + bias_ref[...]
    )
    square = pre * pre
    bend = jnp.tanh(0.7978845608 * pre * (1.0 + 0.044715 * square))
    out_ref[...] = (0.5 * pre[:rows] * (1.0 + bend[:rows])).astype(BF16)
    slope = 0.5 * (1.0 + bend) + 0.5 * pre * (1.0 - bend * bend) * (
        0.7978845608 * (1.0 + 3.0 * 0.044715 * square)
    )
    d_pre = (d_out * slope).astype(BF16)
    transposed = (((1,), (1,)), ((), ()))
    self_ref[...] = lax.dot_general(
        d_pre[:rows], w_self_ref[...], transposed, preferred_element_type=F32
    )
    back = lax.dot_general(d_pre, w_neigh_ref[...], transposed, preferred_element_type=F32)
    send_ref[:half] = (back * inverse).astype(BF16)
    me = lax.axis_index("rep")
    terms = jnp.where(me >> 1 == 0, features, agg)
    grads = lax.dot_general(terms, d_pre, (((0,), (0,)), ((), ())), preferred_element_type=F32)
    middle = width // 2
    low = me & 1 == 0
    bias_term = jnp.sum(d_pre[:rows].astype(F32), axis=0, keepdims=True) + jnp.sum(
        d_pre[rows:].astype(F32), axis=0, keepdims=True
    )
    keep_ref[:middle] = jnp.where(low, grads[:middle], grads[middle:])
    keep_ref[middle:] = split(bias_term).astype(F32)
    send_ref[half : half + middle] = jnp.where(low, grads[middle:], grads[:middle]).astype(BF16)
    send_ref[half + middle :] = split(bias_term)


def spread_kernel(adj_ref, sent_ref, got_ref, keep_ref, *msg_refs):
    half = adj_ref.shape[0] // 2
    size = adj_ref.shape[1] // 4
    g = jnp.concatenate([sent_ref[:half], got_ref[:half]], axis=0)
    for m, ref in enumerate([keep_ref, *msg_refs]):
        blocks = lax.dot_general(
            adj_ref[:, m * size : (m + 1) * size],
            g,
            (((0,), (0,)), ((), ())),
            preferred_element_type=F32,
        )
        ref[...] = blocks.astype(ref.dtype)


def near_sum_kernel(keep_ref, *refs):
    blocks = tree([ref[...].astype(F32) for ref in (keep_ref, *refs[:3])])
    for h, ref in enumerate(refs[3:]):
        ref[...] = blocks[h * BLK : (h + 1) * BLK].astype(ref.dtype)


def finish_kernel(own_out_ref, self_ref, bias_term_ref, *refs):
    *terms, out_ref, d_features_ref, bias_ref = refs
    d_features_ref[...] = self_ref[...] + tree([ref[...].astype(F32) for ref in terms])
    out_ref[...] = own_out_ref[...]
    bias_ref[...] = bias_term_ref[...]


def grads_kernel(*refs):
    *quarters, grad_self_ref, grad_neigh_ref = refs
    me = lax.axis_index("rep")
    low = me >> 1 == 0
    for h in range(2):
        same, other = quarters[h][...].astype(F32), quarters[2 + h][...].astype(F32)
        grad_self_ref[(me & 1) ^ h] = jnp.where(low, same, other)
        grad_neigh_ref[(me & 1) ^ h] = jnp.where(low, other, same)


def core_terms_kernel(keep_ref, got_ref, terms_ref):
    middle = keep_ref.shape[0] - PAD
    at = got_ref.shape[0] - PAD
    grads = keep_ref[:middle] + got_ref[at - middle : at].astype(F32)
    terms_ref[:middle] = grads.astype(BF16)
    terms_ref[middle:] = split(joined(keep_ref[middle:]) + joined(got_ref[at:]))


def add_terms(refs):
    middle = refs[0].shape[0] - PAD
    grads = tree([ref[:middle].astype(F32) for ref in refs]).astype(BF16)
    return grads, tree([joined(ref[middle:]) for ref in refs])


def part_terms_kernel(*refs):
    *terms, sum_ref = refs
    middle = sum_ref.shape[0] - PAD
    grads, bias_term = add_terms(terms)
    sum_ref[:middle] = grads
    sum_ref[middle:] = split(bias_term)


def all_terms_kernel(*refs):
    *terms, quarter_ref, bias_ref = refs
    quarter_ref[...], bias_ref[...] = add_terms(terms)


def call(kernel, out_shape, specs, args, scratch=()):
    outs = out_shape if isinstance(out_shape, (list, tuple)) else [out_shape]
    held = sum(size_of(v) for v in [*args, *outs])
    held += sum(math.prod(v.shape) * 4 for v in scratch)
    return pl.pallas_call(
        kernel,
        out_shape=out_shape,
        in_specs=specs,
        out_specs=[VMEM] * len(outs) if outs is out_shape else VMEM,
        scratch_shapes=list(scratch),
        compiler_params=pltpu.CompilerParams(vmem_limit_bytes=2 * held + 4 * 1024 * 1024),
    )(*args)


def on_device(
    features, w_self, w_neigh, bias, d_out, tile_row, tile_col, tile_count, edge_src, edge_dst
):
    rows, width = features.shape
    row_count, rep_count = lax.axis_size("row"), lax.axis_size("rep")
    group, columns = rep_count * rows, row_count * rows
    half, middle = group // 2, width // 2
    far = row_count // 4
    shape = jax.ShapeDtypeStruct

    def swap(value, axis, bits):
        return lax.ppermute(value, axis, [(i, i ^ bits) for i in range(lax.axis_size(axis))])

    far_pieces = [swap(features, "row", 4 * h) for h in range(1, far)]
    tiles, slots = edge_src.shape
    early = tiles * 7 // 16
    late = tiles - early
    tile_row, tile_col, tile_count, edge_src, edge_dst, held_features = (
        pltpu.with_memory_space_constraint(v, pltpu.HBM)
        for v in (tile_row, tile_col, tile_count, edge_src, edge_dst, features)
    )
    scalars = (tile_row, tile_col, tile_count)
    buffers = [pltpu.SMEM((tiles,), jnp.int32)] * 3
    acc_shape = (rep_count, row_count, BLK, BLK)
    chunk_sems = [pltpu.SemaphoreType.DMA((2,))] * 2
    acc, line, late_src, late_dst = call(
        first_build_kernel,
        (
            shape(acc_shape, F32),
            shape((far * rows, width), BF16),
            shape((late, slots), jnp.int32),
            shape((late, slots), jnp.int32),
        ),
        [HBM] * 6,
        (*scalars, edge_src, edge_dst, held_features),
        buffers
        + [pltpu.VMEM((early, slots), jnp.int32)] * 2
        + [pltpu.SemaphoreType.DMA((6,))]
        + chunk_sems,
    )
    acc, line, far_pieces = lax.optimization_barrier((acc, line, far_pieces))
    for h, piece in enumerate(far_pieces):
        line = lax.dynamic_update_slice(line, piece, ((h + 1) * rows, 0))
    pieces = [line] + [swap(line, "row", m) for m in range(1, 4)]
    near_features, near_d_out, acc = lax.optimization_barrier((features, d_out, acc))
    near = [swap(near_features, "rep", 2), swap(near_d_out, "rep", 2)]
    adjacency = call(
        last_build_kernel,
        shape((group, columns), BF16),
        [HBM] * 3 + [VMEM] * 3,
        (*scalars, late_src, late_dst, acc),
        [pltpu.VMEM(acc_shape, F32)] + buffers + [pltpu.SemaphoreType.DMA((3,))],
    )
    adjacency, near, pieces = lax.optimization_barrier((adjacency, near, pieces))
    send, keep = (
        call(
            functools.partial(gather_kernel, stays),
            shape((half + PAD, width), F32 if stays else BF16),
            [VMEM] * (1 + len(pieces)),
            (adjacency, *pieces),
        )
        for stays in (False, True)
    )
    pair_sum = call(
        pair_kernel,
        shape((half + PAD, width), BF16),
        [VMEM] * 2,
        (keep, swap(send, "rep", 1)),
    )
    out, self_term, keep, send = call(
        node_kernel,
        (
            shape((rows, width), BF16),
            shape((rows, width), F32),
            shape((middle + PAD, width), F32),
            shape((half + middle + PAD, width), BF16),
        ),
        [VMEM] * 9,
        (
            pair_sum,
            swap(pair_sum, "rep", 2),
            features,
            near[0],
            d_out,
            near[1],
            w_self,
            w_neigh,
            bias[None, :],
        ),
    )
    back = swap(send, "rep", 1)
    terms_shape = shape((middle + PAD, width), BF16)
    terms = call(core_terms_kernel, terms_shape, [VMEM] * 2, (keep, back))
    terms, back = lax.optimization_barrier((terms, back))
    keep_blocks, *near_msgs = call(
        spread_kernel,
        (shape((far * BLK, width), F32),) + (shape((far * BLK, width), BF16),) * 3,
        [VMEM] * 3,
        (adjacency, send, back),
    )
    near_terms = [terms] + [swap(terms, "row", m) for m in range(1, 4)]
    got = [swap(msg, "row", m + 1) for m, msg in enumerate(near_msgs)][::-1]
    terms = call(part_terms_kernel, terms_shape, [VMEM] * 4, near_terms)
    far_terms = [terms] + [swap(terms, "row", 4 * h) for h in range(1, far)]
    quarter, bias_term = call(
        all_terms_kernel,
        (shape((middle, width), BF16), shape((1, width), F32)),
        [VMEM] * far,
        far_terms,
    )
    keep_block, *far_msgs = call(
        near_sum_kernel,
        (shape((BLK, width), F32),) + (shape((BLK, width), BF16),) * (far - 1),
        [VMEM] * 4,
        (keep_blocks, *got),
    )
    got = [swap(msg, "row", 4 * (h + 1)) for h, msg in enumerate(far_msgs)]
    quarters = [quarter] + [swap(quarter, "rep", m) for m in range(1, 4)]
    out, d_features, grad_bias = call(
        finish_kernel,
        (shape((rows, width), BF16), shape((rows, width), F32), shape((1, width), F32)),
        [VMEM] * (4 + len(got)),
        (out, self_term, bias_term, keep_block, *got),
    )
    grad_self, grad_neigh = call(
        grads_kernel, (shape((2, middle, width), F32),) * 2, [VMEM] * 4, quarters
    )
    grad_self, grad_neigh = (v.reshape(width, width) for v in (grad_self, grad_neigh))
    return (out, d_features, grad_self, grad_neigh, grad_bias[0])


def solution(mesh):
    return jax.shard_map(
        on_device,
        mesh=mesh,
        in_specs=(
            P(("row", "rep"), None),
            P(),
            P(),
            P(),
            P(("row", "rep"), None),
            P(("row", "rep")),
            P(("row", "rep")),
            P(("row", "rep")),
            P(("row", "rep"), None),
            P(("row", "rep"), None),
        ),
        out_specs=(P(("row", "rep"), None), P(("row", "rep"), None), P(), P(), P()),
        check_vma=False,
    )
```

```python
import functools
import math

import jax
import jax.numpy as jnp
from jax import lax
from jax.experimental import pallas as pl
from jax.experimental.pallas import tpu as pltpu
from jax.sharding import PartitionSpec as P

BLK = 128
PAD = 8
BF16 = jnp.bfloat16
F32 = jnp.float32
HOT = jnp.float8_e4m3fn
VMEM = pl.BlockSpec(memory_space=pltpu.VMEM)
HBM = pl.BlockSpec(memory_space=pltpu.HBM)


def size_of(value):
    return math.prod(value.shape) * jnp.dtype(value.dtype).itemsize


def row_place(block):
    away = block ^ lax.axis_index("rep")
    return ((away & 1) << 1) | (away >> 1)


def col_place(block, row_count):
    away = block ^ lax.axis_index("row")
    return (away & 3) * (row_count // 4) + (away >> 2)


def tree(values):
    while len(values) > 1:
        values = [values[i] + values[i + 1] for i in range(0, len(values), 2)]
    return values[0]


def split(value):
    high = value.astype(BF16).astype(F32)
    line = lax.broadcasted_iota(jnp.int32, (PAD, value.shape[1]), 0)
    return jnp.where(line == 0, high, jnp.where(line == 1, value - high, 0.0)).astype(BF16)


def joined(rows):
    rows = rows.astype(F32)
    return rows[0:1] + rows[1:2]


def add_tiles(first, scalars, src_ref, dst_ref, acc_ref, ready):
    row_ref, col_ref, count_ref = scalars
    tiles, slots = src_ref.shape
    unroll = tiles // 2
    col_blocks = acc_ref.shape[1]
    line = lax.broadcasted_iota(jnp.int32, (BLK, slots), 0).astype(BF16)
    slot = lax.broadcasted_iota(jnp.int32, (1, slots), 1)
    one, zero = jnp.ones((), BF16), jnp.zeros((), BF16)

    def step(i, carry):
        base = pl.multiple_of(i * unroll, unroll)
        ready(i, pl.ds(base, unroll))
        dst, src = dst_ref[pl.ds(base, unroll), :], src_ref[pl.ds(base, unroll), :]
        for u in range(unroll):
            tile = first + base + u
            live = jnp.where(slot < count_ref[tile], dst[u : u + 1], -1)
            dst_hot = jnp.where(line == live.astype(BF16), one, zero).astype(HOT)
            src_hot = jnp.where(line == src[u : u + 1].astype(BF16), one, zero).astype(HOT)
            part = lax.dot_general(
                dst_hot, src_hot, (((1,), (1,)), ((), ())), preferred_element_type=F32
            )
            acc_ref[row_place(row_ref[tile]), col_place(col_ref[tile], col_blocks)] += part
        return carry

    lax.fori_loop(0, tiles // unroll, step, 0)


def first_build_kernel(
    row_ref, col_ref, count_ref, src_ref, dst_ref, features_ref,
    acc_ref, line_ref, late_src_ref, late_dst_ref,
    row_buf, col_buf, count_buf, src_buf, dst_buf, sems, src_sems, dst_sems,
):
    early, late_tiles = src_buf.shape[0], late_src_ref.shape[0]
    rows = features_ref.shape[0]
    unroll = early // 2
    scalars = [row_buf, col_buf, count_buf]
    copies = [
        pltpu.make_async_copy(ref, buf, sems.at[i])
        for i, (ref, buf) in enumerate(zip([row_ref, col_ref, count_ref], scalars))
    ]

    def edges(i, at):
        return (
            pltpu.make_async_copy(src_ref.at[at], src_buf.at[at], src_sems.at[i]),
            pltpu.make_async_copy(dst_ref.at[at], dst_buf.at[at], dst_sems.at[i]),
        )

    late = [
        pltpu.make_async_copy(src_ref.at[pl.ds(early, late_tiles)], late_src_ref, sems.at[3]),
        pltpu.make_async_copy(dst_ref.at[pl.ds(early, late_tiles)], late_dst_ref, sems.at[4]),
        pltpu.make_async_copy(features_ref, line_ref.at[pl.ds(0, rows)], sems.at[5]),
    ]
    for copy in copies:
        copy.start()
    for i in range(2):
        for copy in edges(i, pl.ds(i * unroll, unroll)):
            copy.start()
    for copy in late:
        copy.start()
    acc_ref[...] = jnp.zeros_like(acc_ref)
    for copy in copies:
        copy.wait()

    def ready(i, at):
        for copy in edges(i, at):
            copy.wait()

    add_tiles(0, scalars, src_buf, dst_buf, acc_ref, ready)
    for copy in late:
        copy.wait()


def last_build_kernel(
    row_ref, col_ref, count_ref, src_ref, dst_ref, half_ref, adj_ref,
    acc_ref, row_buf, col_buf, count_buf, sems,
):
    scalars = [row_buf, col_buf, count_buf]
    copies = [
        pltpu.make_async_copy(ref, buf, sems.at[i])
        for i, (ref, buf) in enumerate(zip([row_ref, col_ref, count_ref], scalars))
    ]
    for copy in copies:
        copy.start()
    acc_ref[...] = half_ref[...]
    for copy in copies:
        copy.wait()
    first = row_ref.shape[0] - src_ref.shape[0]
    add_tiles(first, scalars, src_ref, dst_ref, acc_ref, lambda i, at: None)
    row_blocks, col_blocks = acc_ref.shape[:2]
    for g in range(row_blocks):
        for c in range(col_blocks):
            adj_ref[g * BLK : (g + 1) * BLK, c * BLK : (c + 1) * BLK] = acc_ref[g, c].astype(BF16)


def gather_kernel(keep, adj_ref, *refs):
    *feature_refs, sum_ref = refs
    half = sum_ref.shape[0] - PAD
    rows = slice(0, half) if keep else slice(half, 2 * half)
    total, at = None, 0
    for ref in feature_refs:
        size = ref.shape[0]
        part = jnp.dot(adj_ref[rows, at : at + size], ref[...], preferred_element_type=F32)
        total = part if total is None else total + part
        at += size
    ones = jnp.ones((PAD, adj_ref.shape[1]), BF16)
    degree = lax.dot_general(
        ones, adj_ref[rows, :], (((1,), (1,)), ((), ())), preferred_element_type=F32
    )
    sum_ref[:half] = total.astype(sum_ref.dtype)
    sum_ref[half:] = degree if keep else split(degree[:1])


def pair_kernel(keep_ref, got_ref, pair_ref):
    half = keep_ref.shape[0] - PAD
    pair_ref[:half] = (keep_ref[:half] + got_ref[:half].astype(F32)).astype(BF16)
    pair_ref[half:] = split(keep_ref[half : half + 1] + joined(got_ref[half:]))


def node_kernel(
    pair_ref, got_ref, features_ref, near_features_ref, d_out_ref, near_d_out_ref,
    w_self_ref, w_neigh_ref, bias_ref,
    out_ref, self_ref, keep_ref, send_ref,
):
    rows, width = out_ref.shape
    half = 2 * rows
    swapped = jnp.concatenate([got_ref[rows:half], got_ref[:rows]], axis=0).astype(F32)
    sums = pair_ref[:half].astype(F32) + swapped
    far = joined(got_ref[half:])
    degree = joined(pair_ref[half:]) + jnp.concatenate([far[:, rows:], far[:, :rows]], axis=1)
    inverse_row = 1.0 / jnp.maximum(degree, 1.0)
    diagonal = lax.broadcasted_iota(jnp.int32, (half, half), 0) == lax.broadcasted_iota(
        jnp.int32, (half, half), 1
    )
    inverse = jnp.sum(jnp.where(diagonal, inverse_row, 0.0), axis=1, keepdims=True)
    agg = (sums * inverse).astype(BF16)
    features = jnp.concatenate([features_ref[...], near_features_ref[...]], axis=0)
    d_out = jnp.concatenate([d_out_ref[...], near_d_out_ref[...]], axis=0).astype(F32)
    pre = (
        jnp.dot(features, w_self_ref[...], preferred_element_type=F32)
        + jnp.dot(agg, w_neigh_ref[...], preferred_element_type=F32)
        + bias_ref[...]
    )
    square = pre * pre
    bend = jnp.tanh(0.7978845608 * pre * (1.0 + 0.044715 * square))
    out_ref[...] = (0.5 * pre[:rows] * (1.0 + bend[:rows])).astype(BF16)
    slope = 0.5 * (1.0 + bend) + 0.5 * pre * (1.0 - bend * bend) * (
        0.7978845608 * (1.0 + 3.0 * 0.044715 * square)
    )
    d_pre = (d_out * slope).astype(BF16)
    transposed = (((1,), (1,)), ((), ()))
    self_ref[...] = lax.dot_general(
        d_pre[:rows], w_self_ref[...], transposed, preferred_element_type=F32
    )
    back = lax.dot_general(d_pre, w_neigh_ref[...], transposed, preferred_element_type=F32)
    send_ref[:half] = (back * inverse).astype(BF16)
    me = lax.axis_index("rep")
    terms = jnp.where(me >> 1 == 0, features, agg)
    grads = lax.dot_general(terms, d_pre, (((0,), (0,)), ((), ())), preferred_element_type=F32)
    middle = width // 2
    low = me & 1 == 0
    bias_term = jnp.sum(d_pre[:rows].astype(F32), axis=0, keepdims=True) + jnp.sum(
        d_pre[rows:].astype(F32), axis=0, keepdims=True
    )
    keep_ref[:middle] = jnp.where(low, grads[:middle], grads[middle:])
    keep_ref[middle:] = split(bias_term).astype(F32)
    send_ref[half : half + middle] = jnp.where(low, grads[middle:], grads[:middle]).astype(BF16)
    send_ref[half + middle :] = split(bias_term)


def spread_kernel(adj_ref, sent_ref, got_ref, keep_ref, *msg_refs):
    half = adj_ref.shape[0] // 2
    size = adj_ref.shape[1] // 4
    g = jnp.concatenate([sent_ref[:half], got_ref[:half]], axis=0)
    for m, ref in enumerate([keep_ref, *msg_refs]):
        blocks = lax.dot_general(
            adj_ref[:, m * size : (m + 1) * size],
            g,
            (((0,), (0,)), ((), ())),
            preferred_element_type=F32,
        )
        ref[...] = blocks.astype(ref.dtype)


def near_sum_kernel(keep_ref, *refs):
    blocks = tree([ref[...].astype(F32) for ref in (keep_ref, *refs[:3])])
    for h, ref in enumerate(refs[3:]):
        ref[...] = blocks[h * BLK : (h + 1) * BLK].astype(ref.dtype)


def finish_kernel(own_out_ref, self_ref, bias_term_ref, *refs):
    *terms, out_ref, d_features_ref, bias_ref = refs
    d_features_ref[...] = self_ref[...] + tree([ref[...].astype(F32) for ref in terms])
    out_ref[...] = own_out_ref[...]
    bias_ref[...] = bias_term_ref[...]


def grads_kernel(*refs):
    *quarters, grad_self_ref, grad_neigh_ref = refs
    me = lax.axis_index("rep")
    low = me >> 1 == 0
    for h in range(2):
        same, other = quarters[h][...].astype(F32), quarters[2 + h][...].astype(F32)
        grad_self_ref[(me & 1) ^ h] = jnp.where(low, same, other)
        grad_neigh_ref[(me & 1) ^ h] = jnp.where(low, other, same)


def core_terms_kernel(keep_ref, got_ref, terms_ref):
    middle = keep_ref.shape[0] - PAD
    at = got_ref.shape[0] - PAD
    grads = keep_ref[:middle] + got_ref[at - middle : at].astype(F32)
    terms_ref[:middle] = grads.astype(BF16)
    terms_ref[middle:] = split(joined(keep_ref[middle:]) + joined(got_ref[at:]))


def add_terms(refs):
    middle = refs[0].shape[0] - PAD
    grads = tree([ref[:middle].astype(F32) for ref in refs]).astype(BF16)
    return grads, tree([joined(ref[middle:]) for ref in refs])


def part_terms_kernel(*refs):
    *terms, sum_ref = refs
    middle = sum_ref.shape[0] - PAD
    grads, bias_term = add_terms(terms)
    sum_ref[:middle] = grads
    sum_ref[middle:] = split(bias_term)


def all_terms_kernel(*refs):
    *terms, quarter_ref, bias_ref = refs
    quarter_ref[...], bias_ref[...] = add_terms(terms)


def call(kernel, out_shape, specs, args, scratch=()):
    outs = out_shape if isinstance(out_shape, (list, tuple)) else [out_shape]
    held = sum(size_of(v) for v in [*args, *outs])
    held += sum(math.prod(v.shape) * 4 for v in scratch)
    return pl.pallas_call(
        kernel,
        out_shape=out_shape,
        in_specs=specs,
        out_specs=[VMEM] * len(outs) if outs is out_shape else VMEM,
        scratch_shapes=list(scratch),
        compiler_params=pltpu.CompilerParams(vmem_limit_bytes=2 * held + 4 * 1024 * 1024),
    )(*args)


def on_device(
    features, w_self, w_neigh, bias, d_out, tile_row, tile_col, tile_count, edge_src, edge_dst
):
    rows, width = features.shape
    row_count, rep_count = lax.axis_size("row"), lax.axis_size("rep")
    group, columns = rep_count * rows, row_count * rows
    half, middle = group // 2, width // 2
    far = row_count // 4
    shape = jax.ShapeDtypeStruct

    def swap(value, axis, bits):
        return lax.ppermute(value, axis, [(i, i ^ bits) for i in range(lax.axis_size(axis))])

    far_pieces = [swap(features, "row", 4 * h) for h in range(1, far)]
    tiles, slots = edge_src.shape
    early = tiles * 7 // 16
    late = tiles - early
    tile_row, tile_col, tile_count, edge_src, edge_dst, held_features = (
        pltpu.with_memory_space_constraint(v, pltpu.HBM)
        for v in (tile_row, tile_col, tile_count, edge_src, edge_dst, features)
    )
    scalars = (tile_row, tile_col, tile_count)
    buffers = [pltpu.SMEM((tiles,), jnp.int32)] * 3
    acc_shape = (rep_count, row_count, BLK, BLK)
    chunk_sems = [pltpu.SemaphoreType.DMA((2,))] * 2
    acc, line, late_src, late_dst = call(
        first_build_kernel,
        (
            shape(acc_shape, F32),
            shape((far * rows, width), BF16),
            shape((late, slots), jnp.int32),
            shape((late, slots), jnp.int32),
        ),
        [HBM] * 6,
        (*scalars, edge_src, edge_dst, held_features),
        buffers
        + [pltpu.VMEM((early, slots), jnp.int32)] * 2
        + [pltpu.SemaphoreType.DMA((6,))]
        + chunk_sems,
    )
    acc, line, far_pieces = lax.optimization_barrier((acc, line, far_pieces))
    for h, piece in enumerate(far_pieces):
        line = lax.dynamic_update_slice(line, piece, ((h + 1) * rows, 0))
    pieces = [line] + [swap(line, "row", m) for m in range(1, 4)]
    near_features, near_d_out, acc = lax.optimization_barrier((features, d_out, acc))
    near = [swap(near_features, "rep", 2), swap(near_d_out, "rep", 2)]
    adjacency = call(
        last_build_kernel,
        shape((group, columns), BF16),
        [HBM] * 3 + [VMEM] * 3,
        (*scalars, late_src, late_dst, acc),
        [pltpu.VMEM(acc_shape, F32)] + buffers + [pltpu.SemaphoreType.DMA((3,))],
    )
    adjacency, near, pieces = lax.optimization_barrier((adjacency, near, pieces))
    send, keep = (
        call(
            functools.partial(gather_kernel, stays),
            shape((half + PAD, width), F32 if stays else BF16),
            [VMEM] * (1 + len(pieces)),
            (adjacency, *pieces),
        )
        for stays in (False, True)
    )
    pair_sum = call(
        pair_kernel,
        shape((half + PAD, width), BF16),
        [VMEM] * 2,
        (keep, swap(send, "rep", 1)),
    )
    out, self_term, keep, send = call(
        node_kernel,
        (
            shape((rows, width), BF16),
            shape((rows, width), F32),
            shape((middle + PAD, width), F32),
            shape((half + middle + PAD, width), BF16),
        ),
        [VMEM] * 9,
        (
            pair_sum,
            swap(pair_sum, "rep", 2),
            features,
            near[0],
            d_out,
            near[1],
            w_self,
            w_neigh,
            bias[None, :],
        ),
    )
    back = swap(send, "rep", 1)
    terms_shape = shape((middle + PAD, width), BF16)
    terms = call(core_terms_kernel, terms_shape, [VMEM] * 2, (keep, back))
    terms, back = lax.optimization_barrier((terms, back))
    keep_blocks, *near_msgs = call(
        spread_kernel,
        (shape((far * BLK, width), F32),) + (shape((far * BLK, width), BF16),) * 3,
        [VMEM] * 3,
        (adjacency, send, back),
    )
    near_terms = [terms] + [swap(terms, "row", m) for m in range(1, 4)]
    got = [swap(msg, "row", m + 1) for m, msg in enumerate(near_msgs)][::-1]
    terms = call(part_terms_kernel, terms_shape, [VMEM] * 4, near_terms)
    far_terms = [terms] + [swap(terms, "row", 4 * h) for h in range(1, far)]
    quarter, bias_term = call(
        all_terms_kernel,
        (shape((middle, width), BF16), shape((1, width), F32)),
        [VMEM] * far,
        far_terms,
    )
    keep_block, *far_msgs = call(
        near_sum_kernel,
        (shape((BLK, width), F32),) + (shape((BLK, width), BF16),) * (far - 1),
        [VMEM] * 4,
        (keep_blocks, *got),
    )
    got = [swap(msg, "row", 4 * (h + 1)) for h, msg in enumerate(far_msgs)]
    quarters = [quarter] + [swap(quarter, "rep", m) for m in range(1, 4)]
    out, d_features, grad_bias = call(
        finish_kernel,
        (shape((rows, width), BF16), shape((rows, width), F32), shape((1, width), F32)),
        [VMEM] * (4 + len(got)),
        (out, self_term, bias_term, keep_block, *got),
    )
    grad_self, grad_neigh = call(
        grads_kernel, (shape((2, middle, width), F32),) * 2, [VMEM] * 4, quarters
    )
    grad_self, grad_neigh = (v.reshape(width, width) for v in (grad_self, grad_neigh))
    return (out, d_features, grad_self, grad_neigh, grad_bias[0])


def solution(mesh):
    return jax.shard_map(
        on_device,
        mesh=mesh,
        in_specs=(
            P(("row", "rep"), None),
            P(),
            P(),
            P(),
            P(("row", "rep"), None),
            P(("row", "rep")),
            P(("row", "rep")),
            P(("row", "rep")),
            P(("row", "rep"), None),
            P(("row", "rep"), None),
        ),
        out_specs=(P(("row", "rep"), None), P(("row", "rep"), None), P(), P(), P()),
        check_vma=False,
    )
```
